256 devices in a mesh: dp: 8 (over x, core), seq: 32 (over z, y).
Axes of the slice: x: 4, y: 4, z: 8, core: 2. Of those that a mesh axis runs over, the one named last changes fastest.
Arguments:
- layer_input: bfloat16 [8, 4096, 4096], P('dp', 'seq'), may hold values from -6 to 6
- proj_weight: bfloat16 [4096, 256], replicated, may hold values from -0.0078125 to 0.0078125
- inputs: bfloat16 [8, 4096, 2048], P('dp', 'seq'), may hold values from -6 to 6
- step_size: float32 [8, 32, 4096], P('dp', None, 'seq'), may hold values from 0.02 to 0.2
- log_decay: float32 [8, 32, 4096], P('dp', None, 'seq'), may hold values from -0.8 to 0, as said below
- skip_gain: float32 [32], replicated, may hold values from 0.1 to 1.9
- grad_out: bfloat16 [8, 4096, 2048], P('dp', 'seq'), may hold values from -6 to 6
Outputs:
- grad_inputs: bfloat16 [8, 4096, 2048], P('dp', 'seq')
- grad_weight: float32 [4096, 256], P(('dp', 'seq'))
The draws below stay inside these ranges and needn't reach their ends.
Inputs may be any that keep to these rules, and one draw needn't show every extreme that they name: `log_decay`: every entry is negative.
All inputs are finite; a program needn't handle non-finite values.
Results may differ from the reference program's by a relative error of at most 0.0069.
Values sent between devices are 32-bit elements; how exact they have to be, the bound alone decides.
A program may use at most 192 MiB of HBM per device.

```python
import math
import jax
import jax.numpy as jnp
from jax import lax

D = 4096
SHARD_CHANNELS = 32
HEAD_DIM = 64
STATE = 128
SPAN = 128
L_DEV = 128
SAMPLE_COUNT = 8
TIME_EXTENT = 4096
INNER = 2048


def draw_log_decay(key, part):
    stochastic_seed_splits = jax.random.split(key, 7)
    fast_share = 0.5
    slow_low = 1.0 / 16.0
    slow_high = 1.0 / 4.0
    head_picks = jax.random.uniform(stochastic_seed_splits[0], (1, SHARD_CHANNELS, 1))
    fast_rate = jnp.exp(jax.random.uniform(stochastic_seed_splits[1], (1, SHARD_CHANNELS, 1), minval=jnp.log(1.0 / 50.0), maxval=jnp.log(1.0 / 30.0)))
    slow_rate = jnp.exp(jax.random.uniform(stochastic_seed_splits[2], (1, SHARD_CHANNELS, 1), minval=jnp.log(slow_low), maxval=jnp.log(slow_high))) / L_DEV
    nominal_forgetting_speed = jnp.where(head_picks < fast_share, fast_rate, slow_rate)
    segment_factor = jnp.exp(jax.random.uniform(stochastic_seed_splits[3], (SAMPLE_COUNT, SHARD_CHANNELS, TIME_EXTENT // L_DEV), minval=jnp.log(0.5), maxval=jnp.log(2.0)))
    segment_factor = jnp.repeat(segment_factor, L_DEV, axis=2)
    forgetting_perturbation = jax.random.uniform(stochastic_seed_splits[4], (SAMPLE_COUNT, SHARD_CHANNELS, TIME_EXTENT), minval=0.5, maxval=1.5)
    episode_onset = jax.random.randint(stochastic_seed_splits[5], (2,), 0, TIME_EXTENT)
    element_displacements = jnp.arange(TIME_EXTENT)
    within_episode_flags = jnp.any(element_displacements[None, :] == episode_onset[:, None], axis=0)
    episode_duration = jnp.log(jax.random.uniform(stochastic_seed_splits[6], (SAMPLE_COUNT, SHARD_CHANNELS, 1), minval=0.5, maxval=0.8))
    payload_vectors = -nominal_forgetting_speed * segment_factor * forgetting_perturbation + jnp.where(within_episode_flags[None, None, :], episode_duration, 0.0)
    return payload_vectors.astype(jnp.float32)


def with_spikes(drawn, rng, source, target, blocks, factor):
    def block_of(dim):
        return (jnp.arange(drawn.shape[dim]) // (drawn.shape[dim] // blocks)).reshape((-1,) + (1,) * (drawn.ndim - 1 - dim))

    first = jax.random.permutation(rng, blocks)[block_of(target)]
    far = (block_of(target) + blocks // 2) % blocks
    return jnp.where((block_of(source) == first) | (block_of(source) == far), factor * drawn, drawn)


def block_levels(own_key, extent, cuts, least, high):
    loudness = 1.0
    for position, shards_of in cuts:
        heights = jax.random.uniform(jax.random.fold_in(jax.random.fold_in(own_key, 6), position), (shards_of,), jnp.float32, least / len(cuts), high / len(cuts))
        loudness = loudness * jnp.repeat(jnp.exp(heights), extent[position] // shards_of).reshape((-1,) + (1,) * (len(extent) - 1 - position))
    return loudness


def gaussian(key, extent, deviation, limit, cuts=(), held_as=jnp.bfloat16):
    drawn = deviation * jax.random.normal(key, extent, jnp.float32)
    if cuts:
        drawn = drawn * block_levels(key, extent, cuts, -0.22, 0.18)
    return jnp.clip(drawn, -limit, limit).astype(held_as)


def noise_with(rng, shape, spread, reach, shards, heavy, held_as=jnp.bfloat16):
    drawn = spread * jax.random.normal(rng, shape, jnp.float32)
    if shards:
        drawn = drawn * block_levels(rng, shape, shards, -0.22, 0.18)
    return jnp.clip(with_spikes(drawn, jax.random.fold_in(rng, 3), *heavy), -reach, reach).astype(held_as)


def setup_inputs(seed: int = 0) -> dict:
    key_of = jax.random.split(jax.random.key(seed), 8)
    return {
        "layer_input": noise_with(key_of[0], (SAMPLE_COUNT, TIME_EXTENT, D), 1.0, 6.0, ((0, 8), (1, 32)), (1, 2, 32, 2.75)),
        "proj_weight": gaussian(key_of[1], (D, 2 * STATE), (D * STATE) ** -0.5, 0.0078125),
        "inputs": gaussian(key_of[2], (SAMPLE_COUNT, TIME_EXTENT, INNER), 1.0, 6.0, ((0, 8), (1, 32))),
        "step_size": jnp.clip(jnp.exp(math.log(0.2) - 2.3025851 * jax.random.uniform(key_of[3], (SAMPLE_COUNT, SHARD_CHANNELS, TIME_EXTENT), jnp.float32) ** block_levels(key_of[3], (SAMPLE_COUNT, SHARD_CHANNELS, TIME_EXTENT), ((0, 8), (2, 32)), -0.2, 0.2)), 0.02, 0.2),
        "log_decay": draw_log_decay(jax.random.fold_in(key_of[7], 71), 0),
        "skip_gain": jnp.clip(1.0 + 0.18 * jax.random.normal(key_of[5], (SHARD_CHANNELS,), jnp.float32), 0.1, 1.9),
        "grad_out": gaussian(key_of[6], (SAMPLE_COUNT, TIME_EXTENT, INNER), 1.0, 6.0, ((0, 8), (1, 32))),
    }


def span_inputs(proj, inputs, grad_out, step_size, log_decay):
    length = inputs.shape[0]
    spans = length // SPAN
    b_cols = proj[:, :STATE].reshape(spans, SPAN, STATE)
    c_cols = proj[:, STATE:].reshape(spans, SPAN, STATE)
    inputs_c = inputs.reshape(spans, SPAN, SHARD_CHANNELS, HEAD_DIM)
    grad_rows = grad_out.reshape(spans, SPAN, SHARD_CHANNELS, HEAD_DIM)
    step_rows = step_size.reshape(SHARD_CHANNELS, spans, SPAN).transpose(1, 0, 2)
    decay_sum = jnp.cumsum(log_decay.reshape(SHARD_CHANNELS, spans, SPAN).transpose(1, 0, 2), axis=2)
    span_total = decay_sum[:, :, -1]
    to_end = jnp.exp(span_total[:, :, None] - decay_sum)
    weighted = (inputs_c.astype(jnp.float32) * jnp.transpose(step_rows * to_end, (0, 2, 1))[..., None]).astype(jnp.bfloat16)
    scaled = (grad_rows.astype(jnp.float32) * jnp.transpose(jnp.exp(decay_sum), (0, 2, 1))[..., None]).astype(jnp.bfloat16)
    own_state = jnp.einsum('cqhp,cqn->chpn', weighted.astype(jnp.float32), b_cols.astype(jnp.float32))
    own_grad = jnp.einsum('cqhp,cqn->chpn', scaled.astype(jnp.float32), c_cols.astype(jnp.float32))
    return b_cols, c_cols, inputs_c, grad_rows, step_rows, decay_sum, span_total, weighted, scaled, own_state, own_grad


def span_grads(b_cols, c_cols, inputs_c, grad_rows, step_rows, decay_sum, span_total, weighted, scaled, start, after, skip_gain):
    start_bf = start.astype(jnp.bfloat16)
    after_bf = after.astype(jnp.bfloat16)
    row_ids = lax.broadcasted_iota(jnp.int32, (SPAN, SPAN), 0)
    col_ids = lax.broadcasted_iota(jnp.int32, (SPAN, SPAN), 1)
    causal = row_ids >= col_ids
    log_gap = decay_sum[:, :, None] - decay_sum[:, None, :]
    decay_mat = jnp.exp(jnp.where(causal[None], log_gap, -jnp.inf))
    kernel = jnp.dot(c_cols, b_cols.T, preferred_element_type=jnp.float32)
    weights = (decay_mat * kernel[None]).astype(jnp.bfloat16)
    within = jnp.einsum('hsj,shp->jhp', weights.astype(jnp.float32), grad_rows.astype(jnp.float32))
    carried = jnp.einsum('hpn,jn->jhp', after_bf.astype(jnp.float32), b_cols.astype(jnp.float32))
    to_end = jnp.exp(span_total[:, None] - decay_sum)
    grad_x = step_rows.T[:, :, None] * (within + to_end.T[:, :, None] * carried) + skip_gain[None, :, None] * grad_rows.astype(jnp.float32)
    intersection = jnp.einsum('shp,jhp->hsj', grad_rows.astype(jnp.float32), inputs_c.astype(jnp.float32))
    mixing = jnp.sum(decay_mat * step_rows[:, None, :] * intersection, axis=0).astype(jnp.bfloat16)
    grad_c = jnp.dot(mixing, b_cols, preferred_element_type=jnp.float32) + jnp.dot(scaled.reshape(SPAN, -1), start_bf.reshape(-1, STATE), preferred_element_type=jnp.float32)
    grad_b = jnp.dot(mixing.T, c_cols, preferred_element_type=jnp.float32) + jnp.dot(weighted.reshape(SPAN, -1), after_bf.reshape(-1, STATE), preferred_element_type=jnp.float32)
    grad_proj = jnp.concatenate([grad_b, grad_c], axis=1).astype(jnp.bfloat16)
    return grad_x.astype(jnp.bfloat16).reshape(SPAN, -1), grad_proj


def one_sequence(layer_input, inputs, grad_out, step_size, log_decay, proj_weight, skip_gain):
    proj = jnp.dot(layer_input, proj_weight, preferred_element_type=jnp.float32).astype(jnp.bfloat16)
    pieces = span_inputs(proj, inputs, grad_out, step_size, log_decay)
    own_state, own_grad, span_total = pieces[9], pieces[10], pieces[6]
    empty_state = jnp.zeros((SHARD_CHANNELS, HEAD_DIM, STATE), jnp.float32)

    def advance(state_carry, piece):
        return jnp.exp(piece[1])[:, None, None] * state_carry + piece[0], state_carry

    _, starts = lax.scan(advance, empty_state, (own_state, span_total))
    _, afters = lax.scan(advance, empty_state, (own_grad, span_total), reverse=True)

    def finish(parts):
        return span_grads(*parts, skip_gain)

    grad_x, grad_proj = lax.map(finish, pieces[:9] + (starts, afters))
    grad_proj = grad_proj.reshape(-1, 2 * STATE)
    contrib = jnp.dot(layer_input.T, grad_proj, preferred_element_type=jnp.float32)
    return grad_x.reshape(-1, INNER), contrib


def reference(layer_input, proj_weight, inputs, step_size, log_decay, skip_gain, grad_out):
    def per_sequence(parts):
        return one_sequence(parts[0], parts[1], parts[2], parts[3], parts[4], proj_weight, skip_gain)

    grad_inputs, contribs = lax.map(per_sequence, (layer_input, inputs, grad_out, step_size, log_decay))
    grad_weight = jnp.sum(contribs, axis=0) / TIME_EXTENT
    return grad_inputs, grad_weight
```

```python
import jax
import jax.numpy as jnp
from jax import lax
from jax.sharding import PartitionSpec as P

SHARD_CHANNELS = 32
HEAD_DIM = 64
STATE = 128
SPAN = 128


def span_inputs(proj, inputs, grad_out, step_size, log_decay):
    length = inputs.shape[0]
    spans = length // SPAN
    b_cols = proj[:, :STATE].reshape(spans, SPAN, STATE)
    c_cols = proj[:, STATE:].reshape(spans, SPAN, STATE)
    inputs_c = inputs.reshape(spans, SPAN, SHARD_CHANNELS, HEAD_DIM)
    grad_rows = grad_out.reshape(spans, SPAN, SHARD_CHANNELS, HEAD_DIM)
    step_rows = step_size.reshape(SHARD_CHANNELS, spans, SPAN).transpose(1, 0, 2)
    decay_sum = jnp.cumsum(
        log_decay.reshape(SHARD_CHANNELS, spans, SPAN).transpose(1, 0, 2), axis=2
    )
    span_total = decay_sum[:, :, -1]
    to_end = jnp.exp(span_total[:, :, None] - decay_sum)
    weighted = (
        inputs_c.astype(jnp.float32) * jnp.transpose(step_rows * to_end, (0, 2, 1))[..., None]
    ).astype(jnp.bfloat16)
    scaled = (
        grad_rows.astype(jnp.float32) * jnp.transpose(jnp.exp(decay_sum), (0, 2, 1))[..., None]
    ).astype(jnp.bfloat16)
    own_state = jnp.einsum("cqhp,cqn->chpn", weighted, b_cols, preferred_element_type=jnp.float32)
    own_grad = jnp.einsum("cqhp,cqn->chpn", scaled, c_cols, preferred_element_type=jnp.float32)
    return (
        b_cols,
        c_cols,
        inputs_c,
        grad_rows,
        step_rows,
        decay_sum,
        span_total,
        weighted,
        scaled,
        own_state,
        own_grad,
    )


def span_grads(
    b_cols,
    c_cols,
    inputs_c,
    grad_rows,
    step_rows,
    decay_sum,
    span_total,
    weighted,
    scaled,
    start,
    after,
    skip_gain,
):
    start_bf = start.astype(jnp.bfloat16)
    after_bf = after.astype(jnp.bfloat16)
    row_ids = lax.broadcasted_iota(jnp.int32, (SPAN, SPAN), 0)
    col_ids = lax.broadcasted_iota(jnp.int32, (SPAN, SPAN), 1)
    causal = row_ids >= col_ids
    log_gap = decay_sum[:, :, None] - decay_sum[:, None, :]
    decay_mat = jnp.exp(jnp.where(causal[None], log_gap, -jnp.inf))
    kernel = jnp.dot(c_cols, b_cols.T, preferred_element_type=jnp.float32)
    weights = (decay_mat * kernel[None]).astype(jnp.bfloat16)
    within = jnp.einsum("hsj,shp->jhp", weights, grad_rows, preferred_element_type=jnp.float32)
    carried = jnp.einsum("hpn,jn->jhp", after_bf, b_cols, preferred_element_type=jnp.float32)
    to_end = jnp.exp(span_total[:, None] - decay_sum)
    grad_x = step_rows.T[:, :, None] * (within + to_end.T[:, :, None] * carried) + skip_gain[
        None, :, None
    ] * grad_rows.astype(jnp.float32)
    intersection = jnp.einsum(
        "shp,jhp->hsj", grad_rows, inputs_c, preferred_element_type=jnp.float32
    )
    mixing = jnp.sum(decay_mat * step_rows[:, None, :] * intersection, axis=0).astype(jnp.bfloat16)
    grad_c = jnp.dot(mixing, b_cols, preferred_element_type=jnp.float32) + jnp.dot(
        scaled.reshape(SPAN, -1), start_bf.reshape(-1, STATE), preferred_element_type=jnp.float32
    )
    grad_b = jnp.dot(mixing.T, c_cols, preferred_element_type=jnp.float32) + jnp.dot(
        weighted.reshape(SPAN, -1), after_bf.reshape(-1, STATE), preferred_element_type=jnp.float32
    )
    grad_proj = jnp.concatenate([grad_b, grad_c], axis=1).astype(jnp.bfloat16)
    return (grad_x.astype(jnp.bfloat16).reshape(SPAN, -1), grad_proj)


def exchange(own_state, own_grad, device_total):
    count = lax.axis_size("seq")
    heads, rows, cols = own_state.shape
    marks = jnp.broadcast_to(device_total[:, None, None], (heads, 8, cols))
    payload = jnp.stack(
        [
            jnp.concatenate([own_state, marks], axis=1),
            jnp.concatenate([own_grad, marks], axis=1),
        ]
    )
    mine = lax.all_to_all(payload, "seq", 1, 1, tiled=True)
    totals = mine[0, :, rows, 0]
    ends = mine[:, :, :rows, :].reshape(2, count, rows * cols)
    ids = jnp.arange(count)
    target, source, between = ids[:, None, None], ids[None, :, None], ids[None, None, :]
    fwd_span = (source < between) & (between < target)
    bwd_span = (target < between) & (between < source)
    fwd_log = jnp.sum(jnp.where(fwd_span, totals[None, None, :], 0.0), axis=2)
    bwd_log = jnp.sum(jnp.where(bwd_span, totals[None, None, :], 0.0), axis=2)
    fwd_w = jnp.where(ids[None, :] < ids[:, None], jnp.exp(fwd_log), 0.0)
    bwd_w = jnp.where(ids[None, :] > ids[:, None], jnp.exp(bwd_log), 0.0)
    weights = jnp.stack([fwd_w, bwd_w])
    entries = jnp.einsum(
        "ktj,kjx->ktx", weights, ends, precision=lax.Precision.HIGHEST,
        preferred_element_type=jnp.float32,
    ).reshape(2, count, rows, cols)
    back = lax.all_to_all(entries, "seq", 1, 1, tiled=True)
    return back[0], back[1]


def scatter_rows(term):
    dp, seq = lax.axis_size("dp"), lax.axis_size("seq")
    rows, cols = term.shape
    part = lax.all_to_all(term.reshape(dp, rows // dp, cols), "dp", 0, 0, tiled=True).sum(0)
    part = lax.all_to_all(part.reshape(seq, rows // dp // seq, cols), "seq", 0, 0, tiled=True)
    return part.sum(0)


def on_device(layer_input, proj_weight, inputs, step_size, log_decay, skip_gain, grad_out):
    tokens = layer_input[0]
    length = tokens.shape[0]
    proj = jnp.dot(tokens, proj_weight, preferred_element_type=jnp.float32).astype(jnp.bfloat16)
    pieces = span_inputs(proj, inputs[0], grad_out[0], step_size[0], log_decay[0])
    own_state, own_grad, span_total = (pieces[9], pieces[10], pieces[6])
    empty_state = jnp.zeros((SHARD_CHANNELS, HEAD_DIM, STATE), jnp.float32)

    def advance(state_carry, piece):
        return (jnp.exp(piece[1])[:, None, None] * state_carry + piece[0], state_carry)

    last_state, local_starts = lax.scan(advance, empty_state, (own_state, span_total))
    last_grad, local_afters = lax.scan(advance, empty_state, (own_grad, span_total), reverse=True)
    state_entry, grad_entry = exchange(last_state, last_grad, jnp.sum(span_total, axis=0))
    running = jnp.cumsum(span_total, axis=0)
    before = running - span_total
    behind = jnp.sum(span_total, axis=0)[None] - running
    starts = local_starts + jnp.exp(before)[:, :, None, None] * state_entry[None]
    afters = local_afters + jnp.exp(behind)[:, :, None, None] * grad_entry[None]

    def finish(parts):
        return span_grads(*parts, skip_gain)

    grad_x, grad_proj = lax.map(finish, pieces[:9] + (starts, afters))
    grad_proj = grad_proj.reshape(length, 2 * STATE)
    scale_factor = 1.0 / (length * lax.axis_size("seq"))
    term = jnp.einsum("ld,ln->dn", tokens, grad_proj, preferred_element_type=jnp.float32)
    grad_weight = scatter_rows(term) * scale_factor
    return (grad_x, grad_weight)


def solution(mesh):
    return jax.shard_map(
        on_device,
        mesh=mesh,
        in_specs=(
            P("dp", "seq", None),
            P(),
            P("dp", "seq", None),
            P("dp", None, "seq"),
            P("dp", None, "seq"),
            P(),
            P("dp", "seq", None),
        ),
        out_specs=(P("dp", "seq", None), P(("dp", "seq"), None)),
        check_vma=False,
    )
```

```python
import jax
import jax.numpy as jnp
from jax import lax
from jax.sharding import Mesh, PartitionSpec as P

SHARD_CHANNELS = 32
HEAD_DIM = 64
STATE = 128
SPAN = 128


def span_inputs(proj, inputs, grad_out, step_size, log_decay):
    length = inputs.shape[0]
    spans = length // SPAN
    b_cols = proj[:, :STATE].reshape(spans, SPAN, STATE)
    c_cols = proj[:, STATE:].reshape(spans, SPAN, STATE)
    inputs_c = inputs.reshape(spans, SPAN, SHARD_CHANNELS, HEAD_DIM)
    grad_rows = grad_out.reshape(spans, SPAN, SHARD_CHANNELS, HEAD_DIM)
    step_rows = step_size.reshape(SHARD_CHANNELS, spans, SPAN).transpose(1, 0, 2)
    decay_sum = jnp.cumsum(
        log_decay.reshape(SHARD_CHANNELS, spans, SPAN).transpose(1, 0, 2), axis=2
    )
    span_total = decay_sum[:, :, -1]
    to_end = jnp.exp(span_total[:, :, None] - decay_sum)
    weighted = (
        inputs_c.astype(jnp.float32) * jnp.transpose(step_rows * to_end, (0, 2, 1))[..., None]
    ).astype(jnp.bfloat16)
    scaled = (
        grad_rows.astype(jnp.float32) * jnp.transpose(jnp.exp(decay_sum), (0, 2, 1))[..., None]
    ).astype(jnp.bfloat16)
    own_state = jnp.einsum("cqhp,cqn->chpn", weighted, b_cols, preferred_element_type=jnp.float32)
    own_grad = jnp.einsum("cqhp,cqn->chpn", scaled, c_cols, preferred_element_type=jnp.float32)
    return (
        b_cols,
        c_cols,
        inputs_c,
        grad_rows,
        step_rows,
        decay_sum,
        span_total,
        weighted,
        scaled,
        own_state,
        own_grad,
    )


def span_grads(
    b_cols,
    c_cols,
    inputs_c,
    grad_rows,
    step_rows,
    decay_sum,
    span_total,
    weighted,
    scaled,
    start,
    after,
    skip_gain,
):
    start_bf = start.astype(jnp.bfloat16)
    after_bf = after.astype(jnp.bfloat16)
    row_ids = lax.broadcasted_iota(jnp.int32, (SPAN, SPAN), 0)
    col_ids = lax.broadcasted_iota(jnp.int32, (SPAN, SPAN), 1)
    causal = row_ids >= col_ids
    log_gap = decay_sum[:, :, None] - decay_sum[:, None, :]
    decay_mat = jnp.exp(jnp.where(causal[None], log_gap, -jnp.inf))
    kernel = jnp.dot(c_cols, b_cols.T, preferred_element_type=jnp.float32)
    weights = (decay_mat * kernel[None]).astype(jnp.bfloat16)
    within = jnp.einsum("hsj,shp->jhp", weights, grad_rows, preferred_element_type=jnp.float32)
    carried = jnp.einsum("hpn,jn->jhp", after_bf, b_cols, preferred_element_type=jnp.float32)
    to_end = jnp.exp(span_total[:, None] - decay_sum)
    grad_x = step_rows.T[:, :, None] * (within + to_end.T[:, :, None] * carried) + skip_gain[
        None, :, None
    ] * grad_rows.astype(jnp.float32)
    intersection = jnp.einsum(
        "shp,jhp->hsj", grad_rows, inputs_c, preferred_element_type=jnp.float32
    )
    mixing = jnp.sum(decay_mat * step_rows[:, None, :] * intersection, axis=0).astype(jnp.bfloat16)
    grad_c = jnp.dot(mixing, b_cols, preferred_element_type=jnp.float32) + jnp.dot(
        scaled.reshape(SPAN, -1), start_bf.reshape(-1, STATE), preferred_element_type=jnp.float32
    )
    grad_b = jnp.dot(mixing.T, c_cols, preferred_element_type=jnp.float32) + jnp.dot(
        weighted.reshape(SPAN, -1), after_bf.reshape(-1, STATE), preferred_element_type=jnp.float32
    )
    grad_proj = jnp.concatenate([grad_b, grad_c], axis=1).astype(jnp.bfloat16)
    return (grad_x.astype(jnp.bfloat16).reshape(SPAN, -1), grad_proj)


def exchange(own_state, own_grad, device_total):
    count = lax.axis_size("z") * lax.axis_size("y")
    heads, rows, cols = own_state.shape
    marks = jnp.broadcast_to(device_total[:, None, None], (heads, 8, cols))
    payload = jnp.stack(
        [
            jnp.concatenate([own_state, marks], axis=1),
            jnp.concatenate([own_grad, marks], axis=1),
        ]
    )
    mine = lax.all_to_all(payload, ("z", "y"), 1, 1, tiled=True)
    totals = mine[0, :, rows, 0]
    ends = mine[:, :, :rows, :].reshape(2, count, rows * cols)
    ids = jnp.arange(count)
    target, source, between = ids[:, None, None], ids[None, :, None], ids[None, None, :]
    fwd_span = (source < between) & (between < target)
    bwd_span = (target < between) & (between < source)
    fwd_log = jnp.sum(jnp.where(fwd_span, totals[None, None, :], 0.0), axis=2)
    bwd_log = jnp.sum(jnp.where(bwd_span, totals[None, None, :], 0.0), axis=2)
    fwd_w = jnp.where(ids[None, :] < ids[:, None], jnp.exp(fwd_log), 0.0)
    bwd_w = jnp.where(ids[None, :] > ids[:, None], jnp.exp(bwd_log), 0.0)
    weights = jnp.stack([fwd_w, bwd_w])
    entries = jnp.einsum(
        "ktj,kjx->ktx", weights, ends, precision=lax.Precision.HIGHEST,
        preferred_element_type=jnp.float32,
    ).reshape(2, count, rows, cols)
    back = lax.all_to_all(entries, ("z", "y"), 1, 1, tiled=True)
    return back[0], back[1]


def scatter_rows(term):
    cores, chips = lax.axis_size("core"), lax.axis_size("x")
    seq = lax.axis_size("z") * lax.axis_size("y")
    rows, cols = term.shape
    part = term.reshape(chips, cores, rows // (chips * cores), cols)
    part = lax.all_to_all(part, "core", 1, 1, tiled=True).sum(1)
    part = lax.all_to_all(part, "x", 0, 0, tiled=True).sum(0)
    part = lax.all_to_all(part.reshape(seq, -1, cols), ("z", "y"), 0, 0, tiled=True)
    return part.sum(0)


def on_device(layer_input, proj_weight, inputs, step_size, log_decay, skip_gain, grad_out):
    tokens = layer_input[0]
    length = tokens.shape[0]
    proj = jnp.dot(tokens, proj_weight, preferred_element_type=jnp.float32).astype(jnp.bfloat16)
    pieces = span_inputs(proj, inputs[0], grad_out[0], step_size[0], log_decay[0])
    own_state, own_grad, span_total = (pieces[9], pieces[10], pieces[6])
    empty_state = jnp.zeros((SHARD_CHANNELS, HEAD_DIM, STATE), jnp.float32)

    def advance(state_carry, piece):
        return (jnp.exp(piece[1])[:, None, None] * state_carry + piece[0], state_carry)

    last_state, local_starts = lax.scan(advance, empty_state, (own_state, span_total))
    last_grad, local_afters = lax.scan(advance, empty_state, (own_grad, span_total), reverse=True)
    state_entry, grad_entry = exchange(last_state, last_grad, jnp.sum(span_total, axis=0))
    running = jnp.cumsum(span_total, axis=0)
    before = running - span_total
    behind = jnp.sum(span_total, axis=0)[None] - running
    starts = local_starts + jnp.exp(before)[:, :, None, None] * state_entry[None]
    afters = local_afters + jnp.exp(behind)[:, :, None, None] * grad_entry[None]

    def finish(parts):
        return span_grads(*parts, skip_gain)

    grad_x, grad_proj = lax.map(finish, pieces[:9] + (starts, afters))
    grad_proj = grad_proj.reshape(length, 2 * STATE)
    scale_factor = 1.0 / (length * lax.axis_size("z") * lax.axis_size("y"))
    term = jnp.einsum("ld,ln->dn", tokens, grad_proj, preferred_element_type=jnp.float32)
    grad_weight = scatter_rows(term) * scale_factor
    return (grad_x, grad_weight)


def physical_mesh(mesh):
    grid = mesh.devices
    cores = len({d.core_on_chip for d in grid.flat})
    rows = len({d.coords[1] for d in grid.flat})
    dp, seq = grid.shape
    return Mesh(grid.reshape(dp // cores, cores, seq // rows, rows), ("x", "core", "z", "y"))


def solution(mesh):
    fine = physical_mesh(mesh)
    dp, seq = ("x", "core"), ("z", "y")
    return jax.shard_map(
        on_device,
        mesh=fine,
        in_specs=(
            P(dp, seq, None),
            P(),
            P(dp, seq, None),
            P(dp, None, seq),
            P(dp, None, seq),
            P(),
            P(dp, seq, None),
        ),
        out_specs=(P(dp, seq, None), P(dp + seq, None)),
        check_vma=False,
    )
```

```python
import jax
import jax.numpy as jnp
from jax import lax
from jax.experimental import pallas as pl
from jax.experimental.pallas import tpu as pltpu
from jax.sharding import Mesh, PartitionSpec as P

SHARD_CHANNELS = 32
HEAD_DIM = 64
STATE = 128
SPAN = 128


def span_inputs(proj, inputs, grad_out, step_size, log_decay):
    length = inputs.shape[0]
    spans = length // SPAN
    b_cols = proj[:, :STATE].reshape(spans, SPAN, STATE)
    c_cols = proj[:, STATE:].reshape(spans, SPAN, STATE)
    inputs_c = inputs.reshape(spans, SPAN, SHARD_CHANNELS, HEAD_DIM)
    grad_rows = grad_out.reshape(spans, SPAN, SHARD_CHANNELS, HEAD_DIM)
    step_rows = step_size.reshape(SHARD_CHANNELS, spans, SPAN).transpose(1, 0, 2)
    decay_sum = jnp.cumsum(
        log_decay.reshape(SHARD_CHANNELS, spans, SPAN).transpose(1, 0, 2), axis=2
    )
    span_total = decay_sum[:, :, -1]
    to_end = jnp.exp(span_total[:, :, None] - decay_sum)
    weighted = (
        inputs_c.astype(jnp.float32) * jnp.transpose(step_rows * to_end, (0, 2, 1))[..., None]
    ).astype(jnp.bfloat16)
    scaled = (
        grad_rows.astype(jnp.float32) * jnp.transpose(jnp.exp(decay_sum), (0, 2, 1))[..., None]
    ).astype(jnp.bfloat16)
    own_state = jnp.einsum("cqhp,cqn->chpn", weighted, b_cols, preferred_element_type=jnp.float32)
    own_grad = jnp.einsum("cqhp,cqn->chpn", scaled, c_cols, preferred_element_type=jnp.float32)
    return (
        b_cols,
        c_cols,
        inputs_c,
        grad_rows,
        step_rows,
        decay_sum,
        span_total,
        weighted,
        scaled,
        own_state,
        own_grad,
    )


def span_grads(
    b_cols,
    c_cols,
    inputs_c,
    grad_rows,
    step_rows,
    decay_sum,
    span_total,
    weighted,
    scaled,
    start,
    after,
    skip_gain,
):
    start_bf = start.astype(jnp.bfloat16)
    after_bf = after.astype(jnp.bfloat16)
    row_ids = lax.broadcasted_iota(jnp.int32, (SPAN, SPAN), 0)
    col_ids = lax.broadcasted_iota(jnp.int32, (SPAN, SPAN), 1)
    causal = row_ids >= col_ids
    log_gap = decay_sum[:, :, None] - decay_sum[:, None, :]
    decay_mat = jnp.exp(jnp.where(causal[None], log_gap, -jnp.inf))
    kernel = jnp.dot(c_cols, b_cols.T, preferred_element_type=jnp.float32)
    weights = (decay_mat * kernel[None]).astype(jnp.bfloat16)
    within = jnp.einsum("hsj,shp->jhp", weights, grad_rows, preferred_element_type=jnp.float32)
    carried = jnp.einsum("hpn,jn->jhp", after_bf, b_cols, preferred_element_type=jnp.float32)
    to_end = jnp.exp(span_total[:, None] - decay_sum)
    grad_x = step_rows.T[:, :, None] * (within + to_end.T[:, :, None] * carried) + skip_gain[
        None, :, None
    ] * grad_rows.astype(jnp.float32)
    intersection = jnp.einsum(
        "shp,jhp->hsj", grad_rows, inputs_c, preferred_element_type=jnp.float32
    )
    mixing = jnp.sum(decay_mat * step_rows[:, None, :] * intersection, axis=0).astype(jnp.bfloat16)
    grad_c = jnp.dot(mixing, b_cols, preferred_element_type=jnp.float32) + jnp.dot(
        scaled.reshape(SPAN, -1), start_bf.reshape(-1, STATE), preferred_element_type=jnp.float32
    )
    grad_b = jnp.dot(mixing.T, c_cols, preferred_element_type=jnp.float32) + jnp.dot(
        weighted.reshape(SPAN, -1), after_bf.reshape(-1, STATE), preferred_element_type=jnp.float32
    )
    grad_proj = jnp.concatenate([grad_b, grad_c], axis=1).astype(jnp.bfloat16)
    return (grad_x.astype(jnp.bfloat16).reshape(SPAN, -1), grad_proj)


def group_all_to_all(payload):
    width = lax.axis_size("y")
    count = lax.axis_size("z") * width

    def kernel(src_ref, out_ref, land, send_sems, recv_sems, local_sem):
        chip, core = lax.axis_index("x"), lax.axis_index("core")
        me = lax.axis_index("z") * width + lax.axis_index("y")
        local = pltpu.make_async_copy(src_ref.at[me], land.at[me], local_sem)
        local.start()
        outgoing = []
        for step in range(1, count):
            dest = (me + step) % count
            copy = pltpu.make_async_remote_copy(
                src_ref=src_ref.at[dest],
                dst_ref=land.at[me],
                send_sem=send_sems.at[step - 1],
                recv_sem=recv_sems.at[step - 1],
                device_id=(chip, core, dest // width, dest % width),
                device_id_type=pl.DeviceIdType.MESH,
            )
            copy.start()
            outgoing.append(copy)
        local.wait()
        for step in range(1, count):
            outgoing[step - 1].wait_send()
            origin = (me + count - step) % count
            pltpu.make_async_remote_copy(
                src_ref=src_ref.at[origin],
                dst_ref=land.at[origin],
                send_sem=send_sems.at[step - 1],
                recv_sem=recv_sems.at[step - 1],
                device_id=(chip, core, origin // width, origin % width),
                device_id_type=pl.DeviceIdType.MESH,
            ).wait_recv()
        out_ref[...] = land[...]

    return pl.pallas_call(
        kernel,
        out_shape=jax.ShapeDtypeStruct(payload.shape, payload.dtype),
        in_specs=[pl.BlockSpec(memory_space=pltpu.VMEM)],
        out_specs=pl.BlockSpec(memory_space=pltpu.VMEM),
        scratch_shapes=[
            pltpu.VMEM(payload.shape, payload.dtype),
            pltpu.SemaphoreType.DMA((count - 1,)),
            pltpu.SemaphoreType.DMA((count - 1,)),
            pltpu.SemaphoreType.DMA(()),
        ],
        compiler_params=pltpu.CompilerParams(has_side_effects=True, vmem_limit_bytes=48 * 1024 * 1024),
    )(payload)


def exchange(own_state, own_grad, device_total):
    count = lax.axis_size("z") * lax.axis_size("y")
    heads, rows, cols = own_state.shape
    marks = jnp.broadcast_to(device_total[:, None, None], (heads, 8, cols))
    payload = jnp.stack(
        [
            jnp.concatenate([own_state, marks], axis=1),
            jnp.concatenate([own_grad, marks], axis=1),
        ],
        axis=1,
    )
    mine = group_all_to_all(payload)
    totals = mine[:, 0, rows, 0]
    ends = mine[:, :, :rows, :].reshape(count, 2, rows * cols)
    ids = jnp.arange(count)
    target, source, between = ids[:, None, None], ids[None, :, None], ids[None, None, :]
    fwd_span = (source < between) & (between < target)
    bwd_span = (target < between) & (between < source)
    fwd_log = jnp.sum(jnp.where(fwd_span, totals[None, None, :], 0.0), axis=2)
    bwd_log = jnp.sum(jnp.where(bwd_span, totals[None, None, :], 0.0), axis=2)
    fwd_w = jnp.where(ids[None, :] < ids[:, None], jnp.exp(fwd_log), 0.0)
    bwd_w = jnp.where(ids[None, :] > ids[:, None], jnp.exp(bwd_log), 0.0)
    weights = jnp.stack([fwd_w, bwd_w])
    entries = jnp.einsum(
        "ktj,jkx->tkx", weights, ends, precision=lax.Precision.HIGHEST,
        preferred_element_type=jnp.float32,
    ).reshape(count, 2, rows, cols)
    back = group_all_to_all(entries)
    return back[:, 0], back[:, 1]


def scatter_rows(term):
    cores, chips = lax.axis_size("core"), lax.axis_size("x")
    seq = lax.axis_size("z") * lax.axis_size("y")
    rows, cols = term.shape
    part = term.reshape(chips, cores, rows // (chips * cores), cols)
    part = lax.all_to_all(part, "core", 1, 1, tiled=True).sum(1)
    part = lax.all_to_all(part, "x", 0, 0, tiled=True).sum(0)
    part = lax.all_to_all(part.reshape(seq, -1, cols), ("z", "y"), 0, 0, tiled=True)
    return part.sum(0)


def on_device(layer_input, proj_weight, inputs, step_size, log_decay, skip_gain, grad_out):
    tokens = layer_input[0]
    length = tokens.shape[0]
    proj = jnp.dot(tokens, proj_weight, preferred_element_type=jnp.float32).astype(jnp.bfloat16)
    pieces = span_inputs(proj, inputs[0], grad_out[0], step_size[0], log_decay[0])
    own_state, own_grad, span_total = (pieces[9], pieces[10], pieces[6])
    empty_state = jnp.zeros((SHARD_CHANNELS, HEAD_DIM, STATE), jnp.float32)

    def advance(state_carry, piece):
        return (jnp.exp(piece[1])[:, None, None] * state_carry + piece[0], state_carry)

    last_state, local_starts = lax.scan(advance, empty_state, (own_state, span_total))
    last_grad, local_afters = lax.scan(advance, empty_state, (own_grad, span_total), reverse=True)
    state_entry, grad_entry = exchange(last_state, last_grad, jnp.sum(span_total, axis=0))
    running = jnp.cumsum(span_total, axis=0)
    before = running - span_total
    behind = jnp.sum(span_total, axis=0)[None] - running
    starts = local_starts + jnp.exp(before)[:, :, None, None] * state_entry[None]
    afters = local_afters + jnp.exp(behind)[:, :, None, None] * grad_entry[None]

    def finish(parts):
        return span_grads(*parts, skip_gain)

    grad_x, grad_proj = lax.map(finish, pieces[:9] + (starts, afters))
    grad_proj = grad_proj.reshape(length, 2 * STATE)
    scale_factor = 1.0 / (length * lax.axis_size("z") * lax.axis_size("y"))
    term = jnp.einsum("ld,ln->dn", tokens, grad_proj, preferred_element_type=jnp.float32)
    grad_weight = scatter_rows(term) * scale_factor
    return (grad_x, grad_weight)


def physical_mesh(mesh):
    grid = mesh.devices
    cores = len({d.core_on_chip for d in grid.flat})
    rows = len({d.coords[1] for d in grid.flat})
    dp, seq = grid.shape
    return Mesh(grid.reshape(dp // cores, cores, seq // rows, rows), ("x", "core", "z", "y"))


def solution(mesh):
    fine = physical_mesh(mesh)
    dp, seq = ("x", "core"), ("z", "y")
    return jax.shard_map(
        on_device,
        mesh=fine,
        in_specs=(
            P(dp, seq, None),
            P(),
            P(dp, seq, None),
            P(dp, None, seq),
            P(dp, None, seq),
            P(),
            P(dp, seq, None),
        ),
        out_specs=(P(dp, seq, None), P(dp + seq, None)),
        check_vma=False,
    )
```

```python
import jax
import jax.numpy as jnp
from jax import lax
from jax.experimental import pallas as pl
from jax.experimental.pallas import tpu as pltpu
from jax.sharding import Mesh, PartitionSpec as P

SHARD_CHANNELS = 32
HEAD_DIM = 64
STATE = 128
SPAN = 128


def span_inputs(proj, inputs, grad_out, step_size, log_decay):
    length = inputs.shape[0]
    spans = length // SPAN
    b_cols = proj[:, :STATE].reshape(spans, SPAN, STATE)
    c_cols = proj[:, STATE:].reshape(spans, SPAN, STATE)
    inputs_c = inputs.reshape(spans, SPAN, SHARD_CHANNELS, HEAD_DIM)
    grad_rows = grad_out.reshape(spans, SPAN, SHARD_CHANNELS, HEAD_DIM)
    step_rows = step_size.reshape(SHARD_CHANNELS, spans, SPAN).transpose(1, 0, 2)
    decay_sum = jnp.cumsum(
        log_decay.reshape(SHARD_CHANNELS, spans, SPAN).transpose(1, 0, 2), axis=2
    )
    span_total = decay_sum[:, :, -1]
    to_end = jnp.exp(span_total[:, :, None] - decay_sum)
    weighted = (
        inputs_c.astype(jnp.float32) * jnp.transpose(step_rows * to_end, (0, 2, 1))[..., None]
    ).astype(jnp.bfloat16)
    scaled = (
        grad_rows.astype(jnp.float32) * jnp.transpose(jnp.exp(decay_sum), (0, 2, 1))[..., None]
    ).astype(jnp.bfloat16)
    own_state = jnp.einsum("cqhp,cqn->chpn", weighted, b_cols, preferred_element_type=jnp.float32)
    own_grad = jnp.einsum("cqhp,cqn->chpn", scaled, c_cols, preferred_element_type=jnp.float32)
    return (
        b_cols,
        c_cols,
        inputs_c,
        grad_rows,
        step_rows,
        decay_sum,
        span_total,
        weighted,
        scaled,
        own_state,
        own_grad,
    )


def span_grads(
    b_cols,
    c_cols,
    inputs_c,
    grad_rows,
    step_rows,
    decay_sum,
    span_total,
    weighted,
    scaled,
    start,
    after,
    skip_gain,
):
    start_bf = start.astype(jnp.bfloat16)
    after_bf = after.astype(jnp.bfloat16)
    row_ids = lax.broadcasted_iota(jnp.int32, (SPAN, SPAN), 0)
    col_ids = lax.broadcasted_iota(jnp.int32, (SPAN, SPAN), 1)
    causal = row_ids >= col_ids
    log_gap = decay_sum[:, :, None] - decay_sum[:, None, :]
    decay_mat = jnp.exp(jnp.where(causal[None], log_gap, -jnp.inf))
    kernel = jnp.dot(c_cols, b_cols.T, preferred_element_type=jnp.float32)
    weights = (decay_mat * kernel[None]).astype(jnp.bfloat16)
    within = jnp.einsum("hsj,shp->jhp", weights, grad_rows, preferred_element_type=jnp.float32)
    carried = jnp.einsum("hpn,jn->jhp", after_bf, b_cols, preferred_element_type=jnp.float32)
    to_end = jnp.exp(span_total[:, None] - decay_sum)
    grad_x = step_rows.T[:, :, None] * (within + to_end.T[:, :, None] * carried) + skip_gain[
        None, :, None
    ] * grad_rows.astype(jnp.float32)
    intersection = jnp.einsum(
        "shp,jhp->hsj", grad_rows, inputs_c, preferred_element_type=jnp.float32
    )
    mixing = jnp.sum(decay_mat * step_rows[:, None, :] * intersection, axis=0).astype(jnp.bfloat16)
    grad_c = jnp.dot(mixing, b_cols, preferred_element_type=jnp.float32) + jnp.dot(
        scaled.reshape(SPAN, -1), start_bf.reshape(-1, STATE), preferred_element_type=jnp.float32
    )
    grad_b = jnp.dot(mixing.T, c_cols, preferred_element_type=jnp.float32) + jnp.dot(
        weighted.reshape(SPAN, -1), after_bf.reshape(-1, STATE), preferred_element_type=jnp.float32
    )
    grad_proj = jnp.concatenate([grad_b, grad_c], axis=1).astype(jnp.bfloat16)
    return (grad_x.astype(jnp.bfloat16).reshape(SPAN, -1), grad_proj)


def group_all_to_all(payload):
    width = lax.axis_size("y")
    count = lax.axis_size("z") * width

    def kernel(src_ref, out_ref, land, send_sems, recv_sems, local_sem):
        chip, core = lax.axis_index("x"), lax.axis_index("core")
        me = lax.axis_index("z") * width + lax.axis_index("y")
        local = pltpu.make_async_copy(src_ref.at[me], land.at[me], local_sem)
        local.start()
        outgoing = []
        for step in range(1, count):
            dest = (me + step) % count
            copy = pltpu.make_async_remote_copy(
                src_ref=src_ref.at[dest],
                dst_ref=land.at[me],
                send_sem=send_sems.at[step - 1],
                recv_sem=recv_sems.at[step - 1],
                device_id=(chip, core, dest // width, dest % width),
                device_id_type=pl.DeviceIdType.MESH,
            )
            copy.start()
            outgoing.append(copy)
        local.wait()
        for step in range(1, count):
            outgoing[step - 1].wait_send()
            origin = (me + count - step) % count
            pltpu.make_async_remote_copy(
                src_ref=src_ref.at[origin],
                dst_ref=land.at[origin],
                send_sem=send_sems.at[step - 1],
                recv_sem=recv_sems.at[step - 1],
                device_id=(chip, core, origin // width, origin % width),
                device_id_type=pl.DeviceIdType.MESH,
            ).wait_recv()
        out_ref[...] = land[...]

    return pl.pallas_call(
        kernel,
        out_shape=jax.ShapeDtypeStruct(payload.shape, payload.dtype),
        in_specs=[pl.BlockSpec(memory_space=pltpu.VMEM)],
        out_specs=pl.BlockSpec(memory_space=pltpu.VMEM),
        scratch_shapes=[
            pltpu.VMEM(payload.shape, payload.dtype),
            pltpu.SemaphoreType.DMA((count - 1,)),
            pltpu.SemaphoreType.DMA((count - 1,)),
            pltpu.SemaphoreType.DMA(()),
        ],
        compiler_params=pltpu.CompilerParams(has_side_effects=True, vmem_limit_bytes=48 * 1024 * 1024),
    )(payload)


def exchange(own_state, own_grad, device_total):
    count = lax.axis_size("z") * lax.axis_size("y")
    heads, rows, cols = own_state.shape
    marks = jnp.broadcast_to(device_total[:, None, None], (heads, 8, cols))
    payload = jnp.stack(
        [
            jnp.concatenate([own_state, marks], axis=1),
            jnp.concatenate([own_grad, marks], axis=1),
        ],
        axis=1,
    )
    mine = group_all_to_all(payload)
    totals = mine[:, 0, rows, 0]
    ends = mine[:, :, :rows, :].reshape(count, 2, rows * cols)
    ids = jnp.arange(count)
    target, source, between = ids[:, None, None], ids[None, :, None], ids[None, None, :]
    fwd_span = (source < between) & (between < target)
    bwd_span = (target < between) & (between < source)
    fwd_log = jnp.sum(jnp.where(fwd_span, totals[None, None, :], 0.0), axis=2)
    bwd_log = jnp.sum(jnp.where(bwd_span, totals[None, None, :], 0.0), axis=2)
    fwd_w = jnp.where(ids[None, :] < ids[:, None], jnp.exp(fwd_log), 0.0)
    bwd_w = jnp.where(ids[None, :] > ids[:, None], jnp.exp(bwd_log), 0.0)
    weights = jnp.stack([fwd_w, bwd_w])
    entries = jnp.einsum(
        "ktj,jkx->tkx", weights, ends, precision=lax.Precision.HIGHEST,
        preferred_element_type=jnp.float32,
    ).reshape(count, 2, rows, cols)
    back = group_all_to_all(entries)
    return back[:, 0], back[:, 1]


def weight_grad_sum(tokens, grad_proj, scale):
    chips, cores = lax.axis_size("x"), lax.axis_size("core")
    width = lax.axis_size("y")
    count = lax.axis_size("z") * width
    length, depth = tokens.shape
    cols = grad_proj.shape[1]
    slab = depth // (chips * cores)
    piece = slab // count
    by_owner = tokens.T.reshape(chips, cores, slab, length)

    def kernel(tok_ref, gp_ref, out_ref, send1, land1, acc1, land2, acc2, land3, sems):
        chip, core = lax.axis_index("x"), lax.axis_index("core")
        z, y = lax.axis_index("z"), lax.axis_index("y")
        me = z * width + y
        other = 1 - core
        gp = gp_ref[...]
        for c in range(chips):
            send1[c] = jnp.dot(tok_ref[c, other], gp, preferred_element_type=jnp.float32)
        first = pltpu.make_async_remote_copy(
            src_ref=send1, dst_ref=land1, send_sem=sems.at[0, 0], recv_sem=sems.at[1, 0],
            device_id=(chip, other, z, y), device_id_type=pl.DeviceIdType.MESH,
        )
        first.start()
        for c in range(chips):
            acc1[c] = jnp.dot(tok_ref[c, core], gp, preferred_element_type=jnp.float32)
        first.wait()
        acc1[...] = acc1[...] + land1[...]
        second = []
        for step in range(1, chips):
            dest = (chip + step) % chips
            copy = pltpu.make_async_remote_copy(
                src_ref=acc1.at[dest], dst_ref=land2.at[step - 1], send_sem=sems.at[0, step],
                recv_sem=sems.at[1, step], device_id=(dest, core, z, y),
                device_id_type=pl.DeviceIdType.MESH,
            )
            copy.start()
            second.append(copy)
        for copy in second:
            copy.wait()
        total = acc1[chip]
        for step in range(1, chips):
            total = total + land2[step - 1]
        acc2[...] = total.reshape(count, piece, cols)
        third = []
        for step in range(1, count):
            dest = (me + step) % count
            copy = pltpu.make_async_remote_copy(
                src_ref=acc2.at[dest], dst_ref=land3.at[step - 1], send_sem=sems.at[0, chips + step],
                recv_sem=sems.at[1, chips + step], device_id=(chip, core, dest // width, dest % width),
                device_id_type=pl.DeviceIdType.MESH,
            )
            copy.start()
            third.append(copy)
        for copy in third:
            copy.wait()
        total = acc2[me]
        for step in range(1, count):
            total = total + land3[step - 1]
        out_ref[...] = total * scale

    return pl.pallas_call(
        kernel,
        out_shape=jax.ShapeDtypeStruct((piece, cols), jnp.float32),
        in_specs=[pl.BlockSpec(memory_space=pltpu.VMEM)] * 2,
        out_specs=pl.BlockSpec(memory_space=pltpu.VMEM),
        scratch_shapes=[
            pltpu.VMEM((chips, slab, cols), jnp.float32),
            pltpu.VMEM((chips, slab, cols), jnp.float32),
            pltpu.VMEM((chips, slab, cols), jnp.float32),
            pltpu.VMEM((chips - 1, slab, cols), jnp.float32),
            pltpu.VMEM((count, piece, cols), jnp.float32),
            pltpu.VMEM((count - 1, piece, cols), jnp.float32),
            pltpu.SemaphoreType.DMA((2, chips + count)),
        ],
        compiler_params=pltpu.CompilerParams(has_side_effects=True, vmem_limit_bytes=48 * 1024 * 1024),
    )(by_owner, grad_proj)


def on_device(layer_input, proj_weight, inputs, step_size, log_decay, skip_gain, grad_out):
    tokens = layer_input[0]
    length = tokens.shape[0]
    proj = jnp.dot(tokens, proj_weight, preferred_element_type=jnp.float32).astype(jnp.bfloat16)
    pieces = span_inputs(proj, inputs[0], grad_out[0], step_size[0], log_decay[0])
    own_state, own_grad, span_total = (pieces[9], pieces[10], pieces[6])
    empty_state = jnp.zeros((SHARD_CHANNELS, HEAD_DIM, STATE), jnp.float32)

    def advance(state_carry, piece):
        return (jnp.exp(piece[1])[:, None, None] * state_carry + piece[0], state_carry)

    last_state, local_starts = lax.scan(advance, empty_state, (own_state, span_total))
    last_grad, local_afters = lax.scan(advance, empty_state, (own_grad, span_total), reverse=True)
    state_entry, grad_entry = exchange(last_state, last_grad, jnp.sum(span_total, axis=0))
    running = jnp.cumsum(span_total, axis=0)
    before = running - span_total
    behind = jnp.sum(span_total, axis=0)[None] - running
    starts = local_starts + jnp.exp(before)[:, :, None, None] * state_entry[None]
    afters = local_afters + jnp.exp(behind)[:, :, None, None] * grad_entry[None]

    def finish(parts):
        return span_grads(*parts, skip_gain)

    grad_x, grad_proj = lax.map(finish, pieces[:9] + (starts, afters))
    grad_proj = grad_proj.reshape(length, 2 * STATE)
    scale_factor = 1.0 / (length * lax.axis_size("z") * lax.axis_size("y"))
    grad_weight = weight_grad_sum(tokens, grad_proj, scale_factor)
    return (grad_x, grad_weight)


def physical_mesh(mesh):
    grid = mesh.devices
    cores = len({d.core_on_chip for d in grid.flat})
    rows = len({d.coords[1] for d in grid.flat})
    dp, seq = grid.shape
    return Mesh(grid.reshape(dp // cores, cores, seq // rows, rows), ("x", "core", "z", "y"))


def solution(mesh):
    fine = physical_mesh(mesh)
    dp, seq = ("x", "core"), ("z", "y")
    return jax.shard_map(
        on_device,
        mesh=fine,
        in_specs=(
            P(dp, seq, None),
            P(),
            P(dp, seq, None),
            P(dp, None, seq),
            P(dp, None, seq),
            P(),
            P(dp, seq, None),
        ),
        out_specs=(P(dp, seq, None), P(dp + seq, None)),
        check_vma=False,
    )
```

```python
import jax
import jax.numpy as jnp
from jax import lax
from jax.experimental import pallas as pl
from jax.experimental.pallas import tpu as pltpu
from jax.sharding import Mesh, PartitionSpec as P

SHARD_CHANNELS = 32
HEAD_DIM = 64
STATE = 128
SPAN = 128


def span_inputs(proj, inputs, grad_out, step_size, log_decay):
    length = inputs.shape[0]
    spans = length // SPAN
    b_cols = proj[:, :STATE].reshape(spans, SPAN, STATE)
    c_cols = proj[:, STATE:].reshape(spans, SPAN, STATE)
    inputs_c = inputs.reshape(spans, SPAN, SHARD_CHANNELS, HEAD_DIM)
    grad_rows = grad_out.reshape(spans, SPAN, SHARD_CHANNELS, HEAD_DIM)
    step_rows = step_size.reshape(SHARD_CHANNELS, spans, SPAN).transpose(1, 0, 2)
    decay_sum = jnp.cumsum(
        log_decay.reshape(SHARD_CHANNELS, spans, SPAN).transpose(1, 0, 2), axis=2
    )
    span_total = decay_sum[:, :, -1]
    to_end = jnp.exp(span_total[:, :, None] - decay_sum)
    weighted = (
        inputs_c.astype(jnp.float32) * jnp.transpose(step_rows * to_end, (0, 2, 1))[..., None]
    ).astype(jnp.bfloat16)
    scaled = (
        grad_rows.astype(jnp.float32) * jnp.transpose(jnp.exp(decay_sum), (0, 2, 1))[..., None]
    ).astype(jnp.bfloat16)
    own_state = jnp.einsum("cqhp,cqn->chpn", weighted, b_cols, preferred_element_type=jnp.float32)
    own_grad = jnp.einsum("cqhp,cqn->chpn", scaled, c_cols, preferred_element_type=jnp.float32)
    return (
        b_cols,
        c_cols,
        inputs_c,
        grad_rows,
        step_rows,
        decay_sum,
        span_total,
        weighted,
        scaled,
        own_state,
        own_grad,
    )


def span_grads(
    b_cols,
    c_cols,
    inputs_c,
    grad_rows,
    step_rows,
    decay_sum,
    span_total,
    weighted,
    scaled,
    start,
    after,
    skip_gain,
):
    start_bf = start.astype(jnp.bfloat16)
    after_bf = after.astype(jnp.bfloat16)
    row_ids = lax.broadcasted_iota(jnp.int32, (SPAN, SPAN), 0)
    col_ids = lax.broadcasted_iota(jnp.int32, (SPAN, SPAN), 1)
    causal = row_ids >= col_ids
    log_gap = decay_sum[:, :, None] - decay_sum[:, None, :]
    decay_mat = jnp.exp(jnp.where(causal[None], log_gap, -jnp.inf))
    kernel = jnp.dot(c_cols, b_cols.T, preferred_element_type=jnp.float32)
    weights = (decay_mat * kernel[None]).astype(jnp.bfloat16)
    within = jnp.einsum("hsj,shp->jhp", weights, grad_rows, preferred_element_type=jnp.float32)
    carried = jnp.einsum("hpn,jn->jhp", after_bf, b_cols, preferred_element_type=jnp.float32)
    to_end = jnp.exp(span_total[:, None] - decay_sum)
    grad_x = step_rows.T[:, :, None] * (within + to_end.T[:, :, None] * carried) + skip_gain[
        None, :, None
    ] * grad_rows.astype(jnp.float32)
    intersection = jnp.einsum(
        "shp,jhp->hsj", grad_rows, inputs_c, preferred_element_type=jnp.float32
    )
    mixing = jnp.sum(decay_mat * step_rows[:, None, :] * intersection, axis=0).astype(jnp.bfloat16)
    grad_c = jnp.dot(mixing, b_cols, preferred_element_type=jnp.float32) + jnp.dot(
        scaled.reshape(SPAN, -1), start_bf.reshape(-1, STATE), preferred_element_type=jnp.float32
    )
    grad_b = jnp.dot(mixing.T, c_cols, preferred_element_type=jnp.float32) + jnp.dot(
        weighted.reshape(SPAN, -1), after_bf.reshape(-1, STATE), preferred_element_type=jnp.float32
    )
    grad_proj = jnp.concatenate([grad_b, grad_c], axis=1).astype(jnp.bfloat16)
    return (grad_x.astype(jnp.bfloat16).reshape(SPAN, -1), grad_proj)


def group_all_to_all(payload):
    width = lax.axis_size("y")
    count = lax.axis_size("z") * width

    def kernel(src_ref, out_ref, land, send_sems, recv_sems, local_sem):
        chip, core = lax.axis_index("x"), lax.axis_index("core")
        me = lax.axis_index("z") * width + lax.axis_index("y")
        local = pltpu.make_async_copy(src_ref.at[me], land.at[me], local_sem)
        local.start()
        outgoing = []
        for step in range(1, count):
            dest = (me + step) % count
            copy = pltpu.make_async_remote_copy(
                src_ref=src_ref.at[dest],
                dst_ref=land.at[me],
                send_sem=send_sems.at[step - 1],
                recv_sem=recv_sems.at[step - 1],
                device_id=(chip, core, dest // width, dest % width),
                device_id_type=pl.DeviceIdType.MESH,
            )
            copy.start()
            outgoing.append(copy)
        local.wait()
        for step in range(1, count):
            outgoing[step - 1].wait_send()
            origin = (me + count - step) % count
            pltpu.make_async_remote_copy(
                src_ref=src_ref.at[origin],
                dst_ref=land.at[origin],
                send_sem=send_sems.at[step - 1],
                recv_sem=recv_sems.at[step - 1],
                device_id=(chip, core, origin // width, origin % width),
                device_id_type=pl.DeviceIdType.MESH,
            ).wait_recv()
        out_ref[...] = land[...]

    return pl.pallas_call(
        kernel,
        out_shape=jax.ShapeDtypeStruct(payload.shape, payload.dtype),
        in_specs=[pl.BlockSpec(memory_space=pltpu.VMEM)],
        out_specs=pl.BlockSpec(memory_space=pltpu.VMEM),
        scratch_shapes=[
            pltpu.VMEM(payload.shape, payload.dtype),
            pltpu.SemaphoreType.DMA((count - 1,)),
            pltpu.SemaphoreType.DMA((count - 1,)),
            pltpu.SemaphoreType.DMA(()),
        ],
        compiler_params=pltpu.CompilerParams(has_side_effects=True, vmem_limit_bytes=48 * 1024 * 1024),
    )(payload)


def exchange(own_state, own_grad, device_total):
    count = lax.axis_size("z") * lax.axis_size("y")
    heads, rows, cols = own_state.shape
    marks = jnp.broadcast_to(device_total[:, None, None], (heads, 8, cols))
    payload = jnp.stack(
        [
            jnp.concatenate([own_state, marks], axis=1),
            jnp.concatenate([own_grad, marks], axis=1),
        ],
        axis=1,
    )
    mine = lax.all_to_all(payload, ("z", "y"), 0, 0, tiled=True)
    totals = mine[:, 0, rows, 0]
    ends = mine[:, :, :rows, :].reshape(count, 2, rows * cols)
    ids = jnp.arange(count)
    target, source, between = ids[:, None, None], ids[None, :, None], ids[None, None, :]
    fwd_span = (source < between) & (between < target)
    bwd_span = (target < between) & (between < source)
    fwd_log = jnp.sum(jnp.where(fwd_span, totals[None, None, :], 0.0), axis=2)
    bwd_log = jnp.sum(jnp.where(bwd_span, totals[None, None, :], 0.0), axis=2)
    fwd_w = jnp.where(ids[None, :] < ids[:, None], jnp.exp(fwd_log), 0.0)
    bwd_w = jnp.where(ids[None, :] > ids[:, None], jnp.exp(bwd_log), 0.0)
    weights = jnp.stack([fwd_w, bwd_w])
    entries = jnp.einsum(
        "ktj,jkx->tkx", weights, ends, precision=lax.Precision.HIGHEST,
        preferred_element_type=jnp.float32,
    ).reshape(count, 2, rows, cols)
    back = lax.all_to_all(entries, ("z", "y"), 0, 0, tiled=True)
    return back[:, 0], back[:, 1]


def weight_grad_sum(tokens, grad_proj, scale):
    chips, cores = lax.axis_size("x"), lax.axis_size("core")
    width = lax.axis_size("y")
    count = lax.axis_size("z") * width
    length, depth = tokens.shape
    cols = grad_proj.shape[1]
    slab = depth // (chips * cores)
    piece = slab // count
    by_owner = tokens.T.reshape(chips, cores, slab, length)

    def kernel(tok_ref, gp_ref, out_ref, send1, land1, acc1, land2, acc2, land3, sems):
        chip, core = lax.axis_index("x"), lax.axis_index("core")
        z, y = lax.axis_index("z"), lax.axis_index("y")
        me = z * width + y
        other = 1 - core
        gp = gp_ref[...]
        for c in range(chips):
            send1[c] = jnp.dot(tok_ref[c, other], gp, preferred_element_type=jnp.float32)
        first = pltpu.make_async_remote_copy(
            src_ref=send1, dst_ref=land1, send_sem=sems.at[0, 0], recv_sem=sems.at[1, 0],
            device_id=(chip, other, z, y), device_id_type=pl.DeviceIdType.MESH,
        )
        first.start()
        for c in range(chips):
            acc1[c] = jnp.dot(tok_ref[c, core], gp, preferred_element_type=jnp.float32)
        first.wait()
        acc1[...] = acc1[...] + land1[...]
        second = []
        for step in range(1, chips):
            dest = (chip + step) % chips
            copy = pltpu.make_async_remote_copy(
                src_ref=acc1.at[dest], dst_ref=land2.at[step - 1], send_sem=sems.at[0, step],
                recv_sem=sems.at[1, step], device_id=(dest, core, z, y),
                device_id_type=pl.DeviceIdType.MESH,
            )
            copy.start()
            second.append(copy)
        for copy in second:
            copy.wait()
        total = acc1[chip]
        for step in range(1, chips):
            total = total + land2[step - 1]
        acc2[...] = total.reshape(count, piece, cols)
        third = []
        for step in range(1, count):
            dest = (me + step) % count
            copy = pltpu.make_async_remote_copy(
                src_ref=acc2.at[dest], dst_ref=land3.at[step - 1], send_sem=sems.at[0, chips + step],
                recv_sem=sems.at[1, chips + step], device_id=(chip, core, dest // width, dest % width),
                device_id_type=pl.DeviceIdType.MESH,
            )
            copy.start()
            third.append(copy)
        for copy in third:
            copy.wait()
        total = acc2[me]
        for step in range(1, count):
            total = total + land3[step - 1]
        out_ref[...] = total * scale

    return pl.pallas_call(
        kernel,
        out_shape=jax.ShapeDtypeStruct((piece, cols), jnp.float32),
        in_specs=[pl.BlockSpec(memory_space=pltpu.VMEM)] * 2,
        out_specs=pl.BlockSpec(memory_space=pltpu.VMEM),
        scratch_shapes=[
            pltpu.VMEM((chips, slab, cols), jnp.float32),
            pltpu.VMEM((chips, slab, cols), jnp.float32),
            pltpu.VMEM((chips, slab, cols), jnp.float32),
            pltpu.VMEM((chips - 1, slab, cols), jnp.float32),
            pltpu.VMEM((count, piece, cols), jnp.float32),
            pltpu.VMEM((count - 1, piece, cols), jnp.float32),
            pltpu.SemaphoreType.DMA((2, chips + count)),
        ],
        compiler_params=pltpu.CompilerParams(has_side_effects=True, vmem_limit_bytes=48 * 1024 * 1024),
    )(by_owner, grad_proj)


def on_device(layer_input, proj_weight, inputs, step_size, log_decay, skip_gain, grad_out):
    tokens = layer_input[0]
    length = tokens.shape[0]
    proj = jnp.dot(tokens, proj_weight, preferred_element_type=jnp.float32).astype(jnp.bfloat16)
    pieces = span_inputs(proj, inputs[0], grad_out[0], step_size[0], log_decay[0])
    own_state, own_grad, span_total = (pieces[9], pieces[10], pieces[6])
    empty_state = jnp.zeros((SHARD_CHANNELS, HEAD_DIM, STATE), jnp.float32)

    def advance(state_carry, piece):
        return (jnp.exp(piece[1])[:, None, None] * state_carry + piece[0], state_carry)

    last_state, local_starts = lax.scan(advance, empty_state, (own_state, span_total))
    last_grad, local_afters = lax.scan(advance, empty_state, (own_grad, span_total), reverse=True)
    state_entry, grad_entry = exchange(last_state, last_grad, jnp.sum(span_total, axis=0))
    running = jnp.cumsum(span_total, axis=0)
    before = running - span_total
    behind = jnp.sum(span_total, axis=0)[None] - running
    starts = local_starts + jnp.exp(before)[:, :, None, None] * state_entry[None]
    afters = local_afters + jnp.exp(behind)[:, :, None, None] * grad_entry[None]

    def finish(parts):
        return span_grads(*parts, skip_gain)

    grad_x, grad_proj = lax.map(finish, pieces[:9] + (starts, afters))
    grad_proj = grad_proj.reshape(length, 2 * STATE)
    scale_factor = 1.0 / (length * lax.axis_size("z") * lax.axis_size("y"))
    grad_weight = weight_grad_sum(tokens, grad_proj, scale_factor)
    return (grad_x, grad_weight)


def physical_mesh(mesh):
    grid = mesh.devices
    cores = len({d.core_on_chip for d in grid.flat})
    rows = len({d.coords[1] for d in grid.flat})
    dp, seq = grid.shape
    return Mesh(grid.reshape(dp // cores, cores, seq // rows, rows), ("x", "core", "z", "y"))


def solution(mesh):
    fine = physical_mesh(mesh)
    dp, seq = ("x", "core"), ("z", "y")
    return jax.shard_map(
        on_device,
        mesh=fine,
        in_specs=(
            P(dp, seq, None),
            P(),
            P(dp, seq, None),
            P(dp, None, seq),
            P(dp, None, seq),
            P(),
            P(dp, seq, None),
        ),
        out_specs=(P(dp, seq, None), P(dp + seq, None)),
        check_vma=False,
    )
```

```python
import jax
import jax.numpy as jnp
from jax import lax
from jax.experimental import pallas as pl
from jax.experimental.pallas import tpu as pltpu
from jax.sharding import Mesh, PartitionSpec as P

SHARD_CHANNELS = 32
HEAD_DIM = 64
STATE = 128
SPAN = 128


def span_inputs(proj, inputs, grad_out, step_size, log_decay):
    length = inputs.shape[0]
    spans = length // SPAN
    b_cols = proj[:, :STATE].reshape(spans, SPAN, STATE)
    c_cols = proj[:, STATE:].reshape(spans, SPAN, STATE)
    inputs_c = inputs.reshape(spans, SPAN, SHARD_CHANNELS, HEAD_DIM)
    grad_rows = grad_out.reshape(spans, SPAN, SHARD_CHANNELS, HEAD_DIM)
    step_rows = step_size.reshape(SHARD_CHANNELS, spans, SPAN).transpose(1, 0, 2)
    decay_sum = jnp.cumsum(
        log_decay.reshape(SHARD_CHANNELS, spans, SPAN).transpose(1, 0, 2), axis=2
    )
    span_total = decay_sum[:, :, -1]
    to_end = jnp.exp(span_total[:, :, None] - decay_sum)
    weighted = (
        inputs_c.astype(jnp.float32) * jnp.transpose(step_rows * to_end, (0, 2, 1))[..., None]
    ).astype(jnp.bfloat16)
    scaled = (
        grad_rows.astype(jnp.float32) * jnp.transpose(jnp.exp(decay_sum), (0, 2, 1))[..., None]
    ).astype(jnp.bfloat16)
    own_state = jnp.einsum("cqhp,cqn->chpn", weighted, b_cols, preferred_element_type=jnp.float32)
    own_grad = jnp.einsum("cqhp,cqn->chpn", scaled, c_cols, preferred_element_type=jnp.float32)
    return (
        b_cols,
        c_cols,
        inputs_c,
        grad_rows,
        step_rows,
        decay_sum,
        span_total,
        weighted,
        scaled,
        own_state,
        own_grad,
    )


def span_grads(
    b_cols,
    c_cols,
    inputs_c,
    grad_rows,
    step_rows,
    decay_sum,
    span_total,
    weighted,
    scaled,
    start,
    after,
    skip_gain,
):
    start_bf = start.astype(jnp.bfloat16)
    after_bf = after.astype(jnp.bfloat16)
    row_ids = lax.broadcasted_iota(jnp.int32, (SPAN, SPAN), 0)
    col_ids = lax.broadcasted_iota(jnp.int32, (SPAN, SPAN), 1)
    causal = row_ids >= col_ids
    log_gap = decay_sum[:, :, None] - decay_sum[:, None, :]
    decay_mat = jnp.exp(jnp.where(causal[None], log_gap, -jnp.inf))
    kernel = jnp.dot(c_cols, b_cols.T, preferred_element_type=jnp.float32)
    weights = (decay_mat * kernel[None]).astype(jnp.bfloat16)
    within = jnp.einsum("hsj,shp->jhp", weights, grad_rows, preferred_element_type=jnp.float32)
    carried = jnp.einsum("hpn,jn->jhp", after_bf, b_cols, preferred_element_type=jnp.float32)
    to_end = jnp.exp(span_total[:, None] - decay_sum)
    grad_x = step_rows.T[:, :, None] * (within + to_end.T[:, :, None] * carried) + skip_gain[
        None, :, None
    ] * grad_rows.astype(jnp.float32)
    intersection = jnp.einsum(
        "shp,jhp->hsj", grad_rows, inputs_c, preferred_element_type=jnp.float32
    )
    mixing = jnp.sum(decay_mat * step_rows[:, None, :] * intersection, axis=0).astype(jnp.bfloat16)
    grad_c = jnp.dot(mixing, b_cols, preferred_element_type=jnp.float32) + jnp.dot(
        scaled.reshape(SPAN, -1), start_bf.reshape(-1, STATE), preferred_element_type=jnp.float32
    )
    grad_b = jnp.dot(mixing.T, c_cols, preferred_element_type=jnp.float32) + jnp.dot(
        weighted.reshape(SPAN, -1), after_bf.reshape(-1, STATE), preferred_element_type=jnp.float32
    )
    grad_proj = jnp.concatenate([grad_b, grad_c], axis=1).astype(jnp.bfloat16)
    return (grad_x.astype(jnp.bfloat16).reshape(SPAN, -1), grad_proj)


def group_all_to_all(payload):
    width = lax.axis_size("y")
    count = lax.axis_size("z") * width

    def kernel(src_ref, out_ref, land, send_sems, recv_sems, local_sem):
        chip, core = lax.axis_index("x"), lax.axis_index("core")
        me = lax.axis_index("z") * width + lax.axis_index("y")
        local = pltpu.make_async_copy(src_ref.at[me], land.at[me], local_sem)
        local.start()
        outgoing = []
        for step in range(1, count):
            dest = (me + step) % count
            copy = pltpu.make_async_remote_copy(
                src_ref=src_ref.at[dest],
                dst_ref=land.at[me],
                send_sem=send_sems.at[step - 1],
                recv_sem=recv_sems.at[step - 1],
                device_id=(chip, core, dest // width, dest % width),
                device_id_type=pl.DeviceIdType.MESH,
            )
            copy.start()
            outgoing.append(copy)
        local.wait()
        for step in range(1, count):
            outgoing[step - 1].wait_send()
            origin = (me + count - step) % count
            pltpu.make_async_remote_copy(
                src_ref=src_ref.at[origin],
                dst_ref=land.at[origin],
                send_sem=send_sems.at[step - 1],
                recv_sem=recv_sems.at[step - 1],
                device_id=(chip, core, origin // width, origin % width),
                device_id_type=pl.DeviceIdType.MESH,
            ).wait_recv()
        out_ref[...] = land[...]

    return pl.pallas_call(
        kernel,
        out_shape=jax.ShapeDtypeStruct(payload.shape, payload.dtype),
        in_specs=[pl.BlockSpec(memory_space=pltpu.VMEM)],
        out_specs=pl.BlockSpec(memory_space=pltpu.VMEM),
        scratch_shapes=[
            pltpu.VMEM(payload.shape, payload.dtype),
            pltpu.SemaphoreType.DMA((count - 1,)),
            pltpu.SemaphoreType.DMA((count - 1,)),
            pltpu.SemaphoreType.DMA(()),
        ],
        compiler_params=pltpu.CompilerParams(has_side_effects=True, vmem_limit_bytes=48 * 1024 * 1024),
    )(payload)


def exchange(own_state, own_grad, device_total):
    count = lax.axis_size("z") * lax.axis_size("y")
    heads, rows, cols = own_state.shape
    marks = jnp.broadcast_to(device_total[:, None, None], (heads, 8, cols))
    payload = jnp.stack(
        [
            jnp.concatenate([own_state, marks], axis=1),
            jnp.concatenate([own_grad, marks], axis=1),
        ],
        axis=1,
    )
    mine = lax.all_to_all(payload, ("z", "y"), 0, 0, tiled=True)
    totals = mine[:, 0, rows, 0]
    ends = mine[:, :, :rows, :].reshape(count, 2, rows * cols)
    ids = jnp.arange(count)
    target, source, between = ids[:, None, None], ids[None, :, None], ids[None, None, :]
    fwd_span = (source < between) & (between < target)
    bwd_span = (target < between) & (between < source)
    fwd_log = jnp.sum(jnp.where(fwd_span, totals[None, None, :], 0.0), axis=2)
    bwd_log = jnp.sum(jnp.where(bwd_span, totals[None, None, :], 0.0), axis=2)
    fwd_w = jnp.where(ids[None, :] < ids[:, None], jnp.exp(fwd_log), 0.0)
    bwd_w = jnp.where(ids[None, :] > ids[:, None], jnp.exp(bwd_log), 0.0)
    weights = jnp.stack([fwd_w, bwd_w])
    entries = jnp.einsum(
        "ktj,jkx->tkx", weights, ends, precision=lax.Precision.HIGHEST,
        preferred_element_type=jnp.float32,
    ).reshape(count, 2, rows, cols)
    back = lax.all_to_all(entries, ("z", "y"), 0, 0, tiled=True)
    return back[:, 0], back[:, 1]


def weight_grad_sum(tokens, grad_proj, scale):
    chips, cores = lax.axis_size("x"), lax.axis_size("core")
    layers, width = lax.axis_size("z"), lax.axis_size("y")
    count = layers * width
    length, depth = tokens.shape
    cols = grad_proj.shape[1]
    half = cols // 2
    slab = depth // (chips * cores)
    piece = slab // count
    by_owner = tokens.T.reshape(chips, cores, slab, length)
    mesh_id = pl.DeviceIdType.MESH
    ring = count - 1

    def kernel(tok_ref, gp_ref, out_ref, send1, land1, acc_a, acc_b, land_a, land_b,
               sum_a, sum_b, fin_a, fin_b, sems):
        chip, core = lax.axis_index("x"), lax.axis_index("core")
        z, y = lax.axis_index("z"), lax.axis_index("y")
        me = z * width + y
        spot = chip * layers + z
        other = 1 - core
        gp = gp_ref[...]
        for c in range(chips):
            send1[c] = jnp.dot(tok_ref[c, other], gp, preferred_element_type=jnp.float32)
        first = pltpu.make_async_remote_copy(
            src_ref=send1, dst_ref=land1, send_sem=sems.at[0, 0], recv_sem=sems.at[1, 0],
            device_id=(chip, other, z, y), device_id_type=mesh_id,
        )
        first.start()
        own = [jnp.dot(tok_ref[c, core], gp, preferred_element_type=jnp.float32) for c in range(chips)]
        first.wait()
        for c in range(chips):
            summed = own[c] + land1[c]
            acc_a[c] = summed[:, :half]
            blocks = summed[:, half:].reshape(layers, width, piece, half)
            for w in range(width):
                acc_b[w, c] = blocks[:, w]
        second = []
        for step in range(1, chips):
            dest = (chip + step) % chips
            second.append(pltpu.make_async_remote_copy(
                src_ref=acc_a.at[dest], dst_ref=land_a.at[step - 1], send_sem=sems.at[0, step],
                recv_sem=sems.at[1, step], device_id=(dest, core, z, y), device_id_type=mesh_id,
            ))
        for step in range(1, width):
            dest = (y + step) % width
            second.append(pltpu.make_async_remote_copy(
                src_ref=acc_b.at[dest], dst_ref=land_b.at[step - 1], send_sem=sems.at[0, chips + step],
                recv_sem=sems.at[1, chips + step], device_id=(chip, core, z, dest), device_id_type=mesh_id,
            ))
        for copy in second:
            copy.start()
        for copy in second:
            copy.wait()
        total = acc_a[chip]
        for step in range(1, chips):
            total = total + land_a[step - 1]
        sum_a[...] = total.reshape(count, piece, half)
        total = acc_b[y]
        for step in range(1, width):
            total = total + land_b[step - 1]
        sum_b[...] = total.reshape(chips * layers, piece, half)
        base = chips + width
        third = []
        for step in range(1, count):
            dest = (me + step) % count
            third.append(pltpu.make_async_remote_copy(
                src_ref=sum_a.at[dest], dst_ref=fin_a.at[step - 1], send_sem=sems.at[0, base + step],
                recv_sem=sems.at[1, base + step], device_id=(chip, core, dest // width, dest % width),
                device_id_type=mesh_id,
            ))
        for step in range(1, chips * layers):
            dest = (spot + step) % (chips * layers)
            third.append(pltpu.make_async_remote_copy(
                src_ref=sum_b.at[dest], dst_ref=fin_b.at[step - 1], send_sem=sems.at[0, base + ring + step],
                recv_sem=sems.at[1, base + ring + step], device_id=(dest // layers, core, dest % layers, y),
                device_id_type=mesh_id,
            ))
        for copy in third:
            copy.start()
        for copy in third:
            copy.wait()
        total = sum_a[me]
        for step in range(1, count):
            total = total + fin_a[step - 1]
        out_ref[:, :half] = total * scale
        total = sum_b[spot]
        for step in range(1, chips * layers):
            total = total + fin_b[step - 1]
        out_ref[:, half:] = total * scale

    return pl.pallas_call(
        kernel,
        out_shape=jax.ShapeDtypeStruct((piece, cols), jnp.float32),
        in_specs=[pl.BlockSpec(memory_space=pltpu.VMEM)] * 2,
        out_specs=pl.BlockSpec(memory_space=pltpu.VMEM),
        scratch_shapes=[
            pltpu.VMEM((chips, slab, cols), jnp.float32),
            pltpu.VMEM((chips, slab, cols), jnp.float32),
            pltpu.VMEM((chips, slab, half), jnp.float32),
            pltpu.VMEM((width, chips, layers, piece, half), jnp.float32),
            pltpu.VMEM((chips - 1, slab, half), jnp.float32),
            pltpu.VMEM((width - 1, chips, layers, piece, half), jnp.float32),
            pltpu.VMEM((count, piece, half), jnp.float32),
            pltpu.VMEM((chips * layers, piece, half), jnp.float32),
            pltpu.VMEM((count - 1, piece, half), jnp.float32),
            pltpu.VMEM((chips * layers - 1, piece, half), jnp.float32),
            pltpu.SemaphoreType.DMA((2, chips + width + count + chips * layers)),
        ],
        compiler_params=pltpu.CompilerParams(has_side_effects=True, vmem_limit_bytes=48 * 1024 * 1024),
    )(by_owner, grad_proj)


def on_device(layer_input, proj_weight, inputs, step_size, log_decay, skip_gain, grad_out):
    tokens = layer_input[0]
    length = tokens.shape[0]
    proj = jnp.dot(tokens, proj_weight, preferred_element_type=jnp.float32).astype(jnp.bfloat16)
    pieces = span_inputs(proj, inputs[0], grad_out[0], step_size[0], log_decay[0])
    own_state, own_grad, span_total = (pieces[9], pieces[10], pieces[6])
    empty_state = jnp.zeros((SHARD_CHANNELS, HEAD_DIM, STATE), jnp.float32)

    def advance(state_carry, piece):
        return (jnp.exp(piece[1])[:, None, None] * state_carry + piece[0], state_carry)

    last_state, local_starts = lax.scan(advance, empty_state, (own_state, span_total))
    last_grad, local_afters = lax.scan(advance, empty_state, (own_grad, span_total), reverse=True)
    state_entry, grad_entry = exchange(last_state, last_grad, jnp.sum(span_total, axis=0))
    running = jnp.cumsum(span_total, axis=0)
    before = running - span_total
    behind = jnp.sum(span_total, axis=0)[None] - running
    starts = local_starts + jnp.exp(before)[:, :, None, None] * state_entry[None]
    afters = local_afters + jnp.exp(behind)[:, :, None, None] * grad_entry[None]

    def finish(parts):
        return span_grads(*parts, skip_gain)

    grad_x, grad_proj = lax.map(finish, pieces[:9] + (starts, afters))
    grad_proj = grad_proj.reshape(length, 2 * STATE)
    scale_factor = 1.0 / (length * lax.axis_size("z") * lax.axis_size("y"))
    grad_weight = weight_grad_sum(tokens, grad_proj, scale_factor)
    return (grad_x, grad_weight)


def physical_mesh(mesh):
    grid = mesh.devices
    cores = len({d.core_on_chip for d in grid.flat})
    rows = len({d.coords[1] for d in grid.flat})
    dp, seq = grid.shape
    return Mesh(grid.reshape(dp // cores, cores, seq // rows, rows), ("x", "core", "z", "y"))


def solution(mesh):
    fine = physical_mesh(mesh)
    dp, seq = ("x", "core"), ("z", "y")
    return jax.shard_map(
        on_device,
        mesh=fine,
        in_specs=(
            P(dp, seq, None),
            P(),
            P(dp, seq, None),
            P(dp, None, seq),
            P(dp, None, seq),
            P(),
            P(dp, seq, None),
        ),
        out_specs=(P(dp, seq, None), P(dp + seq, None)),
        check_vma=False,
    )
```

```python
import jax
import jax.numpy as jnp
from jax import lax
from jax.experimental import pallas as pl
from jax.experimental.pallas import tpu as pltpu
from jax.sharding import Mesh, PartitionSpec as P

SHARD_CHANNELS = 32
HEAD_DIM = 64
STATE = 128
SPAN = 128


def span_inputs(proj, inputs, grad_out, step_size, log_decay):
    length = inputs.shape[0]
    spans = length // SPAN
    b_cols = proj[:, :STATE].reshape(spans, SPAN, STATE)
    c_cols = proj[:, STATE:].reshape(spans, SPAN, STATE)
    inputs_c = inputs.reshape(spans, SPAN, SHARD_CHANNELS, HEAD_DIM)
    grad_rows = grad_out.reshape(spans, SPAN, SHARD_CHANNELS, HEAD_DIM)
    step_rows = step_size.reshape(SHARD_CHANNELS, spans, SPAN).transpose(1, 0, 2)
    decay_sum = jnp.cumsum(
        log_decay.reshape(SHARD_CHANNELS, spans, SPAN).transpose(1, 0, 2), axis=2
    )
    span_total = decay_sum[:, :, -1]
    to_end = jnp.exp(span_total[:, :, None] - decay_sum)
    weighted = (
        inputs_c.astype(jnp.float32) * jnp.transpose(step_rows * to_end, (0, 2, 1))[..., None]
    ).astype(jnp.bfloat16)
    scaled = (
        grad_rows.astype(jnp.float32) * jnp.transpose(jnp.exp(decay_sum), (0, 2, 1))[..., None]
    ).astype(jnp.bfloat16)
    own_state = jnp.einsum("cqhp,cqn->chpn", weighted, b_cols, preferred_element_type=jnp.float32)
    own_grad = jnp.einsum("cqhp,cqn->chpn", scaled, c_cols, preferred_element_type=jnp.float32)
    return (
        b_cols,
        c_cols,
        inputs_c,
        grad_rows,
        step_rows,
        decay_sum,
        span_total,
        weighted,
        scaled,
        own_state,
        own_grad,
    )


def span_grads(
    b_cols,
    c_cols,
    inputs_c,
    grad_rows,
    step_rows,
    decay_sum,
    span_total,
    weighted,
    scaled,
    start,
    after,
    skip_gain,
):
    start_bf = start.astype(jnp.bfloat16)
    after_bf = after.astype(jnp.bfloat16)
    row_ids = lax.broadcasted_iota(jnp.int32, (SPAN, SPAN), 0)
    col_ids = lax.broadcasted_iota(jnp.int32, (SPAN, SPAN), 1)
    causal = row_ids >= col_ids
    log_gap = decay_sum[:, :, None] - decay_sum[:, None, :]
    decay_mat = jnp.exp(jnp.where(causal[None], log_gap, -jnp.inf))
    kernel = jnp.dot(c_cols, b_cols.T, preferred_element_type=jnp.float32)
    weights = (decay_mat * kernel[None]).astype(jnp.bfloat16)
    within = jnp.einsum("hsj,shp->jhp", weights, grad_rows, preferred_element_type=jnp.float32)
    carried = jnp.einsum("hpn,jn->jhp", after_bf, b_cols, preferred_element_type=jnp.float32)
    to_end = jnp.exp(span_total[:, None] - decay_sum)
    grad_x = step_rows.T[:, :, None] * (within + to_end.T[:, :, None] * carried) + skip_gain[
        None, :, None
    ] * grad_rows.astype(jnp.float32)
    intersection = jnp.einsum(
        "shp,jhp->hsj", grad_rows, inputs_c, preferred_element_type=jnp.float32
    )
    mixing = jnp.sum(decay_mat * step_rows[:, None, :] * intersection, axis=0).astype(jnp.bfloat16)
    grad_c = jnp.dot(mixing, b_cols, preferred_element_type=jnp.float32) + jnp.dot(
        scaled.reshape(SPAN, -1), start_bf.reshape(-1, STATE), preferred_element_type=jnp.float32
    )
    grad_b = jnp.dot(mixing.T, c_cols, preferred_element_type=jnp.float32) + jnp.dot(
        weighted.reshape(SPAN, -1), after_bf.reshape(-1, STATE), preferred_element_type=jnp.float32
    )
    grad_proj = jnp.concatenate([grad_b, grad_c], axis=1).astype(jnp.bfloat16)
    return (grad_x.astype(jnp.bfloat16).reshape(SPAN, -1), grad_proj)


def group_all_to_all(payload):
    width = lax.axis_size("y")
    count = lax.axis_size("z") * width

    def kernel(src_ref, out_ref, land, send_sems, recv_sems, local_sem):
        chip, core = lax.axis_index("x"), lax.axis_index("core")
        me = lax.axis_index("z") * width + lax.axis_index("y")
        local = pltpu.make_async_copy(src_ref.at[me], land.at[me], local_sem)
        local.start()
        outgoing = []
        for step in range(1, count):
            dest = (me + step) % count
            copy = pltpu.make_async_remote_copy(
                src_ref=src_ref.at[dest],
                dst_ref=land.at[me],
                send_sem=send_sems.at[step - 1],
                recv_sem=recv_sems.at[step - 1],
                device_id=(chip, core, dest // width, dest % width),
                device_id_type=pl.DeviceIdType.MESH,
            )
            copy.start()
            outgoing.append(copy)
        local.wait()
        for step in range(1, count):
            outgoing[step - 1].wait_send()
            origin = (me + count - step) % count
            pltpu.make_async_remote_copy(
                src_ref=src_ref.at[origin],
                dst_ref=land.at[origin],
                send_sem=send_sems.at[step - 1],
                recv_sem=recv_sems.at[step - 1],
                device_id=(chip, core, origin // width, origin % width),
                device_id_type=pl.DeviceIdType.MESH,
            ).wait_recv()
        out_ref[...] = land[...]

    return pl.pallas_call(
        kernel,
        out_shape=jax.ShapeDtypeStruct(payload.shape, payload.dtype),
        in_specs=[pl.BlockSpec(memory_space=pltpu.VMEM)],
        out_specs=pl.BlockSpec(memory_space=pltpu.VMEM),
        scratch_shapes=[
            pltpu.VMEM(payload.shape, payload.dtype),
            pltpu.SemaphoreType.DMA((count - 1,)),
            pltpu.SemaphoreType.DMA((count - 1,)),
            pltpu.SemaphoreType.DMA(()),
        ],
        compiler_params=pltpu.CompilerParams(has_side_effects=True, vmem_limit_bytes=48 * 1024 * 1024),
    )(payload)


def chain_kernel(ends_ref, out_ref):
    count, _, _ = ends_ref.shape
    rows = out_ref.shape[1] // 2
    carry = jnp.zeros((rows, out_ref.shape[2]), jnp.float32)
    for j in range(count):
        out_ref[j, :rows] = carry
        carry = jnp.exp(ends_ref[j, 2 * rows : 2 * rows + 1]) * carry + ends_ref[j, :rows]
    carry = jnp.zeros_like(carry)
    for j in reversed(range(count)):
        out_ref[j, rows:] = carry
        carry = jnp.exp(ends_ref[j, 2 * rows : 2 * rows + 1]) * carry + ends_ref[j, rows : 2 * rows]


def exchange(own_state, own_grad, device_total):
    heads, rows, cols = own_state.shape
    marks = jnp.broadcast_to(device_total[:, None, None], (heads, 8, cols))
    payload = jnp.concatenate([own_state, own_grad, marks], axis=1)
    mine = lax.all_to_all(payload, ("z", "y"), 0, 0, tiled=True)
    entries = pl.pallas_call(
        chain_kernel,
        out_shape=jax.ShapeDtypeStruct((heads, 2 * rows, cols), jnp.float32),
        in_specs=[pl.BlockSpec(memory_space=pltpu.VMEM)],
        out_specs=pl.BlockSpec(memory_space=pltpu.VMEM),
    )(mine)
    back = lax.all_to_all(entries, ("z", "y"), 0, 0, tiled=True)
    return back[:, :rows], back[:, rows:]


def weight_grad_sum(tokens, grad_proj, scale):
    chips, cores = lax.axis_size("x"), lax.axis_size("core")
    layers, width = lax.axis_size("z"), lax.axis_size("y")
    count = layers * width
    length, depth = tokens.shape
    cols = grad_proj.shape[1]
    half = cols // 2
    slab = depth // (chips * cores)
    piece = slab // count
    by_owner = tokens.T.reshape(chips, cores, slab, length)
    mesh_id = pl.DeviceIdType.MESH
    ring = count - 1

    def kernel(tok_ref, gp_ref, out_ref, send1, land1, acc_a, acc_b, land_a, land_b,
               sum_a, sum_b, fin_a, fin_b, sems):
        chip, core = lax.axis_index("x"), lax.axis_index("core")
        z, y = lax.axis_index("z"), lax.axis_index("y")
        me = z * width + y
        spot = chip * layers + z
        other = 1 - core
        gp = gp_ref[...]
        for c in range(chips):
            send1[c] = jnp.dot(tok_ref[c, other], gp, preferred_element_type=jnp.float32)
        first = pltpu.make_async_remote_copy(
            src_ref=send1, dst_ref=land1, send_sem=sems.at[0, 0], recv_sem=sems.at[1, 0],
            device_id=(chip, other, z, y), device_id_type=mesh_id,
        )
        first.start()
        own = [jnp.dot(tok_ref[c, core], gp, preferred_element_type=jnp.float32) for c in range(chips)]
        first.wait()
        for c in range(chips):
            summed = own[c] + land1[c]
            acc_a[c] = summed[:, :half]
            blocks = summed[:, half:].reshape(layers, width, piece, half)
            for w in range(width):
                acc_b[w, c] = blocks[:, w]
        second = []
        for step in range(1, chips):
            dest = (chip + step) % chips
            second.append(pltpu.make_async_remote_copy(
                src_ref=acc_a.at[dest], dst_ref=land_a.at[step - 1], send_sem=sems.at[0, step],
                recv_sem=sems.at[1, step], device_id=(dest, core, z, y), device_id_type=mesh_id,
            ))
        for step in range(1, width):
            dest = (y + step) % width
            second.append(pltpu.make_async_remote_copy(
                src_ref=acc_b.at[dest], dst_ref=land_b.at[step - 1], send_sem=sems.at[0, chips + step],
                recv_sem=sems.at[1, chips + step], device_id=(chip, core, z, dest), device_id_type=mesh_id,
            ))
        for copy in second:
            copy.start()
        for copy in second:
            copy.wait()
        total = acc_a[chip]
        for step in range(1, chips):
            total = total + land_a[step - 1]
        sum_a[...] = total.reshape(count, piece, half)
        total = acc_b[y]
        for step in range(1, width):
            total = total + land_b[step - 1]
        sum_b[...] = total.reshape(chips * layers, piece, half)
        base = chips + width
        third = []
        for step in range(1, count):
            dest = (me + step) % count
            third.append(pltpu.make_async_remote_copy(
                src_ref=sum_a.at[dest], dst_ref=fin_a.at[step - 1], send_sem=sems.at[0, base + step],
                recv_sem=sems.at[1, base + step], device_id=(chip, core, dest // width, dest % width),
                device_id_type=mesh_id,
            ))
        for step in range(1, chips * layers):
            dest = (spot + step) % (chips * layers)
            third.append(pltpu.make_async_remote_copy(
                src_ref=sum_b.at[dest], dst_ref=fin_b.at[step - 1], send_sem=sems.at[0, base + ring + step],
                recv_sem=sems.at[1, base + ring + step], device_id=(dest // layers, core, dest % layers, y),
                device_id_type=mesh_id,
            ))
        for copy in third:
            copy.start()
        for copy in third:
            copy.wait()
        total = sum_a[me]
        for step in range(1, count):
            total = total + fin_a[step - 1]
        out_ref[:, :half] = total * scale
        total = sum_b[spot]
        for step in range(1, chips * layers):
            total = total + fin_b[step - 1]
        out_ref[:, half:] = total * scale

    return pl.pallas_call(
        kernel,
        out_shape=jax.ShapeDtypeStruct((piece, cols), jnp.float32),
        in_specs=[pl.BlockSpec(memory_space=pltpu.VMEM)] * 2,
        out_specs=pl.BlockSpec(memory_space=pltpu.VMEM),
        scratch_shapes=[
            pltpu.VMEM((chips, slab, cols), jnp.float32),
            pltpu.VMEM((chips, slab, cols), jnp.float32),
            pltpu.VMEM((chips, slab, half), jnp.float32),
            pltpu.VMEM((width, chips, layers, piece, half), jnp.float32),
            pltpu.VMEM((chips - 1, slab, half), jnp.float32),
            pltpu.VMEM((width - 1, chips, layers, piece, half), jnp.float32),
            pltpu.VMEM((count, piece, half), jnp.float32),
            pltpu.VMEM((chips * layers, piece, half), jnp.float32),
            pltpu.VMEM((count - 1, piece, half), jnp.float32),
            pltpu.VMEM((chips * layers - 1, piece, half), jnp.float32),
            pltpu.SemaphoreType.DMA((2, chips + width + count + chips * layers)),
        ],
        compiler_params=pltpu.CompilerParams(has_side_effects=True, vmem_limit_bytes=48 * 1024 * 1024),
    )(by_owner, grad_proj)


def on_device(layer_input, proj_weight, inputs, step_size, log_decay, skip_gain, grad_out):
    tokens = layer_input[0]
    length = tokens.shape[0]
    proj = jnp.dot(tokens, proj_weight, preferred_element_type=jnp.float32).astype(jnp.bfloat16)
    pieces = span_inputs(proj, inputs[0], grad_out[0], step_size[0], log_decay[0])
    own_state, own_grad, span_total = (pieces[9], pieces[10], pieces[6])
    empty_state = jnp.zeros((SHARD_CHANNELS, HEAD_DIM, STATE), jnp.float32)

    def advance(state_carry, piece):
        return (jnp.exp(piece[1])[:, None, None] * state_carry + piece[0], state_carry)

    last_state, local_starts = lax.scan(advance, empty_state, (own_state, span_total))
    last_grad, local_afters = lax.scan(advance, empty_state, (own_grad, span_total), reverse=True)
    state_entry, grad_entry = exchange(last_state, last_grad, jnp.sum(span_total, axis=0))
    running = jnp.cumsum(span_total, axis=0)
    before = running - span_total
    behind = jnp.sum(span_total, axis=0)[None] - running
    starts = local_starts + jnp.exp(before)[:, :, None, None] * state_entry[None]
    afters = local_afters + jnp.exp(behind)[:, :, None, None] * grad_entry[None]

    def finish(parts):
        return span_grads(*parts, skip_gain)

    grad_x, grad_proj = lax.map(finish, pieces[:9] + (starts, afters))
    grad_proj = grad_proj.reshape(length, 2 * STATE)
    scale_factor = 1.0 / (length * lax.axis_size("z") * lax.axis_size("y"))
    grad_weight = weight_grad_sum(tokens, grad_proj, scale_factor)
    return (grad_x, grad_weight)


def physical_mesh(mesh):
    grid = mesh.devices
    cores = len({d.core_on_chip for d in grid.flat})
    rows = len({d.coords[1] for d in grid.flat})
    dp, seq = grid.shape
    return Mesh(grid.reshape(dp // cores, cores, seq // rows, rows), ("x", "core", "z", "y"))


def solution(mesh):
    fine = physical_mesh(mesh)
    dp, seq = ("x", "core"), ("z", "y")
    return jax.shard_map(
        on_device,
        mesh=fine,
        in_specs=(
            P(dp, seq, None),
            P(),
            P(dp, seq, None),
            P(dp, None, seq),
            P(dp, None, seq),
            P(),
            P(dp, seq, None),
        ),
        out_specs=(P(dp, seq, None), P(dp + seq, None)),
        check_vma=False,
    )
```

```python
import jax
import jax.numpy as jnp
from jax import lax
from jax.experimental import pallas as pl
from jax.experimental.pallas import tpu as pltpu
from jax.sharding import Mesh, PartitionSpec as P

SHARD_CHANNELS = 32
HEAD_DIM = 64
STATE = 128
SPAN = 128


def span_inputs(proj, inputs, grad_out, step_size, log_decay):
    length = inputs.shape[0]
    spans = length // SPAN
    b_cols = proj[:, :STATE].reshape(spans, SPAN, STATE)
    c_cols = proj[:, STATE:].reshape(spans, SPAN, STATE)
    inputs_c = inputs.reshape(spans, SPAN, SHARD_CHANNELS, HEAD_DIM)
    grad_rows = grad_out.reshape(spans, SPAN, SHARD_CHANNELS, HEAD_DIM)
    step_rows = step_size.reshape(SHARD_CHANNELS, spans, SPAN).transpose(1, 0, 2)
    decay_sum = jnp.cumsum(
        log_decay.reshape(SHARD_CHANNELS, spans, SPAN).transpose(1, 0, 2), axis=2
    )
    span_total = decay_sum[:, :, -1]
    to_end = jnp.exp(span_total[:, :, None] - decay_sum)
    weighted = (
        inputs_c.astype(jnp.float32) * jnp.transpose(step_rows * to_end, (0, 2, 1))[..., None]
    ).astype(jnp.bfloat16)
    scaled = (
        grad_rows.astype(jnp.float32) * jnp.transpose(jnp.exp(decay_sum), (0, 2, 1))[..., None]
    ).astype(jnp.bfloat16)
    own_state = jnp.einsum("cqhp,cqn->chpn", weighted, b_cols, preferred_element_type=jnp.float32)
    own_grad = jnp.einsum("cqhp,cqn->chpn", scaled, c_cols, preferred_element_type=jnp.float32)
    return (
        b_cols,
        c_cols,
        inputs_c,
        grad_rows,
        step_rows,
        decay_sum,
        span_total,
        weighted,
        scaled,
        own_state,
        own_grad,
    )


def span_grads(
    b_cols,
    c_cols,
    inputs_c,
    grad_rows,
    step_rows,
    decay_sum,
    span_total,
    weighted,
    scaled,
    start,
    after,
    skip_gain,
):
    start_bf = start.astype(jnp.bfloat16)
    after_bf = after.astype(jnp.bfloat16)
    row_ids = lax.broadcasted_iota(jnp.int32, (SPAN, SPAN), 0)
    col_ids = lax.broadcasted_iota(jnp.int32, (SPAN, SPAN), 1)
    causal = row_ids >= col_ids
    log_gap = decay_sum[:, :, None] - decay_sum[:, None, :]
    decay_mat = jnp.exp(jnp.where(causal[None], log_gap, -jnp.inf))
    kernel = jnp.dot(c_cols, b_cols.T, preferred_element_type=jnp.float32)
    weights = (decay_mat * kernel[None]).astype(jnp.bfloat16)
    within = jnp.einsum("hsj,shp->jhp", weights, grad_rows, preferred_element_type=jnp.float32)
    carried = jnp.einsum("hpn,jn->jhp", after_bf, b_cols, preferred_element_type=jnp.float32)
    to_end = jnp.exp(span_total[:, None] - decay_sum)
    grad_x = step_rows.T[:, :, None] * (within + to_end.T[:, :, None] * carried) + skip_gain[
        None, :, None
    ] * grad_rows.astype(jnp.float32)
    intersection = jnp.einsum(
        "shp,jhp->hsj", grad_rows, inputs_c, preferred_element_type=jnp.float32
    )
    mixing = jnp.sum(decay_mat * step_rows[:, None, :] * intersection, axis=0).astype(jnp.bfloat16)
    grad_c = jnp.dot(mixing, b_cols, preferred_element_type=jnp.float32) + jnp.dot(
        scaled.reshape(SPAN, -1), start_bf.reshape(-1, STATE), preferred_element_type=jnp.float32
    )
    grad_b = jnp.dot(mixing.T, c_cols, preferred_element_type=jnp.float32) + jnp.dot(
        weighted.reshape(SPAN, -1), after_bf.reshape(-1, STATE), preferred_element_type=jnp.float32
    )
    grad_proj = jnp.concatenate([grad_b, grad_c], axis=1).astype(jnp.bfloat16)
    return (grad_x.astype(jnp.bfloat16).reshape(SPAN, -1), grad_proj)


def group_all_to_all(payload):
    width = lax.axis_size("y")
    count = lax.axis_size("z") * width

    def kernel(src_ref, out_ref, land, send_sems, recv_sems, local_sem):
        chip, core = lax.axis_index("x"), lax.axis_index("core")
        me = lax.axis_index("z") * width + lax.axis_index("y")
        local = pltpu.make_async_copy(src_ref.at[me], land.at[me], local_sem)
        local.start()
        outgoing = []
        for step in range(1, count):
            dest = (me + step) % count
            copy = pltpu.make_async_remote_copy(
                src_ref=src_ref.at[dest],
                dst_ref=land.at[me],
                send_sem=send_sems.at[step - 1],
                recv_sem=recv_sems.at[step - 1],
                device_id=(chip, core, dest // width, dest % width),
                device_id_type=pl.DeviceIdType.MESH,
            )
            copy.start()
            outgoing.append(copy)
        local.wait()
        for step in range(1, count):
            outgoing[step - 1].wait_send()
            origin = (me + count - step) % count
            pltpu.make_async_remote_copy(
                src_ref=src_ref.at[origin],
                dst_ref=land.at[origin],
                send_sem=send_sems.at[step - 1],
                recv_sem=recv_sems.at[step - 1],
                device_id=(chip, core, origin // width, origin % width),
                device_id_type=pl.DeviceIdType.MESH,
            ).wait_recv()
        out_ref[...] = land[...]

    return pl.pallas_call(
        kernel,
        out_shape=jax.ShapeDtypeStruct(payload.shape, payload.dtype),
        in_specs=[pl.BlockSpec(memory_space=pltpu.VMEM)],
        out_specs=pl.BlockSpec(memory_space=pltpu.VMEM),
        scratch_shapes=[
            pltpu.VMEM(payload.shape, payload.dtype),
            pltpu.SemaphoreType.DMA((count - 1,)),
            pltpu.SemaphoreType.DMA((count - 1,)),
            pltpu.SemaphoreType.DMA(()),
        ],
        compiler_params=pltpu.CompilerParams(has_side_effects=True, vmem_limit_bytes=48 * 1024 * 1024),
    )(payload)


def tiered_exchange(payload):
    width, layers = lax.axis_size("y"), lax.axis_size("z")
    heads, span, cols = payload.shape
    rows = (span - 8) // 2
    group = heads // width
    mesh_id = pl.DeviceIdType.MESH

    def kernel(pay, out_ref, land1, agg, land2, res, land3, out4, land4, sems, local):
        chip, core = lax.axis_index("x"), lax.axis_index("core")
        z, y = lax.axis_index("z"), lax.axis_index("y")

        def run(copies):
            for copy in copies:
                copy.start()
            for copy in copies:
                copy.wait()

        mine = pltpu.make_async_copy(pay.at[pl.ds(y * group, group)], land1.at[y], local.at[0])
        mine.start()
        first = []
        for step in range(1, width):
            dest = (y + step) % width
            first.append(pltpu.make_async_remote_copy(
                src_ref=pay.at[pl.ds(dest * group, group)], dst_ref=land1.at[y],
                send_sem=sems.at[0, step - 1], recv_sem=sems.at[1, step - 1],
                device_id=(chip, core, z, dest), device_id_type=mesh_id,
            ))
        run(first)
        mine.wait()
        for k in range(group):
            fwd = jnp.zeros((rows, cols), jnp.float32)
            bwd = jnp.zeros((rows, cols), jnp.float32)
            total = jnp.zeros((1, cols), jnp.float32)
            for w in range(width):
                mark = land1[w, k, 2 * rows : 2 * rows + 1]
                fwd = jnp.exp(mark) * fwd + land1[w, k, :rows]
                total = total + mark
            for w in reversed(range(width)):
                mark = land1[w, k, 2 * rows : 2 * rows + 1]
                bwd = jnp.exp(mark) * bwd + land1[w, k, rows : 2 * rows]
            agg[k, :rows] = fwd
            agg[k, rows : 2 * rows] = bwd
            agg[k, 2 * rows :] = jnp.broadcast_to(total, (8, cols))
        mine = pltpu.make_async_copy(agg.at[z], land2.at[z], local.at[1])
        mine.start()
        base = width - 1
        second = []
        for step in range(1, layers):
            dest = (z + step) % layers
            second.append(pltpu.make_async_remote_copy(
                src_ref=agg.at[dest], dst_ref=land2.at[z],
                send_sem=sems.at[0, base + step - 1], recv_sem=sems.at[1, base + step - 1],
                device_id=(chip, core, dest, y), device_id_type=mesh_id,
            ))
        run(second)
        mine.wait()
        carry = jnp.zeros((rows, cols), jnp.float32)
        for r in range(layers):
            res[r, :rows] = carry
            carry = jnp.exp(land2[r, 2 * rows : 2 * rows + 1]) * carry + land2[r, :rows]
        carry = jnp.zeros((rows, cols), jnp.float32)
        for r in reversed(range(layers)):
            res[r, rows:] = carry
            carry = jnp.exp(land2[r, 2 * rows : 2 * rows + 1]) * carry + land2[r, rows : 2 * rows]
        mine = pltpu.make_async_copy(res.at[z], land3.at[z], local.at[2])
        mine.start()
        base = width - 1 + layers - 1
        third = []
        for step in range(1, layers):
            dest = (z + step) % layers
            third.append(pltpu.make_async_remote_copy(
                src_ref=res.at[dest], dst_ref=land3.at[z],
                send_sem=sems.at[0, base + step - 1], recv_sem=sems.at[1, base + step - 1],
                device_id=(chip, core, dest, y), device_id_type=mesh_id,
            ))
        run(third)
        mine.wait()
        for k in range(group):
            carry = land3[k, :rows]
            for w in range(width):
                out4[w, k, :rows] = carry
                carry = jnp.exp(land1[w, k, 2 * rows : 2 * rows + 1]) * carry + land1[w, k, :rows]
            carry = land3[k, rows:]
            for w in reversed(range(width)):
                out4[w, k, rows:] = carry
                carry = jnp.exp(land1[w, k, 2 * rows : 2 * rows + 1]) * carry + land1[w, k, rows : 2 * rows]
        mine = pltpu.make_async_copy(out4.at[y], land4.at[y], local.at[3])
        mine.start()
        base = width - 1 + 2 * (layers - 1)
        fourth = []
        for step in range(1, width):
            dest = (y + step) % width
            fourth.append(pltpu.make_async_remote_copy(
                src_ref=out4.at[dest], dst_ref=land4.at[y],
                send_sem=sems.at[0, base + step - 1], recv_sem=sems.at[1, base + step - 1],
                device_id=(chip, core, z, dest), device_id_type=mesh_id,
            ))
        run(fourth)
        mine.wait()
        out_ref[...] = land4[...].reshape(heads, 2 * rows, cols)

    links = 2 * (width - 1) + 2 * (layers - 1)
    return pl.pallas_call(
        kernel,
        out_shape=jax.ShapeDtypeStruct((heads, 2 * rows, cols), jnp.float32),
        in_specs=[pl.BlockSpec(memory_space=pltpu.VMEM)],
        out_specs=pl.BlockSpec(memory_space=pltpu.VMEM),
        scratch_shapes=[
            pltpu.VMEM((width, group, span, cols), jnp.float32),
            pltpu.VMEM((group, span, cols), jnp.float32),
            pltpu.VMEM((layers, span, cols), jnp.float32),
            pltpu.VMEM((layers, 2 * rows, cols), jnp.float32),
            pltpu.VMEM((layers, 2 * rows, cols), jnp.float32),
            pltpu.VMEM((width, group, 2 * rows, cols), jnp.float32),
            pltpu.VMEM((width, group, 2 * rows, cols), jnp.float32),
            pltpu.SemaphoreType.DMA((2, links)),
            pltpu.SemaphoreType.DMA((4,)),
        ],
        compiler_params=pltpu.CompilerParams(has_side_effects=True, vmem_limit_bytes=48 * 1024 * 1024),
    )(payload)


def exchange(own_state, own_grad, device_total):
    heads, rows, cols = own_state.shape
    marks = jnp.broadcast_to(device_total[:, None, None], (heads, 8, cols))
    payload = jnp.concatenate([own_state, own_grad, marks], axis=1)
    back = tiered_exchange(payload)
    return back[:, :rows], back[:, rows:]


def weight_grad_sum(tokens, grad_proj, scale):
    chips, cores = lax.axis_size("x"), lax.axis_size("core")
    layers, width = lax.axis_size("z"), lax.axis_size("y")
    count = layers * width
    length, depth = tokens.shape
    cols = grad_proj.shape[1]
    half = cols // 2
    slab = depth // (chips * cores)
    piece = slab // count
    by_owner = tokens.T.reshape(chips, cores, slab, length)
    mesh_id = pl.DeviceIdType.MESH
    ring = count - 1

    def kernel(tok_ref, gp_ref, out_ref, send1, land1, acc_a, acc_b, land_a, land_b,
               sum_a, sum_b, fin_a, fin_b, sems):
        chip, core = lax.axis_index("x"), lax.axis_index("core")
        z, y = lax.axis_index("z"), lax.axis_index("y")
        me = z * width + y
        spot = chip * layers + z
        other = 1 - core
        gp = gp_ref[...]
        for c in range(chips):
            send1[c] = jnp.dot(tok_ref[c, other], gp, preferred_element_type=jnp.float32)
        first = pltpu.make_async_remote_copy(
            src_ref=send1, dst_ref=land1, send_sem=sems.at[0, 0], recv_sem=sems.at[1, 0],
            device_id=(chip, other, z, y), device_id_type=mesh_id,
        )
        first.start()
        own = [jnp.dot(tok_ref[c, core], gp, preferred_element_type=jnp.float32) for c in range(chips)]
        first.wait()
        for c in range(chips):
            summed = own[c] + land1[c]
            acc_a[c] = summed[:, :half]
            blocks = summed[:, half:].reshape(layers, width, piece, half)
            for w in range(width):
                acc_b[w, c] = blocks[:, w]
        second = []
        for step in range(1, chips):
            dest = (chip + step) % chips
            second.append(pltpu.make_async_remote_copy(
                src_ref=acc_a.at[dest], dst_ref=land_a.at[step - 1], send_sem=sems.at[0, step],
                recv_sem=sems.at[1, step], device_id=(dest, core, z, y), device_id_type=mesh_id,
            ))
        for step in range(1, width):
            dest = (y + step) % width
            second.append(pltpu.make_async_remote_copy(
                src_ref=acc_b.at[dest], dst_ref=land_b.at[step - 1], send_sem=sems.at[0, chips + step],
                recv_sem=sems.at[1, chips + step], device_id=(chip, core, z, dest), device_id_type=mesh_id,
            ))
        for copy in second:
            copy.start()
        for copy in second:
            copy.wait()
        total = acc_a[chip]
        for step in range(1, chips):
            total = total + land_a[step - 1]
        sum_a[...] = total.reshape(count, piece, half)
        total = acc_b[y]
        for step in range(1, width):
            total = total + land_b[step - 1]
        sum_b[...] = total.reshape(chips * layers, piece, half)
        base = chips + width
        third = []
        for step in range(1, count):
            dest = (me + step) % count
            third.append(pltpu.make_async_remote_copy(
                src_ref=sum_a.at[dest], dst_ref=fin_a.at[step - 1], send_sem=sems.at[0, base + step],
                recv_sem=sems.at[1, base + step], device_id=(chip, core, dest // width, dest % width),
                device_id_type=mesh_id,
            ))
        for step in range(1, chips * layers):
            dest = (spot + step) % (chips * layers)
            third.append(pltpu.make_async_remote_copy(
                src_ref=sum_b.at[dest], dst_ref=fin_b.at[step - 1], send_sem=sems.at[0, base + ring + step],
                recv_sem=sems.at[1, base + ring + step], device_id=(dest // layers, core, dest % layers, y),
                device_id_type=mesh_id,
            ))
        for copy in third:
            copy.start()
        for copy in third:
            copy.wait()
        total = sum_a[me]
        for step in range(1, count):
            total = total + fin_a[step - 1]
        out_ref[:, :half] = total * scale
        total = sum_b[spot]
        for step in range(1, chips * layers):
            total = total + fin_b[step - 1]
        out_ref[:, half:] = total * scale

    return pl.pallas_call(
        kernel,
        out_shape=jax.ShapeDtypeStruct((piece, cols), jnp.float32),
        in_specs=[pl.BlockSpec(memory_space=pltpu.VMEM)] * 2,
        out_specs=pl.BlockSpec(memory_space=pltpu.VMEM),
        scratch_shapes=[
            pltpu.VMEM((chips, slab, cols), jnp.float32),
            pltpu.VMEM((chips, slab, cols), jnp.float32),
            pltpu.VMEM((chips, slab, half), jnp.float32),
            pltpu.VMEM((width, chips, layers, piece, half), jnp.float32),
            pltpu.VMEM((chips - 1, slab, half), jnp.float32),
            pltpu.VMEM((width - 1, chips, layers, piece, half), jnp.float32),
            pltpu.VMEM((count, piece, half), jnp.float32),
            pltpu.VMEM((chips * layers, piece, half), jnp.float32),
            pltpu.VMEM((count - 1, piece, half), jnp.float32),
            pltpu.VMEM((chips * layers - 1, piece, half), jnp.float32),
            pltpu.SemaphoreType.DMA((2, chips + width + count + chips * layers)),
        ],
        compiler_params=pltpu.CompilerParams(has_side_effects=True, vmem_limit_bytes=48 * 1024 * 1024),
    )(by_owner, grad_proj)


def on_device(layer_input, proj_weight, inputs, step_size, log_decay, skip_gain, grad_out):
    tokens = layer_input[0]
    length = tokens.shape[0]
    proj = jnp.dot(tokens, proj_weight, preferred_element_type=jnp.float32).astype(jnp.bfloat16)
    pieces = span_inputs(proj, inputs[0], grad_out[0], step_size[0], log_decay[0])
    own_state, own_grad, span_total = (pieces[9], pieces[10], pieces[6])
    empty_state = jnp.zeros((SHARD_CHANNELS, HEAD_DIM, STATE), jnp.float32)

    def advance(state_carry, piece):
        return (jnp.exp(piece[1])[:, None, None] * state_carry + piece[0], state_carry)

    last_state, local_starts = lax.scan(advance, empty_state, (own_state, span_total))
    last_grad, local_afters = lax.scan(advance, empty_state, (own_grad, span_total), reverse=True)
    state_entry, grad_entry = exchange(last_state, last_grad, jnp.sum(span_total, axis=0))
    running = jnp.cumsum(span_total, axis=0)
    before = running - span_total
    behind = jnp.sum(span_total, axis=0)[None] - running
    starts = local_starts + jnp.exp(before)[:, :, None, None] * state_entry[None]
    afters = local_afters + jnp.exp(behind)[:, :, None, None] * grad_entry[None]

    def finish(parts):
        return span_grads(*parts, skip_gain)

    grad_x, grad_proj = lax.map(finish, pieces[:9] + (starts, afters))
    grad_proj = grad_proj.reshape(length, 2 * STATE)
    scale_factor = 1.0 / (length * lax.axis_size("z") * lax.axis_size("y"))
    grad_weight = weight_grad_sum(tokens, grad_proj, scale_factor)
    return (grad_x, grad_weight)


def physical_mesh(mesh):
    grid = mesh.devices
    cores = len({d.core_on_chip for d in grid.flat})
    rows = len({d.coords[1] for d in grid.flat})
    dp, seq = grid.shape
    return Mesh(grid.reshape(dp // cores, cores, seq // rows, rows), ("x", "core", "z", "y"))


def solution(mesh):
    fine = physical_mesh(mesh)
    dp, seq = ("x", "core"), ("z", "y")
    return jax.shard_map(
        on_device,
        mesh=fine,
        in_specs=(
            P(dp, seq, None),
            P(),
            P(dp, seq, None),
            P(dp, None, seq),
            P(dp, None, seq),
            P(),
            P(dp, seq, None),
        ),
        out_specs=(P(dp, seq, None), P(dp + seq, None)),
        check_vma=False,
    )
```

```python
import jax
import jax.numpy as jnp
from jax import lax
from jax.experimental import pallas as pl
from jax.experimental.pallas import tpu as pltpu
from jax.sharding import Mesh, PartitionSpec as P

SHARD_CHANNELS = 32
HEAD_DIM = 64
STATE = 128
SPAN = 128


def span_inputs(proj, inputs, grad_out, step_size, log_decay):
    length = inputs.shape[0]
    spans = length // SPAN
    b_cols = proj[:, :STATE].reshape(spans, SPAN, STATE)
    c_cols = proj[:, STATE:].reshape(spans, SPAN, STATE)
    inputs_c = inputs.reshape(spans, SPAN, SHARD_CHANNELS, HEAD_DIM)
    grad_rows = grad_out.reshape(spans, SPAN, SHARD_CHANNELS, HEAD_DIM)
    step_rows = step_size.reshape(SHARD_CHANNELS, spans, SPAN).transpose(1, 0, 2)
    decay_sum = jnp.cumsum(
        log_decay.reshape(SHARD_CHANNELS, spans, SPAN).transpose(1, 0, 2), axis=2
    )
    span_total = decay_sum[:, :, -1]
    to_end = jnp.exp(span_total[:, :, None] - decay_sum)
    weighted = (
        inputs_c.astype(jnp.float32) * jnp.transpose(step_rows * to_end, (0, 2, 1))[..., None]
    ).astype(jnp.bfloat16)
    scaled = (
        grad_rows.astype(jnp.float32) * jnp.transpose(jnp.exp(decay_sum), (0, 2, 1))[..., None]
    ).astype(jnp.bfloat16)
    own_state = jnp.einsum("cqhp,cqn->chpn", weighted, b_cols, preferred_element_type=jnp.float32)
    own_grad = jnp.einsum("cqhp,cqn->chpn", scaled, c_cols, preferred_element_type=jnp.float32)
    return (
        b_cols,
        c_cols,
        inputs_c,
        grad_rows,
        step_rows,
        decay_sum,
        span_total,
        weighted,
        scaled,
        own_state,
        own_grad,
    )


def span_grads(
    b_cols,
    c_cols,
    inputs_c,
    grad_rows,
    step_rows,
    decay_sum,
    span_total,
    weighted,
    scaled,
    start,
    after,
    skip_gain,
):
    start_bf = start.astype(jnp.bfloat16)
    after_bf = after.astype(jnp.bfloat16)
    row_ids = lax.broadcasted_iota(jnp.int32, (SPAN, SPAN), 0)
    col_ids = lax.broadcasted_iota(jnp.int32, (SPAN, SPAN), 1)
    causal = row_ids >= col_ids
    log_gap = decay_sum[:, :, None] - decay_sum[:, None, :]
    decay_mat = jnp.exp(jnp.where(causal[None], log_gap, -jnp.inf))
    kernel = jnp.dot(c_cols, b_cols.T, preferred_element_type=jnp.float32)
    weights = (decay_mat * kernel[None]).astype(jnp.bfloat16)
    within = jnp.einsum("hsj,shp->jhp", weights, grad_rows, preferred_element_type=jnp.float32)
    carried = jnp.einsum("hpn,jn->jhp", after_bf, b_cols, preferred_element_type=jnp.float32)
    to_end = jnp.exp(span_total[:, None] - decay_sum)
    grad_x = step_rows.T[:, :, None] * (within + to_end.T[:, :, None] * carried) + skip_gain[
        None, :, None
    ] * grad_rows.astype(jnp.float32)
    intersection = jnp.einsum(
        "shp,jhp->hsj", grad_rows, inputs_c, preferred_element_type=jnp.float32
    )
    mixing = jnp.sum(decay_mat * step_rows[:, None, :] * intersection, axis=0).astype(jnp.bfloat16)
    grad_c = jnp.dot(mixing, b_cols, preferred_element_type=jnp.float32) + jnp.dot(
        scaled.reshape(SPAN, -1), start_bf.reshape(-1, STATE), preferred_element_type=jnp.float32
    )
    grad_b = jnp.dot(mixing.T, c_cols, preferred_element_type=jnp.float32) + jnp.dot(
        weighted.reshape(SPAN, -1), after_bf.reshape(-1, STATE), preferred_element_type=jnp.float32
    )
    grad_proj = jnp.concatenate([grad_b, grad_c], axis=1).astype(jnp.bfloat16)
    return (grad_x.astype(jnp.bfloat16).reshape(SPAN, -1), grad_proj)


def group_all_to_all(payload):
    width = lax.axis_size("y")
    count = lax.axis_size("z") * width

    def kernel(src_ref, out_ref, land, send_sems, recv_sems, local_sem):
        chip, core = lax.axis_index("x"), lax.axis_index("core")
        me = lax.axis_index("z") * width + lax.axis_index("y")
        local = pltpu.make_async_copy(src_ref.at[me], land.at[me], local_sem)
        local.start()
        outgoing = []
        for step in range(1, count):
            dest = (me + step) % count
            copy = pltpu.make_async_remote_copy(
                src_ref=src_ref.at[dest],
                dst_ref=land.at[me],
                send_sem=send_sems.at[step - 1],
                recv_sem=recv_sems.at[step - 1],
                device_id=(chip, core, dest // width, dest % width),
                device_id_type=pl.DeviceIdType.MESH,
            )
            copy.start()
            outgoing.append(copy)
        local.wait()
        for step in range(1, count):
            outgoing[step - 1].wait_send()
            origin = (me + count - step) % count
            pltpu.make_async_remote_copy(
                src_ref=src_ref.at[origin],
                dst_ref=land.at[origin],
                send_sem=send_sems.at[step - 1],
                recv_sem=recv_sems.at[step - 1],
                device_id=(chip, core, origin // width, origin % width),
                device_id_type=pl.DeviceIdType.MESH,
            ).wait_recv()
        out_ref[...] = land[...]

    return pl.pallas_call(
        kernel,
        out_shape=jax.ShapeDtypeStruct(payload.shape, payload.dtype),
        in_specs=[pl.BlockSpec(memory_space=pltpu.VMEM)],
        out_specs=pl.BlockSpec(memory_space=pltpu.VMEM),
        scratch_shapes=[
            pltpu.VMEM(payload.shape, payload.dtype),
            pltpu.SemaphoreType.DMA((count - 1,)),
            pltpu.SemaphoreType.DMA((count - 1,)),
            pltpu.SemaphoreType.DMA(()),
        ],
        compiler_params=pltpu.CompilerParams(has_side_effects=True, vmem_limit_bytes=48 * 1024 * 1024),
    )(payload)


def tiered_exchange(payload):
    width, layers = lax.axis_size("y"), lax.axis_size("z")
    heads, span, cols = payload.shape
    rows = (span - 8) // 2
    group = heads // width
    mesh_id = pl.DeviceIdType.MESH

    def kernel(pay, out_ref, land1, agg, land2, res, land3, out4, land4, sems, local):
        chip, core = lax.axis_index("x"), lax.axis_index("core")
        z, y = lax.axis_index("z"), lax.axis_index("y")
        barrier = pltpu.get_barrier_semaphore()
        for step in range(1, width):
            pl.semaphore_signal(barrier, inc=1, device_id=(chip, core, z, (y + step) % width), device_id_type=mesh_id)
        for step in range(1, layers):
            pl.semaphore_signal(barrier, inc=1, device_id=(chip, core, (z + step) % layers, y), device_id_type=mesh_id)
        pl.semaphore_wait(barrier, width - 1 + layers - 1)

        def run(copies):
            for copy in copies:
                copy.start()
            for copy in copies:
                copy.wait()

        mine = pltpu.make_async_copy(pay.at[pl.ds(y * group, group)], land1.at[y], local.at[0])
        mine.start()
        first = []
        for step in range(1, width):
            dest = (y + step) % width
            first.append(pltpu.make_async_remote_copy(
                src_ref=pay.at[pl.ds(dest * group, group)], dst_ref=land1.at[y],
                send_sem=sems.at[0, step - 1], recv_sem=sems.at[1, step - 1],
                device_id=(chip, core, z, dest), device_id_type=mesh_id,
            ))
        run(first)
        mine.wait()
        for k in range(group):
            fwd = jnp.zeros((rows, cols), jnp.float32)
            bwd = jnp.zeros((rows, cols), jnp.float32)
            total = jnp.zeros((1, cols), jnp.float32)
            for w in range(width):
                mark = land1[w, k, 2 * rows : 2 * rows + 1]
                fwd = jnp.exp(mark) * fwd + land1[w, k, :rows]
                total = total + mark
            for w in reversed(range(width)):
                mark = land1[w, k, 2 * rows : 2 * rows + 1]
                bwd = jnp.exp(mark) * bwd + land1[w, k, rows : 2 * rows]
            agg[k, :rows] = fwd
            agg[k, rows : 2 * rows] = bwd
            agg[k, 2 * rows :] = jnp.broadcast_to(total, (8, cols))
        mine = pltpu.make_async_copy(agg.at[z], land2.at[z], local.at[1])
        mine.start()
        base = width - 1
        second = []
        for step in range(1, layers):
            dest = (z + step) % layers
            second.append(pltpu.make_async_remote_copy(
                src_ref=agg.at[dest], dst_ref=land2.at[z],
                send_sem=sems.at[0, base + step - 1], recv_sem=sems.at[1, base + step - 1],
                device_id=(chip, core, dest, y), device_id_type=mesh_id,
            ))
        run(second)
        mine.wait()
        carry = jnp.zeros((rows, cols), jnp.float32)
        for r in range(layers):
            res[r, :rows] = carry
            carry = jnp.exp(land2[r, 2 * rows : 2 * rows + 1]) * carry + land2[r, :rows]
        carry = jnp.zeros((rows, cols), jnp.float32)
        for r in reversed(range(layers)):
            res[r, rows:] = carry
            carry = jnp.exp(land2[r, 2 * rows : 2 * rows + 1]) * carry + land2[r, rows : 2 * rows]
        mine = pltpu.make_async_copy(res.at[z], land3.at[z], local.at[2])
        mine.start()
        base = width - 1 + layers - 1
        third = []
        for step in range(1, layers):
            dest = (z + step) % layers
            third.append(pltpu.make_async_remote_copy(
                src_ref=res.at[dest], dst_ref=land3.at[z],
                send_sem=sems.at[0, base + step - 1], recv_sem=sems.at[1, base + step - 1],
                device_id=(chip, core, dest, y), device_id_type=mesh_id,
            ))
        run(third)
        mine.wait()
        for k in range(group):
            carry = land3[k, :rows]
            for w in range(width):
                out4[w, k, :rows] = carry
                carry = jnp.exp(land1[w, k, 2 * rows : 2 * rows + 1]) * carry + land1[w, k, :rows]
            carry = land3[k, rows:]
            for w in reversed(range(width)):
                out4[w, k, rows:] = carry
                carry = jnp.exp(land1[w, k, 2 * rows : 2 * rows + 1]) * carry + land1[w, k, rows : 2 * rows]
        mine = pltpu.make_async_copy(out4.at[y], land4.at[y], local.at[3])
        mine.start()
        base = width - 1 + 2 * (layers - 1)
        fourth = []
        for step in range(1, width):
            dest = (y + step) % width
            fourth.append(pltpu.make_async_remote_copy(
                src_ref=out4.at[dest], dst_ref=land4.at[y],
                send_sem=sems.at[0, base + step - 1], recv_sem=sems.at[1, base + step - 1],
                device_id=(chip, core, z, dest), device_id_type=mesh_id,
            ))
        run(fourth)
        mine.wait()
        out_ref[...] = land4[...].reshape(heads, 2 * rows, cols)

    links = 2 * (width - 1) + 2 * (layers - 1)
    return pl.pallas_call(
        kernel,
        out_shape=jax.ShapeDtypeStruct((heads, 2 * rows, cols), jnp.float32),
        in_specs=[pl.BlockSpec(memory_space=pltpu.VMEM)],
        out_specs=pl.BlockSpec(memory_space=pltpu.VMEM),
        scratch_shapes=[
            pltpu.VMEM((width, group, span, cols), jnp.float32),
            pltpu.VMEM((group, span, cols), jnp.float32),
            pltpu.VMEM((layers, span, cols), jnp.float32),
            pltpu.VMEM((layers, 2 * rows, cols), jnp.float32),
            pltpu.VMEM((layers, 2 * rows, cols), jnp.float32),
            pltpu.VMEM((width, group, 2 * rows, cols), jnp.float32),
            pltpu.VMEM((width, group, 2 * rows, cols), jnp.float32),
            pltpu.SemaphoreType.DMA((2, links)),
            pltpu.SemaphoreType.DMA((4,)),
        ],
        compiler_params=pltpu.CompilerParams(
            collective_id=0, has_side_effects=True, vmem_limit_bytes=48 * 1024 * 1024
        ),
    )(payload)


def exchange(own_state, own_grad, device_total):
    heads, rows, cols = own_state.shape
    marks = jnp.broadcast_to(device_total[:, None, None], (heads, 8, cols))
    payload = jnp.concatenate([own_state, own_grad, marks], axis=1)
    back = tiered_exchange(payload)
    return back[:, :rows], back[:, rows:]


def weight_grad_sum(tokens, grad_proj, scale):
    chips, cores = lax.axis_size("x"), lax.axis_size("core")
    layers, width = lax.axis_size("z"), lax.axis_size("y")
    count = layers * width
    length, depth = tokens.shape
    cols = grad_proj.shape[1]
    half = cols // 2
    slab = depth // (chips * cores)
    piece = slab // count
    by_owner = tokens.T.reshape(chips, cores, slab, length)
    mesh_id = pl.DeviceIdType.MESH
    ring = count - 1

    def kernel(tok_ref, gp_ref, out_ref, send1, land1, acc_a, acc_b, land_a, land_b,
               sum_a, sum_b, fin_a, fin_b, sems):
        chip, core = lax.axis_index("x"), lax.axis_index("core")
        z, y = lax.axis_index("z"), lax.axis_index("y")
        me = z * width + y
        spot = chip * layers + z
        other = 1 - core
        barrier = pltpu.get_barrier_semaphore()
        pl.semaphore_signal(barrier, inc=1, device_id=(chip, other, z, y), device_id_type=mesh_id)
        for step in range(1, count):
            dest = (me + step) % count
            pl.semaphore_signal(barrier, inc=1, device_id=(chip, core, dest // width, dest % width), device_id_type=mesh_id)
        for step in range(1, chips * layers):
            dest = (spot + step) % (chips * layers)
            pl.semaphore_signal(barrier, inc=1, device_id=(dest // layers, core, dest % layers, y), device_id_type=mesh_id)
        pl.semaphore_wait(barrier, count + chips * layers - 1)
        gp = gp_ref[...]
        for c in range(chips):
            send1[c] = jnp.dot(tok_ref[c, other], gp, preferred_element_type=jnp.float32)
        first = pltpu.make_async_remote_copy(
            src_ref=send1, dst_ref=land1, send_sem=sems.at[0, 0], recv_sem=sems.at[1, 0],
            device_id=(chip, other, z, y), device_id_type=mesh_id,
        )
        first.start()
        own = [jnp.dot(tok_ref[c, core], gp, preferred_element_type=jnp.float32) for c in range(chips)]
        first.wait()
        for c in range(chips):
            summed = own[c] + land1[c]
            acc_a[c] = summed[:, :half]
            blocks = summed[:, half:].reshape(layers, width, piece, half)
            for w in range(width):
                acc_b[w, c] = blocks[:, w]
        second = []
        for step in range(1, chips):
            dest = (chip + step) % chips
            second.append(pltpu.make_async_remote_copy(
                src_ref=acc_a.at[dest], dst_ref=land_a.at[step - 1], send_sem=sems.at[0, step],
                recv_sem=sems.at[1, step], device_id=(dest, core, z, y), device_id_type=mesh_id,
            ))
        for step in range(1, width):
            dest = (y + step) % width
            second.append(pltpu.make_async_remote_copy(
                src_ref=acc_b.at[dest], dst_ref=land_b.at[step - 1], send_sem=sems.at[0, chips + step],
                recv_sem=sems.at[1, chips + step], device_id=(chip, core, z, dest), device_id_type=mesh_id,
            ))
        for copy in second:
            copy.start()
        for copy in second:
            copy.wait()
        total = acc_a[chip]
        for step in range(1, chips):
            total = total + land_a[step - 1]
        sum_a[...] = total.reshape(count, piece, half)
        total = acc_b[y]
        for step in range(1, width):
            total = total + land_b[step - 1]
        sum_b[...] = total.reshape(chips * layers, piece, half)
        base = chips + width
        third = []
        for step in range(1, count):
            dest = (me + step) % count
            third.append(pltpu.make_async_remote_copy(
                src_ref=sum_a.at[dest], dst_ref=fin_a.at[step - 1], send_sem=sems.at[0, base + step],
                recv_sem=sems.at[1, base + step], device_id=(chip, core, dest // width, dest % width),
                device_id_type=mesh_id,
            ))
        for step in range(1, chips * layers):
            dest = (spot + step) % (chips * layers)
            third.append(pltpu.make_async_remote_copy(
                src_ref=sum_b.at[dest], dst_ref=fin_b.at[step - 1], send_sem=sems.at[0, base + ring + step],
                recv_sem=sems.at[1, base + ring + step], device_id=(dest // layers, core, dest % layers, y),
                device_id_type=mesh_id,
            ))
        for copy in third:
            copy.start()
        for copy in third:
            copy.wait()
        total = sum_a[me]
        for step in range(1, count):
            total = total + fin_a[step - 1]
        out_ref[:, :half] = total * scale
        total = sum_b[spot]
        for step in range(1, chips * layers):
            total = total + fin_b[step - 1]
        out_ref[:, half:] = total * scale

    return pl.pallas_call(
        kernel,
        out_shape=jax.ShapeDtypeStruct((piece, cols), jnp.float32),
        in_specs=[pl.BlockSpec(memory_space=pltpu.VMEM)] * 2,
        out_specs=pl.BlockSpec(memory_space=pltpu.VMEM),
        scratch_shapes=[
            pltpu.VMEM((chips, slab, cols), jnp.float32),
            pltpu.VMEM((chips, slab, cols), jnp.float32),
            pltpu.VMEM((chips, slab, half), jnp.float32),
            pltpu.VMEM((width, chips, layers, piece, half), jnp.float32),
            pltpu.VMEM((chips - 1, slab, half), jnp.float32),
            pltpu.VMEM((width - 1, chips, layers, piece, half), jnp.float32),
            pltpu.VMEM((count, piece, half), jnp.float32),
            pltpu.VMEM((chips * layers, piece, half), jnp.float32),
            pltpu.VMEM((count - 1, piece, half), jnp.float32),
            pltpu.VMEM((chips * layers - 1, piece, half), jnp.float32),
            pltpu.SemaphoreType.DMA((2, chips + width + count + chips * layers)),
        ],
        compiler_params=pltpu.CompilerParams(
            collective_id=1, has_side_effects=True, vmem_limit_bytes=48 * 1024 * 1024
        ),
    )(by_owner, grad_proj)


def on_device(layer_input, proj_weight, inputs, step_size, log_decay, skip_gain, grad_out):
    tokens = layer_input[0]
    length = tokens.shape[0]
    proj = jnp.dot(tokens, proj_weight, preferred_element_type=jnp.float32).astype(jnp.bfloat16)
    pieces = span_inputs(proj, inputs[0], grad_out[0], step_size[0], log_decay[0])
    own_state, own_grad, span_total = (pieces[9], pieces[10], pieces[6])
    empty_state = jnp.zeros((SHARD_CHANNELS, HEAD_DIM, STATE), jnp.float32)

    def advance(state_carry, piece):
        return (jnp.exp(piece[1])[:, None, None] * state_carry + piece[0], state_carry)

    last_state, local_starts = lax.scan(advance, empty_state, (own_state, span_total))
    last_grad, local_afters = lax.scan(advance, empty_state, (own_grad, span_total), reverse=True)
    state_entry, grad_entry = exchange(last_state, last_grad, jnp.sum(span_total, axis=0))
    running = jnp.cumsum(span_total, axis=0)
    before = running - span_total
    behind = jnp.sum(span_total, axis=0)[None] - running
    starts = local_starts + jnp.exp(before)[:, :, None, None] * state_entry[None]
    afters = local_afters + jnp.exp(behind)[:, :, None, None] * grad_entry[None]

    def finish(parts):
        return span_grads(*parts, skip_gain)

    grad_x, grad_proj = lax.map(finish, pieces[:9] + (starts, afters))
    grad_proj = grad_proj.reshape(length, 2 * STATE)
    scale_factor = 1.0 / (length * lax.axis_size("z") * lax.axis_size("y"))
    grad_weight = weight_grad_sum(tokens, grad_proj, scale_factor)
    return (grad_x, grad_weight)


def physical_mesh(mesh):
    grid = mesh.devices
    cores = len({d.core_on_chip for d in grid.flat})
    rows = len({d.coords[1] for d in grid.flat})
    dp, seq = grid.shape
    return Mesh(grid.reshape(dp // cores, cores, seq // rows, rows), ("x", "core", "z", "y"))


def solution(mesh):
    fine = physical_mesh(mesh)
    dp, seq = ("x", "core"), ("z", "y")
    return jax.shard_map(
        on_device,
        mesh=fine,
        in_specs=(
            P(dp, seq, None),
            P(),
            P(dp, seq, None),
            P(dp, None, seq),
            P(dp, None, seq),
            P(),
            P(dp, seq, None),
        ),
        out_specs=(P(dp, seq, None), P(dp + seq, None)),
        check_vma=False,
    )
```

```python
import jax
import jax.numpy as jnp
from jax import lax
from jax.experimental import pallas as pl
from jax.experimental.pallas import tpu as pltpu
from jax.sharding import Mesh, PartitionSpec as P

SHARD_CHANNELS = 32
HEAD_DIM = 64
STATE = 128
SPAN = 128


def span_inputs(proj, inputs, grad_out, step_size, log_decay):
    length = inputs.shape[0]
    spans = length // SPAN
    b_cols = proj[:, :STATE].reshape(spans, SPAN, STATE)
    c_cols = proj[:, STATE:].reshape(spans, SPAN, STATE)
    inputs_c = inputs.reshape(spans, SPAN, SHARD_CHANNELS, HEAD_DIM)
    grad_rows = grad_out.reshape(spans, SPAN, SHARD_CHANNELS, HEAD_DIM)
    step_rows = step_size.reshape(SHARD_CHANNELS, spans, SPAN).transpose(1, 0, 2)
    decay_sum = jnp.cumsum(
        log_decay.reshape(SHARD_CHANNELS, spans, SPAN).transpose(1, 0, 2), axis=2
    )
    span_total = decay_sum[:, :, -1]
    to_end = jnp.exp(span_total[:, :, None] - decay_sum)
    weighted = (
        inputs_c.astype(jnp.float32) * jnp.transpose(step_rows * to_end, (0, 2, 1))[..., None]
    ).astype(jnp.bfloat16)
    scaled = (
        grad_rows.astype(jnp.float32) * jnp.transpose(jnp.exp(decay_sum), (0, 2, 1))[..., None]
    ).astype(jnp.bfloat16)
    own_state = jnp.einsum("cqhp,cqn->chpn", weighted, b_cols, preferred_element_type=jnp.float32)
    own_grad = jnp.einsum("cqhp,cqn->chpn", scaled, c_cols, preferred_element_type=jnp.float32)
    return (
        b_cols,
        c_cols,
        inputs_c,
        grad_rows,
        step_rows,
        decay_sum,
        span_total,
        weighted,
        scaled,
        own_state,
        own_grad,
    )


def span_grads(
    b_cols,
    c_cols,
    inputs_c,
    grad_rows,
    step_rows,
    decay_sum,
    span_total,
    weighted,
    scaled,
    start,
    after,
    skip_gain,
):
    start_bf = start.astype(jnp.bfloat16)
    after_bf = after.astype(jnp.bfloat16)
    row_ids = lax.broadcasted_iota(jnp.int32, (SPAN, SPAN), 0)
    col_ids = lax.broadcasted_iota(jnp.int32, (SPAN, SPAN), 1)
    causal = row_ids >= col_ids
    log_gap = decay_sum[:, :, None] - decay_sum[:, None, :]
    decay_mat = jnp.exp(jnp.where(causal[None], log_gap, -jnp.inf))
    kernel = jnp.dot(c_cols, b_cols.T, preferred_element_type=jnp.float32)
    weights = (decay_mat * kernel[None]).astype(jnp.bfloat16)
    within = jnp.einsum("hsj,shp->jhp", weights, grad_rows, preferred_element_type=jnp.float32)
    carried = jnp.einsum("hpn,jn->jhp", after_bf, b_cols, preferred_element_type=jnp.float32)
    to_end = jnp.exp(span_total[:, None] - decay_sum)
    grad_x = step_rows.T[:, :, None] * (within + to_end.T[:, :, None] * carried) + skip_gain[
        None, :, None
    ] * grad_rows.astype(jnp.float32)
    intersection = jnp.einsum(
        "shp,jhp->hsj", grad_rows, inputs_c, preferred_element_type=jnp.float32
    )
    mixing = jnp.sum(decay_mat * step_rows[:, None, :] * intersection, axis=0).astype(jnp.bfloat16)
    grad_c = jnp.dot(mixing, b_cols, preferred_element_type=jnp.float32) + jnp.dot(
        scaled.reshape(SPAN, -1), start_bf.reshape(-1, STATE), preferred_element_type=jnp.float32
    )
    grad_b = jnp.dot(mixing.T, c_cols, preferred_element_type=jnp.float32) + jnp.dot(
        weighted.reshape(SPAN, -1), after_bf.reshape(-1, STATE), preferred_element_type=jnp.float32
    )
    grad_proj = jnp.concatenate([grad_b, grad_c], axis=1).astype(jnp.bfloat16)
    return (grad_x.astype(jnp.bfloat16).reshape(SPAN, -1), grad_proj)


def group_all_to_all(payload):
    width = lax.axis_size("y")
    count = lax.axis_size("z") * width

    def kernel(src_ref, out_ref, land, send_sems, recv_sems, local_sem):
        chip, core = lax.axis_index("x"), lax.axis_index("core")
        me = lax.axis_index("z") * width + lax.axis_index("y")
        local = pltpu.make_async_copy(src_ref.at[me], land.at[me], local_sem)
        local.start()
        outgoing = []
        for step in range(1, count):
            dest = (me + step) % count
            copy = pltpu.make_async_remote_copy(
                src_ref=src_ref.at[dest],
                dst_ref=land.at[me],
                send_sem=send_sems.at[step - 1],
                recv_sem=recv_sems.at[step - 1],
                device_id=(chip, core, dest // width, dest % width),
                device_id_type=pl.DeviceIdType.MESH,
            )
            copy.start()
            outgoing.append(copy)
        local.wait()
        for step in range(1, count):
            outgoing[step - 1].wait_send()
            origin = (me + count - step) % count
            pltpu.make_async_remote_copy(
                src_ref=src_ref.at[origin],
                dst_ref=land.at[origin],
                send_sem=send_sems.at[step - 1],
                recv_sem=recv_sems.at[step - 1],
                device_id=(chip, core, origin // width, origin % width),
                device_id_type=pl.DeviceIdType.MESH,
            ).wait_recv()
        out_ref[...] = land[...]

    return pl.pallas_call(
        kernel,
        out_shape=jax.ShapeDtypeStruct(payload.shape, payload.dtype),
        in_specs=[pl.BlockSpec(memory_space=pltpu.VMEM)],
        out_specs=pl.BlockSpec(memory_space=pltpu.VMEM),
        scratch_shapes=[
            pltpu.VMEM(payload.shape, payload.dtype),
            pltpu.SemaphoreType.DMA((count - 1,)),
            pltpu.SemaphoreType.DMA((count - 1,)),
            pltpu.SemaphoreType.DMA(()),
        ],
        compiler_params=pltpu.CompilerParams(has_side_effects=True, vmem_limit_bytes=48 * 1024 * 1024),
    )(payload)


def tiered_exchange(payload):
    width, layers = lax.axis_size("y"), lax.axis_size("z")
    heads, span, cols = payload.shape
    rows = (span - 8) // 2
    group = heads // width
    mesh_id = pl.DeviceIdType.MESH

    def kernel(pay, out_ref, land1, agg, land2, res, land3, out4, land4, relay1, relay4, sems, local):
        chip, core = lax.axis_index("x"), lax.axis_index("core")
        z, y = lax.axis_index("z"), lax.axis_index("y")
        barrier = pltpu.get_barrier_semaphore()
        for step in range(1, width):
            pl.semaphore_signal(barrier, inc=1, device_id=(chip, core, z, (y + step) % width), device_id_type=mesh_id)
        for step in range(1, layers):
            pl.semaphore_signal(barrier, inc=1, device_id=(chip, core, (z + step) % layers, y), device_id_type=mesh_id)
        pl.semaphore_wait(barrier, width - 1 + layers - 1)

        def run(copies):
            for copy in copies:
                copy.start()
            for copy in copies:
                copy.wait()

        def across_row(src_of, land, relay, base):
            near, far = (y + 1) % width, (y + width - 1) % width
            opposite = (y + 2) % width
            cut = group // 2
            direct = []
            for step, dest in ((1, near), (width - 1, far)):
                direct.append(pltpu.make_async_remote_copy(
                    src_ref=src_of(dest), dst_ref=land.at[y], send_sem=sems.at[0, base + step - 1],
                    recv_sem=sems.at[1, base + step - 1], device_id=(chip, core, z, dest), device_id_type=mesh_id,
                ))
            hop = [
                pltpu.make_async_remote_copy(
                    src_ref=src_of(opposite).at[pl.ds(0, cut)], dst_ref=relay.at[0], send_sem=sems.at[0, base + 1],
                    recv_sem=sems.at[1, base + 1], device_id=(chip, core, z, near), device_id_type=mesh_id,
                ),
                pltpu.make_async_remote_copy(
                    src_ref=src_of(opposite).at[pl.ds(cut, cut)], dst_ref=relay.at[1], send_sem=sems.at[0, base + 3],
                    recv_sem=sems.at[1, base + 3], device_id=(chip, core, z, far), device_id_type=mesh_id,
                ),
            ]
            for copy in direct + hop:
                copy.start()
            for copy in hop:
                copy.wait()
            onward = [
                pltpu.make_async_remote_copy(
                    src_ref=relay.at[0], dst_ref=land.at[far, pl.ds(0, cut)], send_sem=sems.at[0, base + 4],
                    recv_sem=sems.at[1, base + 4], device_id=(chip, core, z, near), device_id_type=mesh_id,
                ),
                pltpu.make_async_remote_copy(
                    src_ref=relay.at[1], dst_ref=land.at[near, pl.ds(cut, cut)], send_sem=sems.at[0, base + 5],
                    recv_sem=sems.at[1, base + 5], device_id=(chip, core, z, far), device_id_type=mesh_id,
                ),
            ]
            for copy in onward:
                copy.start()
            for copy in direct + onward:
                copy.wait()

        mine = pltpu.make_async_copy(pay.at[pl.ds(y * group, group)], land1.at[y], local.at[0])
        mine.start()
        across_row(lambda m: pay.at[pl.ds(m * group, group)], land1, relay1, 0)
        mine.wait()
        for k in range(group):
            fwd = jnp.zeros((rows, cols), jnp.float32)
            bwd = jnp.zeros((rows, cols), jnp.float32)
            total = jnp.zeros((1, cols), jnp.float32)
            for w in range(width):
                mark = land1[w, k, 2 * rows : 2 * rows + 1]
                fwd = jnp.exp(mark) * fwd + land1[w, k, :rows]
                total = total + mark
            for w in reversed(range(width)):
                mark = land1[w, k, 2 * rows : 2 * rows + 1]
                bwd = jnp.exp(mark) * bwd + land1[w, k, rows : 2 * rows]
            agg[k, :rows] = fwd
            agg[k, rows : 2 * rows] = bwd
            agg[k, 2 * rows :] = jnp.broadcast_to(total, (8, cols))
        mine = pltpu.make_async_copy(agg.at[z], land2.at[z], local.at[1])
        mine.start()
        base = 6
        second = []
        for step in range(1, layers):
            dest = (z + step) % layers
            second.append(pltpu.make_async_remote_copy(
                src_ref=agg.at[dest], dst_ref=land2.at[z],
                send_sem=sems.at[0, base + step - 1], recv_sem=sems.at[1, base + step - 1],
                device_id=(chip, core, dest, y), device_id_type=mesh_id,
            ))
        run(second)
        mine.wait()
        carry = jnp.zeros((rows, cols), jnp.float32)
        for r in range(layers):
            res[r, :rows] = carry
            carry = jnp.exp(land2[r, 2 * rows : 2 * rows + 1]) * carry + land2[r, :rows]
        carry = jnp.zeros((rows, cols), jnp.float32)
        for r in reversed(range(layers)):
            res[r, rows:] = carry
            carry = jnp.exp(land2[r, 2 * rows : 2 * rows + 1]) * carry + land2[r, rows : 2 * rows]
        mine = pltpu.make_async_copy(res.at[z], land3.at[z], local.at[2])
        mine.start()
        base = 6 + layers - 1
        third = []
        for step in range(1, layers):
            dest = (z + step) % layers
            third.append(pltpu.make_async_remote_copy(
                src_ref=res.at[dest], dst_ref=land3.at[z],
                send_sem=sems.at[0, base + step - 1], recv_sem=sems.at[1, base + step - 1],
                device_id=(chip, core, dest, y), device_id_type=mesh_id,
            ))
        run(third)
        mine.wait()
        for k in range(group):
            carry = land3[k, :rows]
            for w in range(width):
                out4[w, k, :rows] = carry
                carry = jnp.exp(land1[w, k, 2 * rows : 2 * rows + 1]) * carry + land1[w, k, :rows]
            carry = land3[k, rows:]
            for w in reversed(range(width)):
                out4[w, k, rows:] = carry
                carry = jnp.exp(land1[w, k, 2 * rows : 2 * rows + 1]) * carry + land1[w, k, rows : 2 * rows]
        mine = pltpu.make_async_copy(out4.at[y], land4.at[y], local.at[3])
        mine.start()
        across_row(lambda m: out4.at[m], land4, relay4, 6 + 2 * (layers - 1))
        mine.wait()
        out_ref[...] = land4[...].reshape(heads, 2 * rows, cols)

    links = 12 + 2 * (layers - 1)
    return pl.pallas_call(
        kernel,
        out_shape=jax.ShapeDtypeStruct((heads, 2 * rows, cols), jnp.float32),
        in_specs=[pl.BlockSpec(memory_space=pltpu.VMEM)],
        out_specs=pl.BlockSpec(memory_space=pltpu.VMEM),
        scratch_shapes=[
            pltpu.VMEM((width, group, span, cols), jnp.float32),
            pltpu.VMEM((group, span, cols), jnp.float32),
            pltpu.VMEM((layers, span, cols), jnp.float32),
            pltpu.VMEM((layers, 2 * rows, cols), jnp.float32),
            pltpu.VMEM((layers, 2 * rows, cols), jnp.float32),
            pltpu.VMEM((width, group, 2 * rows, cols), jnp.float32),
            pltpu.VMEM((width, group, 2 * rows, cols), jnp.float32),
            pltpu.VMEM((2, group // 2, span, cols), jnp.float32),
            pltpu.VMEM((2, group // 2, 2 * rows, cols), jnp.float32),
            pltpu.SemaphoreType.DMA((2, links)),
            pltpu.SemaphoreType.DMA((4,)),
        ],
        compiler_params=pltpu.CompilerParams(
            collective_id=0, has_side_effects=True, vmem_limit_bytes=48 * 1024 * 1024
        ),
    )(payload)


def exchange(own_state, own_grad, device_total):
    heads, rows, cols = own_state.shape
    marks = jnp.broadcast_to(device_total[:, None, None], (heads, 8, cols))
    payload = jnp.concatenate([own_state, own_grad, marks], axis=1)
    back = tiered_exchange(payload)
    return back[:, :rows], back[:, rows:]


def weight_grad_sum(tokens, grad_proj, scale):
    chips, cores = lax.axis_size("x"), lax.axis_size("core")
    layers, width = lax.axis_size("z"), lax.axis_size("y")
    count = layers * width
    length, depth = tokens.shape
    cols = grad_proj.shape[1]
    half = cols // 2
    slab = depth // (chips * cores)
    piece = slab // count
    by_owner = tokens.T.reshape(chips, cores, slab, length)
    mesh_id = pl.DeviceIdType.MESH
    ring = count - 1

    def kernel(tok_ref, gp_ref, out_ref, send1, land1, acc_a, acc_b, land_a, land_b,
               sum_a, sum_b, fin_a, fin_b, sems):
        chip, core = lax.axis_index("x"), lax.axis_index("core")
        z, y = lax.axis_index("z"), lax.axis_index("y")
        me = z * width + y
        spot = chip * layers + z
        other = 1 - core
        barrier = pltpu.get_barrier_semaphore()
        pl.semaphore_signal(barrier, inc=1, device_id=(chip, other, z, y), device_id_type=mesh_id)
        for step in range(1, count):
            dest = (me + step) % count
            pl.semaphore_signal(barrier, inc=1, device_id=(chip, core, dest // width, dest % width), device_id_type=mesh_id)
        for step in range(1, chips * layers):
            dest = (spot + step) % (chips * layers)
            pl.semaphore_signal(barrier, inc=1, device_id=(dest // layers, core, dest % layers, y), device_id_type=mesh_id)
        pl.semaphore_wait(barrier, count + chips * layers - 1)
        gp = gp_ref[...]
        for c in range(chips):
            send1[c] = jnp.dot(tok_ref[c, other], gp, preferred_element_type=jnp.float32)
        first = pltpu.make_async_remote_copy(
            src_ref=send1, dst_ref=land1, send_sem=sems.at[0, 0], recv_sem=sems.at[1, 0],
            device_id=(chip, other, z, y), device_id_type=mesh_id,
        )
        first.start()
        own = [jnp.dot(tok_ref[c, core], gp, preferred_element_type=jnp.float32) for c in range(chips)]
        first.wait()
        for c in range(chips):
            summed = own[c] + land1[c]
            acc_a[c] = summed[:, :half]
            blocks = summed[:, half:].reshape(layers, width, piece, half)
            for w in range(width):
                acc_b[w, c] = blocks[:, w]
        second = []
        for step in range(1, chips):
            dest = (chip + step) % chips
            second.append(pltpu.make_async_remote_copy(
                src_ref=acc_a.at[dest], dst_ref=land_a.at[step - 1], send_sem=sems.at[0, step],
                recv_sem=sems.at[1, step], device_id=(dest, core, z, y), device_id_type=mesh_id,
            ))
        for step in range(1, width):
            dest = (y + step) % width
            second.append(pltpu.make_async_remote_copy(
                src_ref=acc_b.at[dest], dst_ref=land_b.at[step - 1], send_sem=sems.at[0, chips + step],
                recv_sem=sems.at[1, chips + step], device_id=(chip, core, z, dest), device_id_type=mesh_id,
            ))
        for copy in second:
            copy.start()
        for copy in second:
            copy.wait()
        total = acc_a[chip]
        for step in range(1, chips):
            total = total + land_a[step - 1]
        sum_a[...] = total.reshape(count, piece, half)
        total = acc_b[y]
        for step in range(1, width):
            total = total + land_b[step - 1]
        sum_b[...] = total.reshape(chips * layers, piece, half)
        base = chips + width
        third = []
        for step in range(1, count):
            dest = (me + step) % count
            third.append(pltpu.make_async_remote_copy(
                src_ref=sum_a.at[dest], dst_ref=fin_a.at[step - 1], send_sem=sems.at[0, base + step],
                recv_sem=sems.at[1, base + step], device_id=(chip, core, dest // width, dest % width),
                device_id_type=mesh_id,
            ))
        for step in range(1, chips * layers):
            dest = (spot + step) % (chips * layers)
            third.append(pltpu.make_async_remote_copy(
                src_ref=sum_b.at[dest], dst_ref=fin_b.at[step - 1], send_sem=sems.at[0, base + ring + step],
                recv_sem=sems.at[1, base + ring + step], device_id=(dest // layers, core, dest % layers, y),
                device_id_type=mesh_id,
            ))
        for copy in third:
            copy.start()
        for copy in third:
            copy.wait()
        total = sum_a[me]
        for step in range(1, count):
            total = total + fin_a[step - 1]
        out_ref[:, :half] = total * scale
        total = sum_b[spot]
        for step in range(1, chips * layers):
            total = total + fin_b[step - 1]
        out_ref[:, half:] = total * scale

    return pl.pallas_call(
        kernel,
        out_shape=jax.ShapeDtypeStruct((piece, cols), jnp.float32),
        in_specs=[pl.BlockSpec(memory_space=pltpu.VMEM)] * 2,
        out_specs=pl.BlockSpec(memory_space=pltpu.VMEM),
        scratch_shapes=[
            pltpu.VMEM((chips, slab, cols), jnp.float32),
            pltpu.VMEM((chips, slab, cols), jnp.float32),
            pltpu.VMEM((chips, slab, half), jnp.float32),
            pltpu.VMEM((width, chips, layers, piece, half), jnp.float32),
            pltpu.VMEM((chips - 1, slab, half), jnp.float32),
            pltpu.VMEM((width - 1, chips, layers, piece, half), jnp.float32),
            pltpu.VMEM((count, piece, half), jnp.float32),
            pltpu.VMEM((chips * layers, piece, half), jnp.float32),
            pltpu.VMEM((count - 1, piece, half), jnp.float32),
            pltpu.VMEM((chips * layers - 1, piece, half), jnp.float32),
            pltpu.SemaphoreType.DMA((2, chips + width + count + chips * layers)),
        ],
        compiler_params=pltpu.CompilerParams(
            collective_id=1, has_side_effects=True, vmem_limit_bytes=48 * 1024 * 1024
        ),
    )(by_owner, grad_proj)


def on_device(layer_input, proj_weight, inputs, step_size, log_decay, skip_gain, grad_out):
    tokens = layer_input[0]
    length = tokens.shape[0]
    proj = jnp.dot(tokens, proj_weight, preferred_element_type=jnp.float32).astype(jnp.bfloat16)
    pieces = span_inputs(proj, inputs[0], grad_out[0], step_size[0], log_decay[0])
    own_state, own_grad, span_total = (pieces[9], pieces[10], pieces[6])
    empty_state = jnp.zeros((SHARD_CHANNELS, HEAD_DIM, STATE), jnp.float32)

    def advance(state_carry, piece):
        return (jnp.exp(piece[1])[:, None, None] * state_carry + piece[0], state_carry)

    last_state, local_starts = lax.scan(advance, empty_state, (own_state, span_total))
    last_grad, local_afters = lax.scan(advance, empty_state, (own_grad, span_total), reverse=True)
    state_entry, grad_entry = exchange(last_state, last_grad, jnp.sum(span_total, axis=0))
    running = jnp.cumsum(span_total, axis=0)
    before = running - span_total
    behind = jnp.sum(span_total, axis=0)[None] - running
    starts = local_starts + jnp.exp(before)[:, :, None, None] * state_entry[None]
    afters = local_afters + jnp.exp(behind)[:, :, None, None] * grad_entry[None]

    def finish(parts):
        return span_grads(*parts, skip_gain)

    grad_x, grad_proj = lax.map(finish, pieces[:9] + (starts, afters))
    grad_proj = grad_proj.reshape(length, 2 * STATE)
    scale_factor = 1.0 / (length * lax.axis_size("z") * lax.axis_size("y"))
    grad_weight = weight_grad_sum(tokens, grad_proj, scale_factor)
    return (grad_x, grad_weight)


def physical_mesh(mesh):
    grid = mesh.devices
    cores = len({d.core_on_chip for d in grid.flat})
    rows = len({d.coords[1] for d in grid.flat})
    dp, seq = grid.shape
    return Mesh(grid.reshape(dp // cores, cores, seq // rows, rows), ("x", "core", "z", "y"))


def solution(mesh):
    fine = physical_mesh(mesh)
    dp, seq = ("x", "core"), ("z", "y")
    return jax.shard_map(
        on_device,
        mesh=fine,
        in_specs=(
            P(dp, seq, None),
            P(),
            P(dp, seq, None),
            P(dp, None, seq),
            P(dp, None, seq),
            P(),
            P(dp, seq, None),
        ),
        out_specs=(P(dp, seq, None), P(dp + seq, None)),
        check_vma=False,
    )
```

```python
import jax
import jax.numpy as jnp
from jax import lax
from jax.experimental import pallas as pl
from jax.experimental.pallas import tpu as pltpu
from jax.sharding import Mesh, PartitionSpec as P

SHARD_CHANNELS = 32
HEAD_DIM = 64
STATE = 128
SPAN = 128


def span_inputs(proj, inputs, grad_out, step_size, log_decay):
    length = inputs.shape[0]
    spans = length // SPAN
    b_cols = proj[:, :STATE].reshape(spans, SPAN, STATE)
    c_cols = proj[:, STATE:].reshape(spans, SPAN, STATE)
    inputs_c = inputs.reshape(spans, SPAN, SHARD_CHANNELS, HEAD_DIM)
    grad_rows = grad_out.reshape(spans, SPAN, SHARD_CHANNELS, HEAD_DIM)
    step_rows = step_size.reshape(SHARD_CHANNELS, spans, SPAN).transpose(1, 0, 2)
    decay_sum = jnp.cumsum(
        log_decay.reshape(SHARD_CHANNELS, spans, SPAN).transpose(1, 0, 2), axis=2
    )
    span_total = decay_sum[:, :, -1]
    to_end = jnp.exp(span_total[:, :, None] - decay_sum)
    weighted = (
        inputs_c.astype(jnp.float32) * jnp.transpose(step_rows * to_end, (0, 2, 1))[..., None]
    ).astype(jnp.bfloat16)
    scaled = (
        grad_rows.astype(jnp.float32) * jnp.transpose(jnp.exp(decay_sum), (0, 2, 1))[..., None]
    ).astype(jnp.bfloat16)
    own_state = jnp.einsum("cqhp,cqn->chpn", weighted, b_cols, preferred_element_type=jnp.float32)
    own_grad = jnp.einsum("cqhp,cqn->chpn", scaled, c_cols, preferred_element_type=jnp.float32)
    return (
        b_cols,
        c_cols,
        inputs_c,
        grad_rows,
        step_rows,
        decay_sum,
        span_total,
        weighted,
        scaled,
        own_state,
        own_grad,
    )


def span_grads(
    b_cols,
    c_cols,
    inputs_c,
    grad_rows,
    step_rows,
    decay_sum,
    span_total,
    weighted,
    scaled,
    start,
    after,
    skip_gain,
):
    start_bf = start.astype(jnp.bfloat16)
    after_bf = after.astype(jnp.bfloat16)
    row_ids = lax.broadcasted_iota(jnp.int32, (SPAN, SPAN), 0)
    col_ids = lax.broadcasted_iota(jnp.int32, (SPAN, SPAN), 1)
    causal = row_ids >= col_ids
    log_gap = decay_sum[:, :, None] - decay_sum[:, None, :]
    decay_mat = jnp.exp(jnp.where(causal[None], log_gap, -jnp.inf))
    kernel = jnp.dot(c_cols, b_cols.T, preferred_element_type=jnp.float32)
    weights = (decay_mat * kernel[None]).astype(jnp.bfloat16)
    within = jnp.einsum("hsj,shp->jhp", weights, grad_rows, preferred_element_type=jnp.float32)
    carried = jnp.einsum("hpn,jn->jhp", after_bf, b_cols, preferred_element_type=jnp.float32)
    to_end = jnp.exp(span_total[:, None] - decay_sum)
    grad_x = step_rows.T[:, :, None] * (within + to_end.T[:, :, None] * carried) + skip_gain[
        None, :, None
    ] * grad_rows.astype(jnp.float32)
    intersection = jnp.einsum(
        "shp,jhp->hsj", grad_rows, inputs_c, preferred_element_type=jnp.float32
    )
    mixing = jnp.sum(decay_mat * step_rows[:, None, :] * intersection, axis=0).astype(jnp.bfloat16)
    grad_c = jnp.dot(mixing, b_cols, preferred_element_type=jnp.float32) + jnp.dot(
        scaled.reshape(SPAN, -1), start_bf.reshape(-1, STATE), preferred_element_type=jnp.float32
    )
    grad_b = jnp.dot(mixing.T, c_cols, preferred_element_type=jnp.float32) + jnp.dot(
        weighted.reshape(SPAN, -1), after_bf.reshape(-1, STATE), preferred_element_type=jnp.float32
    )
    grad_proj = jnp.concatenate([grad_b, grad_c], axis=1).astype(jnp.bfloat16)
    return (grad_x.astype(jnp.bfloat16).reshape(SPAN, -1), grad_proj)


def group_all_to_all(payload):
    width = lax.axis_size("y")
    count = lax.axis_size("z") * width

    def kernel(src_ref, out_ref, land, send_sems, recv_sems, local_sem):
        chip, core = lax.axis_index("x"), lax.axis_index("core")
        me = lax.axis_index("z") * width + lax.axis_index("y")
        local = pltpu.make_async_copy(src_ref.at[me], land.at[me], local_sem)
        local.start()
        outgoing = []
        for step in range(1, count):
            dest = (me + step) % count
            copy = pltpu.make_async_remote_copy(
                src_ref=src_ref.at[dest],
                dst_ref=land.at[me],
                send_sem=send_sems.at[step - 1],
                recv_sem=recv_sems.at[step - 1],
                device_id=(chip, core, dest // width, dest % width),
                device_id_type=pl.DeviceIdType.MESH,
            )
            copy.start()
            outgoing.append(copy)
        local.wait()
        for step in range(1, count):
            outgoing[step - 1].wait_send()
            origin = (me + count - step) % count
            pltpu.make_async_remote_copy(
                src_ref=src_ref.at[origin],
                dst_ref=land.at[origin],
                send_sem=send_sems.at[step - 1],
                recv_sem=recv_sems.at[step - 1],
                device_id=(chip, core, origin // width, origin % width),
                device_id_type=pl.DeviceIdType.MESH,
            ).wait_recv()
        out_ref[...] = land[...]

    return pl.pallas_call(
        kernel,
        out_shape=jax.ShapeDtypeStruct(payload.shape, payload.dtype),
        in_specs=[pl.BlockSpec(memory_space=pltpu.VMEM)],
        out_specs=pl.BlockSpec(memory_space=pltpu.VMEM),
        scratch_shapes=[
            pltpu.VMEM(payload.shape, payload.dtype),
            pltpu.SemaphoreType.DMA((count - 1,)),
            pltpu.SemaphoreType.DMA((count - 1,)),
            pltpu.SemaphoreType.DMA(()),
        ],
        compiler_params=pltpu.CompilerParams(has_side_effects=True, vmem_limit_bytes=48 * 1024 * 1024),
    )(payload)


def tiered_exchange(payload):
    width, layers = lax.axis_size("y"), lax.axis_size("z")
    heads, span, cols = payload.shape
    rows = (span - 8) // 2
    group = heads // width
    mesh_id = pl.DeviceIdType.MESH
    per_wave = 2 * (width - 1) + 2 * (layers - 1)

    def kernel(pay, out_ref, land1, agg, land2, res, land3, out4, land4, sems, local):
        chip, core = lax.axis_index("x"), lax.axis_index("core")
        z, y = lax.axis_index("z"), lax.axis_index("y")
        barrier = pltpu.get_barrier_semaphore()
        for step in range(1, width):
            pl.semaphore_signal(barrier, inc=1, device_id=(chip, core, z, (y + step) % width), device_id_type=mesh_id)
        for step in range(1, layers):
            pl.semaphore_signal(barrier, inc=1, device_id=(chip, core, (z + step) % layers, y), device_id_type=mesh_id)
        pl.semaphore_wait(barrier, width - 1 + layers - 1)

        def tier(src_of, dst, size, where, place, wave, base, slot):
            first = pltpu.make_async_copy(src_of(where), dst, local.at[wave, slot])
            copies = [first]
            for step in range(1, size):
                dest = (where + step) % size
                copies.append(pltpu.make_async_remote_copy(
                    src_ref=src_of(dest), dst_ref=dst, send_sem=sems.at[0, wave, base + step - 1],
                    recv_sem=sems.at[1, wave, base + step - 1], device_id=place(dest), device_id_type=mesh_id,
                ))
            for copy in copies:
                copy.start()
            return copies

        def finish(copies):
            for copy in copies:
                copy.wait()

        row_place = lambda m: (chip, core, z, m)
        col_place = lambda m: (chip, core, m, y)
        lo = (0, rows)
        n = (rows + 8, rows)
        t1 = [
            tier(lambda m, w=w: pay.at[pl.ds(m * group, group), w], land1.at[w, y], width, y, row_place, w, 0, 0)
            for w in range(2)
        ]
        for w in range(2):
            finish(t1[w])
            for k in range(group):
                carry = jnp.zeros((rows, cols), jnp.float32)
                total = jnp.zeros((1, cols), jnp.float32)
                order = range(width) if w == 0 else reversed(range(width))
                for m in order:
                    mark = land1[0, m, k, rows : rows + 1]
                    carry = jnp.exp(mark) * carry + land1[w, m, k, :rows]
                    total = total + mark
                agg[w, k, :rows] = carry
                agg[w, k, rows:] = jnp.broadcast_to(total * (1 - w), (8, cols))
            t2 = tier(lambda m, w=w: agg.at[w, m], land2.at[w, z], layers, z, col_place, w, width - 1, 1)
            if w == 0:
                t2_first = t2
        finish(t2_first)
        finish(t2)
        for w in range(2):
            carry = jnp.zeros((rows, cols), jnp.float32)
            order = range(layers) if w == 0 else reversed(range(layers))
            for r in order:
                res[w, r] = carry
                carry = jnp.exp(land2[0, r, rows : rows + 1]) * carry + land2[w, r, :rows]
            t3 = tier(lambda m, w=w: res.at[w, m], land3.at[w, z], layers, z, col_place, w, width + layers - 2, 2)
            if w == 0:
                t3_first = t3
        t4 = []
        for w, t3w in ((0, t3_first), (1, t3)):
            finish(t3w)
            for k in range(group):
                carry = land3[w, k]
                order = range(width) if w == 0 else reversed(range(width))
                for m in order:
                    out4[w, m, k] = carry
                    carry = jnp.exp(land1[0, m, k, rows : rows + 1]) * carry + land1[w, m, k, :rows]
            t4.append(tier(lambda m, w=w: out4.at[w, m], land4.at[w, y], width, y, row_place, w, width + 2 * layers - 3, 3))
        for copies in t4:
            finish(copies)
        out_ref[:, :rows] = land4[0].reshape(heads, rows, cols)
        out_ref[:, rows:] = land4[1].reshape(heads, rows, cols)

    fwd = jnp.concatenate([payload[:, :rows], payload[:, 2 * rows :]], axis=1)
    bwd = jnp.pad(payload[:, rows : 2 * rows], ((0, 0), (0, 8), (0, 0)))
    body = jnp.stack([fwd, bwd], axis=1)
    return pl.pallas_call(
        kernel,
        out_shape=jax.ShapeDtypeStruct((heads, 2 * rows, cols), jnp.float32),
        in_specs=[pl.BlockSpec(memory_space=pltpu.VMEM)],
        out_specs=pl.BlockSpec(memory_space=pltpu.VMEM),
        scratch_shapes=[
            pltpu.VMEM((2, width, group, rows + 8, cols), jnp.float32),
            pltpu.VMEM((2, group, rows + 8, cols), jnp.float32),
            pltpu.VMEM((2, layers, rows + 8, cols), jnp.float32),
            pltpu.VMEM((2, layers, rows, cols), jnp.float32),
            pltpu.VMEM((2, layers, rows, cols), jnp.float32),
            pltpu.VMEM((2, width, group, rows, cols), jnp.float32),
            pltpu.VMEM((2, width, group, rows, cols), jnp.float32),
            pltpu.SemaphoreType.DMA((2, 2, per_wave)),
            pltpu.SemaphoreType.DMA((2, 4)),
        ],
        compiler_params=pltpu.CompilerParams(
            collective_id=0, has_side_effects=True, vmem_limit_bytes=48 * 1024 * 1024
        ),
    )(body)


def exchange(own_state, own_grad, device_total):
    heads, rows, cols = own_state.shape
    marks = jnp.broadcast_to(device_total[:, None, None], (heads, 8, cols))
    payload = jnp.concatenate([own_state, own_grad, marks], axis=1)
    back = tiered_exchange(payload)
    return back[:, :rows], back[:, rows:]


def weight_grad_sum(tokens, grad_proj, scale):
    chips, cores = lax.axis_size("x"), lax.axis_size("core")
    layers, width = lax.axis_size("z"), lax.axis_size("y")
    count = layers * width
    length, depth = tokens.shape
    cols = grad_proj.shape[1]
    half = cols // 2
    slab = depth // (chips * cores)
    piece = slab // count
    by_owner = tokens.T.reshape(chips, cores, slab, length)
    mesh_id = pl.DeviceIdType.MESH
    ring = count - 1

    def kernel(tok_ref, gp_ref, out_ref, send1, land1, acc_a, acc_b, land_a, land_b,
               sum_a, sum_b, fin_a, fin_b, sems):
        chip, core = lax.axis_index("x"), lax.axis_index("core")
        z, y = lax.axis_index("z"), lax.axis_index("y")
        me = z * width + y
        spot = chip * layers + z
        other = 1 - core
        barrier = pltpu.get_barrier_semaphore()
        pl.semaphore_signal(barrier, inc=1, device_id=(chip, other, z, y), device_id_type=mesh_id)
        for step in range(1, count):
            dest = (me + step) % count
            pl.semaphore_signal(barrier, inc=1, device_id=(chip, core, dest // width, dest % width), device_id_type=mesh_id)
        for step in range(1, chips * layers):
            dest = (spot + step) % (chips * layers)
            pl.semaphore_signal(barrier, inc=1, device_id=(dest // layers, core, dest % layers, y), device_id_type=mesh_id)
        pl.semaphore_wait(barrier, count + chips * layers - 1)
        gp = gp_ref[...]
        for c in range(chips):
            send1[c] = jnp.dot(tok_ref[c, other], gp, preferred_element_type=jnp.float32)
        first = pltpu.make_async_remote_copy(
            src_ref=send1, dst_ref=land1, send_sem=sems.at[0, 0], recv_sem=sems.at[1, 0],
            device_id=(chip, other, z, y), device_id_type=mesh_id,
        )
        first.start()
        own = [jnp.dot(tok_ref[c, core], gp, preferred_element_type=jnp.float32) for c in range(chips)]
        first.wait()
        for c in range(chips):
            summed = own[c] + land1[c]
            acc_a[c] = summed[:, :half]
            blocks = summed[:, half:].reshape(layers, width, piece, half)
            for w in range(width):
                acc_b[w, c] = blocks[:, w]
        second = []
        for step in range(1, chips):
            dest = (chip + step) % chips
            second.append(pltpu.make_async_remote_copy(
                src_ref=acc_a.at[dest], dst_ref=land_a.at[step - 1], send_sem=sems.at[0, step],
                recv_sem=sems.at[1, step], device_id=(dest, core, z, y), device_id_type=mesh_id,
            ))
        for step in range(1, width):
            dest = (y + step) % width
            second.append(pltpu.make_async_remote_copy(
                src_ref=acc_b.at[dest], dst_ref=land_b.at[step - 1], send_sem=sems.at[0, chips + step],
                recv_sem=sems.at[1, chips + step], device_id=(chip, core, z, dest), device_id_type=mesh_id,
            ))
        for copy in second:
            copy.start()
        for copy in second:
            copy.wait()
        total = acc_a[chip]
        for step in range(1, chips):
            total = total + land_a[step - 1]
        sum_a[...] = total.reshape(count, piece, half)
        total = acc_b[y]
        for step in range(1, width):
            total = total + land_b[step - 1]
        sum_b[...] = total.reshape(chips * layers, piece, half)
        base = chips + width
        third = []
        for step in range(1, count):
            dest = (me + step) % count
            third.append(pltpu.make_async_remote_copy(
                src_ref=sum_a.at[dest], dst_ref=fin_a.at[step - 1], send_sem=sems.at[0, base + step],
                recv_sem=sems.at[1, base + step], device_id=(chip, core, dest // width, dest % width),
                device_id_type=mesh_id,
            ))
        for step in range(1, chips * layers):
            dest = (spot + step) % (chips * layers)
            third.append(pltpu.make_async_remote_copy(
                src_ref=sum_b.at[dest], dst_ref=fin_b.at[step - 1], send_sem=sems.at[0, base + ring + step],
                recv_sem=sems.at[1, base + ring + step], device_id=(dest // layers, core, dest % layers, y),
                device_id_type=mesh_id,
            ))
        for copy in third:
            copy.start()
        for copy in third:
            copy.wait()
        total = sum_a[me]
        for step in range(1, count):
            total = total + fin_a[step - 1]
        out_ref[:, :half] = total * scale
        total = sum_b[spot]
        for step in range(1, chips * layers):
            total = total + fin_b[step - 1]
        out_ref[:, half:] = total * scale

    return pl.pallas_call(
        kernel,
        out_shape=jax.ShapeDtypeStruct((piece, cols), jnp.float32),
        in_specs=[pl.BlockSpec(memory_space=pltpu.VMEM)] * 2,
        out_specs=pl.BlockSpec(memory_space=pltpu.VMEM),
        scratch_shapes=[
            pltpu.VMEM((chips, slab, cols), jnp.float32),
            pltpu.VMEM((chips, slab, cols), jnp.float32),
            pltpu.VMEM((chips, slab, half), jnp.float32),
            pltpu.VMEM((width, chips, layers, piece, half), jnp.float32),
            pltpu.VMEM((chips - 1, slab, half), jnp.float32),
            pltpu.VMEM((width - 1, chips, layers, piece, half), jnp.float32),
            pltpu.VMEM((count, piece, half), jnp.float32),
            pltpu.VMEM((chips * layers, piece, half), jnp.float32),
            pltpu.VMEM((count - 1, piece, half), jnp.float32),
            pltpu.VMEM((chips * layers - 1, piece, half), jnp.float32),
            pltpu.SemaphoreType.DMA((2, chips + width + count + chips * layers)),
        ],
        compiler_params=pltpu.CompilerParams(
            collective_id=1, has_side_effects=True, vmem_limit_bytes=48 * 1024 * 1024
        ),
    )(by_owner, grad_proj)


def on_device(layer_input, proj_weight, inputs, step_size, log_decay, skip_gain, grad_out):
    tokens = layer_input[0]
    length = tokens.shape[0]
    proj = jnp.dot(tokens, proj_weight, preferred_element_type=jnp.float32).astype(jnp.bfloat16)
    pieces = span_inputs(proj, inputs[0], grad_out[0], step_size[0], log_decay[0])
    own_state, own_grad, span_total = (pieces[9], pieces[10], pieces[6])
    empty_state = jnp.zeros((SHARD_CHANNELS, HEAD_DIM, STATE), jnp.float32)

    def advance(state_carry, piece):
        return (jnp.exp(piece[1])[:, None, None] * state_carry + piece[0], state_carry)

    last_state, local_starts = lax.scan(advance, empty_state, (own_state, span_total))
    last_grad, local_afters = lax.scan(advance, empty_state, (own_grad, span_total), reverse=True)
    state_entry, grad_entry = exchange(last_state, last_grad, jnp.sum(span_total, axis=0))
    running = jnp.cumsum(span_total, axis=0)
    before = running - span_total
    behind = jnp.sum(span_total, axis=0)[None] - running
    starts = local_starts + jnp.exp(before)[:, :, None, None] * state_entry[None]
    afters = local_afters + jnp.exp(behind)[:, :, None, None] * grad_entry[None]

    def finish(parts):
        return span_grads(*parts, skip_gain)

    grad_x, grad_proj = lax.map(finish, pieces[:9] + (starts, afters))
    grad_proj = grad_proj.reshape(length, 2 * STATE)
    scale_factor = 1.0 / (length * lax.axis_size("z") * lax.axis_size("y"))
    grad_weight = weight_grad_sum(tokens, grad_proj, scale_factor)
    return (grad_x, grad_weight)


def physical_mesh(mesh):
    grid = mesh.devices
    cores = len({d.core_on_chip for d in grid.flat})
    rows = len({d.coords[1] for d in grid.flat})
    dp, seq = grid.shape
    return Mesh(grid.reshape(dp // cores, cores, seq // rows, rows), ("x", "core", "z", "y"))


def solution(mesh):
    fine = physical_mesh(mesh)
    dp, seq = ("x", "core"), ("z", "y")
    return jax.shard_map(
        on_device,
        mesh=fine,
        in_specs=(
            P(dp, seq, None),
            P(),
            P(dp, seq, None),
            P(dp, None, seq),
            P(dp, None, seq),
            P(),
            P(dp, seq, None),
        ),
        out_specs=(P(dp, seq, None), P(dp + seq, None)),
        check_vma=False,
    )
```

```python
import jax
import jax.numpy as jnp
from jax import lax
from jax.experimental import pallas as pl
from jax.experimental.pallas import tpu as pltpu
from jax.sharding import Mesh, PartitionSpec as P

SHARD_CHANNELS = 32
HEAD_DIM = 64
STATE = 128
SPAN = 128


def span_inputs(proj, inputs, grad_out, step_size, log_decay):
    length = inputs.shape[0]
    spans = length // SPAN
    b_cols = proj[:, :STATE].reshape(spans, SPAN, STATE)
    c_cols = proj[:, STATE:].reshape(spans, SPAN, STATE)
    inputs_c = inputs.reshape(spans, SPAN, SHARD_CHANNELS, HEAD_DIM)
    grad_rows = grad_out.reshape(spans, SPAN, SHARD_CHANNELS, HEAD_DIM)
    step_rows = step_size.reshape(SHARD_CHANNELS, spans, SPAN).transpose(1, 0, 2)
    decay_sum = jnp.cumsum(
        log_decay.reshape(SHARD_CHANNELS, spans, SPAN).transpose(1, 0, 2), axis=2
    )
    span_total = decay_sum[:, :, -1]
    to_end = jnp.exp(span_total[:, :, None] - decay_sum)
    weighted = (
        inputs_c.astype(jnp.float32) * jnp.transpose(step_rows * to_end, (0, 2, 1))[..., None]
    ).astype(jnp.bfloat16)
    scaled = (
        grad_rows.astype(jnp.float32) * jnp.transpose(jnp.exp(decay_sum), (0, 2, 1))[..., None]
    ).astype(jnp.bfloat16)
    own_state = jnp.einsum("cqhp,cqn->chpn", weighted, b_cols, preferred_element_type=jnp.float32)
    own_grad = jnp.einsum("cqhp,cqn->chpn", scaled, c_cols, preferred_element_type=jnp.float32)
    return (
        b_cols,
        c_cols,
        inputs_c,
        grad_rows,
        step_rows,
        decay_sum,
        span_total,
        weighted,
        scaled,
        own_state,
        own_grad,
    )


def span_grads(
    b_cols,
    c_cols,
    inputs_c,
    grad_rows,
    step_rows,
    decay_sum,
    span_total,
    weighted,
    scaled,
    start,
    after,
    skip_gain,
):
    start_bf = start.astype(jnp.bfloat16)
    after_bf = after.astype(jnp.bfloat16)
    row_ids = lax.broadcasted_iota(jnp.int32, (SPAN, SPAN), 0)
    col_ids = lax.broadcasted_iota(jnp.int32, (SPAN, SPAN), 1)
    causal = row_ids >= col_ids
    log_gap = decay_sum[:, :, None] - decay_sum[:, None, :]
    decay_mat = jnp.exp(jnp.where(causal[None], log_gap, -jnp.inf))
    kernel = jnp.dot(c_cols, b_cols.T, preferred_element_type=jnp.float32)
    weights = (decay_mat * kernel[None]).astype(jnp.bfloat16)
    within = jnp.einsum("hsj,shp->jhp", weights, grad_rows, preferred_element_type=jnp.float32)
    carried = jnp.einsum("hpn,jn->jhp", after_bf, b_cols, preferred_element_type=jnp.float32)
    to_end = jnp.exp(span_total[:, None] - decay_sum)
    grad_x = step_rows.T[:, :, None] * (within + to_end.T[:, :, None] * carried) + skip_gain[
        None, :, None
    ] * grad_rows.astype(jnp.float32)
    intersection = jnp.einsum(
        "shp,jhp->hsj", grad_rows, inputs_c, preferred_element_type=jnp.float32
    )
    mixing = jnp.sum(decay_mat * step_rows[:, None, :] * intersection, axis=0).astype(jnp.bfloat16)
    grad_c = jnp.dot(mixing, b_cols, preferred_element_type=jnp.float32) + jnp.dot(
        scaled.reshape(SPAN, -1), start_bf.reshape(-1, STATE), preferred_element_type=jnp.float32
    )
    grad_b = jnp.dot(mixing.T, c_cols, preferred_element_type=jnp.float32) + jnp.dot(
        weighted.reshape(SPAN, -1), after_bf.reshape(-1, STATE), preferred_element_type=jnp.float32
    )
    grad_proj = jnp.concatenate([grad_b, grad_c], axis=1).astype(jnp.bfloat16)
    return (grad_x.astype(jnp.bfloat16).reshape(SPAN, -1), grad_proj)


def group_all_to_all(payload):
    width = lax.axis_size("y")
    count = lax.axis_size("z") * width

    def kernel(src_ref, out_ref, land, send_sems, recv_sems, local_sem):
        chip, core = lax.axis_index("x"), lax.axis_index("core")
        me = lax.axis_index("z") * width + lax.axis_index("y")
        local = pltpu.make_async_copy(src_ref.at[me], land.at[me], local_sem)
        local.start()
        outgoing = []
        for step in range(1, count):
            dest = (me + step) % count
            copy = pltpu.make_async_remote_copy(
                src_ref=src_ref.at[dest],
                dst_ref=land.at[me],
                send_sem=send_sems.at[step - 1],
                recv_sem=recv_sems.at[step - 1],
                device_id=(chip, core, dest // width, dest % width),
                device_id_type=pl.DeviceIdType.MESH,
            )
            copy.start()
            outgoing.append(copy)
        local.wait()
        for step in range(1, count):
            outgoing[step - 1].wait_send()
            origin = (me + count - step) % count
            pltpu.make_async_remote_copy(
                src_ref=src_ref.at[origin],
                dst_ref=land.at[origin],
                send_sem=send_sems.at[step - 1],
                recv_sem=recv_sems.at[step - 1],
                device_id=(chip, core, origin // width, origin % width),
                device_id_type=pl.DeviceIdType.MESH,
            ).wait_recv()
        out_ref[...] = land[...]

    return pl.pallas_call(
        kernel,
        out_shape=jax.ShapeDtypeStruct(payload.shape, payload.dtype),
        in_specs=[pl.BlockSpec(memory_space=pltpu.VMEM)],
        out_specs=pl.BlockSpec(memory_space=pltpu.VMEM),
        scratch_shapes=[
            pltpu.VMEM(payload.shape, payload.dtype),
            pltpu.SemaphoreType.DMA((count - 1,)),
            pltpu.SemaphoreType.DMA((count - 1,)),
            pltpu.SemaphoreType.DMA(()),
        ],
        compiler_params=pltpu.CompilerParams(has_side_effects=True, vmem_limit_bytes=48 * 1024 * 1024),
    )(payload)


def tiered_exchange(payload):
    width, layers = lax.axis_size("y"), lax.axis_size("z")
    heads, span, cols = payload.shape
    rows = (span - 8) // 2
    group = heads // width
    mesh_id = pl.DeviceIdType.MESH
    per_wave = 2 * (width - 1) + 2 * (layers - 1)

    def kernel(pay, out_ref, land1, agg, land2, res, land3, out4, land4, sems, local):
        chip, core = lax.axis_index("x"), lax.axis_index("core")
        z, y = lax.axis_index("z"), lax.axis_index("y")
        barrier = pltpu.get_barrier_semaphore()
        for step in range(1, width):
            pl.semaphore_signal(barrier, inc=1, device_id=(chip, core, z, (y + step) % width), device_id_type=mesh_id)
        for step in range(1, layers):
            pl.semaphore_signal(barrier, inc=1, device_id=(chip, core, (z + step) % layers, y), device_id_type=mesh_id)
        pl.semaphore_wait(barrier, width - 1 + layers - 1)

        def tier(src_of, dst, size, where, place, wave, base, slot):
            first = pltpu.make_async_copy(src_of(where), dst, local.at[wave, slot])
            copies = [first]
            for step in range(1, size):
                dest = (where + step) % size
                copies.append(pltpu.make_async_remote_copy(
                    src_ref=src_of(dest), dst_ref=dst, send_sem=sems.at[0, wave, base + step - 1],
                    recv_sem=sems.at[1, wave, base + step - 1], device_id=place(dest), device_id_type=mesh_id,
                ))
            for copy in copies:
                copy.start()
            return copies

        def finish(copies):
            for copy in copies:
                copy.wait()

        row_place = lambda m: (chip, core, z, m)
        col_place = lambda m: (chip, core, m, y)
        lo = (0, rows)
        n = (rows + 8, rows)
        def row_tier(w):
            return tier(lambda m: pay.at[pl.ds(m * group, group), w], land1.at[w, y], width, y, row_place, w, 0, 0)

        t1 = [row_tier(0)]
        for w in range(2):
            finish(t1[w])
            if w == 0:
                t1.append(row_tier(1))
            for k in range(group):
                carry = jnp.zeros((rows, cols), jnp.float32)
                total = jnp.zeros((1, cols), jnp.float32)
                order = range(width) if w == 0 else reversed(range(width))
                for m in order:
                    mark = land1[0, m, k, rows : rows + 1]
                    carry = jnp.exp(mark) * carry + land1[w, m, k, :rows]
                    total = total + mark
                agg[w, k, :rows] = carry
                agg[w, k, rows:] = jnp.broadcast_to(total * (1 - w), (8, cols))
            t2 = tier(lambda m, w=w: agg.at[w, m], land2.at[w, z], layers, z, col_place, w, width - 1, 1)
            if w == 0:
                t2_first = t2
        finish(t2_first)
        finish(t2)
        for w in range(2):
            carry = jnp.zeros((rows, cols), jnp.float32)
            order = range(layers) if w == 0 else reversed(range(layers))
            for r in order:
                res[w, r] = carry
                carry = jnp.exp(land2[0, r, rows : rows + 1]) * carry + land2[w, r, :rows]
            if w == 0:
                t3 = [tier(lambda m: res.at[0, m], land3.at[0, z], layers, z, col_place, 0, width + layers - 2, 2)]
        t4 = []
        for w in range(2):
            finish(t3[w])
            if w == 0:
                t3.append(tier(lambda m: res.at[1, m], land3.at[1, z], layers, z, col_place, 1, width + layers - 2, 2))
            for k in range(group):
                carry = land3[w, k]
                order = range(width) if w == 0 else reversed(range(width))
                for m in order:
                    out4[w, m, k] = carry
                    carry = jnp.exp(land1[0, m, k, rows : rows + 1]) * carry + land1[w, m, k, :rows]
            t4.append(tier(lambda m, w=w: out4.at[w, m], land4.at[w, y], width, y, row_place, w, width + 2 * layers - 3, 3))
        for copies in t4:
            finish(copies)
        out_ref[:, :rows] = land4[0].reshape(heads, rows, cols)
        out_ref[:, rows:] = land4[1].reshape(heads, rows, cols)

    fwd = jnp.concatenate([payload[:, :rows], payload[:, 2 * rows :]], axis=1)
    bwd = jnp.pad(payload[:, rows : 2 * rows], ((0, 0), (0, 8), (0, 0)))
    body = jnp.stack([fwd, bwd], axis=1)
    return pl.pallas_call(
        kernel,
        out_shape=jax.ShapeDtypeStruct((heads, 2 * rows, cols), jnp.float32),
        in_specs=[pl.BlockSpec(memory_space=pltpu.VMEM)],
        out_specs=pl.BlockSpec(memory_space=pltpu.VMEM),
        scratch_shapes=[
            pltpu.VMEM((2, width, group, rows + 8, cols), jnp.float32),
            pltpu.VMEM((2, group, rows + 8, cols), jnp.float32),
            pltpu.VMEM((2, layers, rows + 8, cols), jnp.float32),
            pltpu.VMEM((2, layers, rows, cols), jnp.float32),
            pltpu.VMEM((2, layers, rows, cols), jnp.float32),
            pltpu.VMEM((2, width, group, rows, cols), jnp.float32),
            pltpu.VMEM((2, width, group, rows, cols), jnp.float32),
            pltpu.SemaphoreType.DMA((2, 2, per_wave)),
            pltpu.SemaphoreType.DMA((2, 4)),
        ],
        compiler_params=pltpu.CompilerParams(
            collective_id=0, has_side_effects=True, vmem_limit_bytes=48 * 1024 * 1024
        ),
    )(body)


def exchange(own_state, own_grad, device_total):
    heads, rows, cols = own_state.shape
    marks = jnp.broadcast_to(device_total[:, None, None], (heads, 8, cols))
    payload = jnp.concatenate([own_state, own_grad, marks], axis=1)
    back = tiered_exchange(payload)
    return back[:, :rows], back[:, rows:]


def weight_grad_sum(tokens, grad_proj, scale):
    chips, cores = lax.axis_size("x"), lax.axis_size("core")
    layers, width = lax.axis_size("z"), lax.axis_size("y")
    count = layers * width
    length, depth = tokens.shape
    cols = grad_proj.shape[1]
    half = cols // 2
    slab = depth // (chips * cores)
    piece = slab // count
    by_owner = tokens.T.reshape(chips, cores, slab, length)
    mesh_id = pl.DeviceIdType.MESH
    ring = count - 1

    def kernel(tok_ref, gp_ref, out_ref, send1, land1, acc_a, acc_b, land_a, land_b,
               sum_a, sum_b, fin_a, fin_b, sems):
        chip, core = lax.axis_index("x"), lax.axis_index("core")
        z, y = lax.axis_index("z"), lax.axis_index("y")
        me = z * width + y
        spot = chip * layers + z
        other = 1 - core
        barrier = pltpu.get_barrier_semaphore()
        pl.semaphore_signal(barrier, inc=1, device_id=(chip, other, z, y), device_id_type=mesh_id)
        for step in range(1, count):
            dest = (me + step) % count
            pl.semaphore_signal(barrier, inc=1, device_id=(chip, core, dest // width, dest % width), device_id_type=mesh_id)
        for step in range(1, chips * layers):
            dest = (spot + step) % (chips * layers)
            pl.semaphore_signal(barrier, inc=1, device_id=(dest // layers, core, dest % layers, y), device_id_type=mesh_id)
        pl.semaphore_wait(barrier, count + chips * layers - 1)
        gp = gp_ref[...]
        for c in range(chips):
            send1[c] = jnp.dot(tok_ref[c, other], gp, preferred_element_type=jnp.float32)
        first = pltpu.make_async_remote_copy(
            src_ref=send1, dst_ref=land1, send_sem=sems.at[0, 0], recv_sem=sems.at[1, 0],
            device_id=(chip, other, z, y), device_id_type=mesh_id,
        )
        first.start()
        own = [jnp.dot(tok_ref[c, core], gp, preferred_element_type=jnp.float32) for c in range(chips)]
        first.wait()
        for c in range(chips):
            summed = own[c] + land1[c]
            acc_a[c] = summed[:, :half]
            blocks = summed[:, half:].reshape(layers, width, piece, half)
            for w in range(width):
                acc_b[w, c] = blocks[:, w]
        second = []
        for step in range(1, chips):
            dest = (chip + step) % chips
            second.append(pltpu.make_async_remote_copy(
                src_ref=acc_a.at[dest], dst_ref=land_a.at[step - 1], send_sem=sems.at[0, step],
                recv_sem=sems.at[1, step], device_id=(dest, core, z, y), device_id_type=mesh_id,
            ))
        for step in range(1, width):
            dest = (y + step) % width
            second.append(pltpu.make_async_remote_copy(
                src_ref=acc_b.at[dest], dst_ref=land_b.at[step - 1], send_sem=sems.at[0, chips + step],
                recv_sem=sems.at[1, chips + step], device_id=(chip, core, z, dest), device_id_type=mesh_id,
            ))
        for copy in second:
            copy.start()
        for copy in second:
            copy.wait()
        total = acc_a[chip]
        for step in range(1, chips):
            total = total + land_a[step - 1]
        sum_a[...] = total.reshape(count, piece, half)
        total = acc_b[y]
        for step in range(1, width):
            total = total + land_b[step - 1]
        sum_b[...] = total.reshape(chips * layers, piece, half)
        base = chips + width
        third = []
        for step in range(1, count):
            dest = (me + step) % count
            third.append(pltpu.make_async_remote_copy(
                src_ref=sum_a.at[dest], dst_ref=fin_a.at[step - 1], send_sem=sems.at[0, base + step],
                recv_sem=sems.at[1, base + step], device_id=(chip, core, dest // width, dest % width),
                device_id_type=mesh_id,
            ))
        for step in range(1, chips * layers):
            dest = (spot + step) % (chips * layers)
            third.append(pltpu.make_async_remote_copy(
                src_ref=sum_b.at[dest], dst_ref=fin_b.at[step - 1], send_sem=sems.at[0, base + ring + step],
                recv_sem=sems.at[1, base + ring + step], device_id=(dest // layers, core, dest % layers, y),
                device_id_type=mesh_id,
            ))
        for copy in third:
            copy.start()
        for copy in third:
            copy.wait()
        total = sum_a[me]
        for step in range(1, count):
            total = total + fin_a[step - 1]
        out_ref[:, :half] = total * scale
        total = sum_b[spot]
        for step in range(1, chips * layers):
            total = total + fin_b[step - 1]
        out_ref[:, half:] = total * scale

    return pl.pallas_call(
        kernel,
        out_shape=jax.ShapeDtypeStruct((piece, cols), jnp.float32),
        in_specs=[pl.BlockSpec(memory_space=pltpu.VMEM)] * 2,
        out_specs=pl.BlockSpec(memory_space=pltpu.VMEM),
        scratch_shapes=[
            pltpu.VMEM((chips, slab, cols), jnp.float32),
            pltpu.VMEM((chips, slab, cols), jnp.float32),
            pltpu.VMEM((chips, slab, half), jnp.float32),
            pltpu.VMEM((width, chips, layers, piece, half), jnp.float32),
            pltpu.VMEM((chips - 1, slab, half), jnp.float32),
            pltpu.VMEM((width - 1, chips, layers, piece, half), jnp.float32),
            pltpu.VMEM((count, piece, half), jnp.float32),
            pltpu.VMEM((chips * layers, piece, half), jnp.float32),
            pltpu.VMEM((count - 1, piece, half), jnp.float32),
            pltpu.VMEM((chips * layers - 1, piece, half), jnp.float32),
            pltpu.SemaphoreType.DMA((2, chips + width + count + chips * layers)),
        ],
        compiler_params=pltpu.CompilerParams(
            collective_id=1, has_side_effects=True, vmem_limit_bytes=48 * 1024 * 1024
        ),
    )(by_owner, grad_proj)


def on_device(layer_input, proj_weight, inputs, step_size, log_decay, skip_gain, grad_out):
    tokens = layer_input[0]
    length = tokens.shape[0]
    proj = jnp.dot(tokens, proj_weight, preferred_element_type=jnp.float32).astype(jnp.bfloat16)
    pieces = span_inputs(proj, inputs[0], grad_out[0], step_size[0], log_decay[0])
    own_state, own_grad, span_total = (pieces[9], pieces[10], pieces[6])
    empty_state = jnp.zeros((SHARD_CHANNELS, HEAD_DIM, STATE), jnp.float32)

    def advance(state_carry, piece):
        return (jnp.exp(piece[1])[:, None, None] * state_carry + piece[0], state_carry)

    last_state, local_starts = lax.scan(advance, empty_state, (own_state, span_total))
    last_grad, local_afters = lax.scan(advance, empty_state, (own_grad, span_total), reverse=True)
    state_entry, grad_entry = exchange(last_state, last_grad, jnp.sum(span_total, axis=0))
    running = jnp.cumsum(span_total, axis=0)
    before = running - span_total
    behind = jnp.sum(span_total, axis=0)[None] - running
    starts = local_starts + jnp.exp(before)[:, :, None, None] * state_entry[None]
    afters = local_afters + jnp.exp(behind)[:, :, None, None] * grad_entry[None]

    def finish(parts):
        return span_grads(*parts, skip_gain)

    grad_x, grad_proj = lax.map(finish, pieces[:9] + (starts, afters))
    grad_proj = grad_proj.reshape(length, 2 * STATE)
    scale_factor = 1.0 / (length * lax.axis_size("z") * lax.axis_size("y"))
    grad_weight = weight_grad_sum(tokens, grad_proj, scale_factor)
    return (grad_x, grad_weight)


def physical_mesh(mesh):
    grid = mesh.devices
    cores = len({d.core_on_chip for d in grid.flat})
    rows = len({d.coords[1] for d in grid.flat})
    dp, seq = grid.shape
    return Mesh(grid.reshape(dp // cores, cores, seq // rows, rows), ("x", "core", "z", "y"))


def solution(mesh):
    fine = physical_mesh(mesh)
    dp, seq = ("x", "core"), ("z", "y")
    return jax.shard_map(
        on_device,
        mesh=fine,
        in_specs=(
            P(dp, seq, None),
            P(),
            P(dp, seq, None),
            P(dp, None, seq),
            P(dp, None, seq),
            P(),
            P(dp, seq, None),
        ),
        out_specs=(P(dp, seq, None), P(dp + seq, None)),
        check_vma=False,
    )
```

```python
import jax
import jax.numpy as jnp
from jax import lax
from jax.experimental import pallas as pl
from jax.experimental.pallas import tpu as pltpu
from jax.sharding import Mesh, PartitionSpec as P

SHARD_CHANNELS = 32
HEAD_DIM = 64
STATE = 128
SPAN = 128


def span_inputs(proj, inputs, grad_out, step_size, log_decay):
    length = inputs.shape[0]
    spans = length // SPAN
    b_cols = proj[:, :STATE].reshape(spans, SPAN, STATE)
    c_cols = proj[:, STATE:].reshape(spans, SPAN, STATE)
    inputs_c = inputs.reshape(spans, SPAN, SHARD_CHANNELS, HEAD_DIM)
    grad_rows = grad_out.reshape(spans, SPAN, SHARD_CHANNELS, HEAD_DIM)
    step_rows = step_size.reshape(SHARD_CHANNELS, spans, SPAN).transpose(1, 0, 2)
    decay_sum = jnp.cumsum(
        log_decay.reshape(SHARD_CHANNELS, spans, SPAN).transpose(1, 0, 2), axis=2
    )
    span_total = decay_sum[:, :, -1]
    to_end = jnp.exp(span_total[:, :, None] - decay_sum)
    weighted = (
        inputs_c.astype(jnp.float32) * jnp.transpose(step_rows * to_end, (0, 2, 1))[..., None]
    ).astype(jnp.bfloat16)
    scaled = (
        grad_rows.astype(jnp.float32) * jnp.transpose(jnp.exp(decay_sum), (0, 2, 1))[..., None]
    ).astype(jnp.bfloat16)
    own_state = jnp.einsum("cqhp,cqn->chpn", weighted, b_cols, preferred_element_type=jnp.float32)
    own_grad = jnp.einsum("cqhp,cqn->chpn", scaled, c_cols, preferred_element_type=jnp.float32)
    return (
        b_cols,
        c_cols,
        inputs_c,
        grad_rows,
        step_rows,
        decay_sum,
        span_total,
        weighted,
        scaled,
        own_state,
        own_grad,
    )


def span_grads(
    b_cols,
    c_cols,
    inputs_c,
    grad_rows,
    step_rows,
    decay_sum,
    span_total,
    weighted,
    scaled,
    start,
    after,
    skip_gain,
):
    start_bf = start.astype(jnp.bfloat16)
    after_bf = after.astype(jnp.bfloat16)
    row_ids = lax.broadcasted_iota(jnp.int32, (SPAN, SPAN), 0)
    col_ids = lax.broadcasted_iota(jnp.int32, (SPAN, SPAN), 1)
    causal = row_ids >= col_ids
    log_gap = decay_sum[:, :, None] - decay_sum[:, None, :]
    decay_mat = jnp.exp(jnp.where(causal[None], log_gap, -jnp.inf))
    kernel = jnp.dot(c_cols, b_cols.T, preferred_element_type=jnp.float32)
    weights = (decay_mat * kernel[None]).astype(jnp.bfloat16)
    within = jnp.einsum("hsj,shp->jhp", weights, grad_rows, preferred_element_type=jnp.float32)
    carried = jnp.einsum("hpn,jn->jhp", after_bf, b_cols, preferred_element_type=jnp.float32)
    to_end = jnp.exp(span_total[:, None] - decay_sum)
    grad_x = step_rows.T[:, :, None] * (within + to_end.T[:, :, None] * carried) + skip_gain[
        None, :, None
    ] * grad_rows.astype(jnp.float32)
    intersection = jnp.einsum(
        "shp,jhp->hsj", grad_rows, inputs_c, preferred_element_type=jnp.float32
    )
    mixing = jnp.sum(decay_mat * step_rows[:, None, :] * intersection, axis=0).astype(jnp.bfloat16)
    grad_c = jnp.dot(mixing, b_cols, preferred_element_type=jnp.float32) + jnp.dot(
        scaled.reshape(SPAN, -1), start_bf.reshape(-1, STATE), preferred_element_type=jnp.float32
    )
    grad_b = jnp.dot(mixing.T, c_cols, preferred_element_type=jnp.float32) + jnp.dot(
        weighted.reshape(SPAN, -1), after_bf.reshape(-1, STATE), preferred_element_type=jnp.float32
    )
    grad_proj = jnp.concatenate([grad_b, grad_c], axis=1).astype(jnp.bfloat16)
    return (grad_x.astype(jnp.bfloat16).reshape(SPAN, -1), grad_proj)


def group_all_to_all(payload):
    width = lax.axis_size("y")
    count = lax.axis_size("z") * width

    def kernel(src_ref, out_ref, land, send_sems, recv_sems, local_sem):
        chip, core = lax.axis_index("x"), lax.axis_index("core")
        me = lax.axis_index("z") * width + lax.axis_index("y")
        local = pltpu.make_async_copy(src_ref.at[me], land.at[me], local_sem)
        local.start()
        outgoing = []
        for step in range(1, count):
            dest = (me + step) % count
            copy = pltpu.make_async_remote_copy(
                src_ref=src_ref.at[dest],
                dst_ref=land.at[me],
                send_sem=send_sems.at[step - 1],
                recv_sem=recv_sems.at[step - 1],
                device_id=(chip, core, dest // width, dest % width),
                device_id_type=pl.DeviceIdType.MESH,
            )
            copy.start()
            outgoing.append(copy)
        local.wait()
        for step in range(1, count):
            outgoing[step - 1].wait_send()
            origin = (me + count - step) % count
            pltpu.make_async_remote_copy(
                src_ref=src_ref.at[origin],
                dst_ref=land.at[origin],
                send_sem=send_sems.at[step - 1],
                recv_sem=recv_sems.at[step - 1],
                device_id=(chip, core, origin // width, origin % width),
                device_id_type=pl.DeviceIdType.MESH,
            ).wait_recv()
        out_ref[...] = land[...]

    return pl.pallas_call(
        kernel,
        out_shape=jax.ShapeDtypeStruct(payload.shape, payload.dtype),
        in_specs=[pl.BlockSpec(memory_space=pltpu.VMEM)],
        out_specs=pl.BlockSpec(memory_space=pltpu.VMEM),
        scratch_shapes=[
            pltpu.VMEM(payload.shape, payload.dtype),
            pltpu.SemaphoreType.DMA((count - 1,)),
            pltpu.SemaphoreType.DMA((count - 1,)),
            pltpu.SemaphoreType.DMA(()),
        ],
        compiler_params=pltpu.CompilerParams(has_side_effects=True, vmem_limit_bytes=48 * 1024 * 1024),
    )(payload)


def tiered_exchange(payload):
    width, layers = lax.axis_size("y"), lax.axis_size("z")
    heads, span, cols = payload.shape
    rows = (span - 8) // 2
    group = heads // width
    part = rows // 2
    waves = 4
    mesh_id = pl.DeviceIdType.MESH
    per_wave = 2 * (width - 1) + 2 * (layers - 1)

    def kernel(pay, out_ref, land1, agg, land2, res, land3, out4, land4, sems, local):
        chip, core = lax.axis_index("x"), lax.axis_index("core")
        z, y = lax.axis_index("z"), lax.axis_index("y")
        barrier = pltpu.get_barrier_semaphore()
        for step in range(1, width):
            pl.semaphore_signal(barrier, inc=1, device_id=(chip, core, z, (y + step) % width), device_id_type=mesh_id)
        for step in range(1, layers):
            pl.semaphore_signal(barrier, inc=1, device_id=(chip, core, (z + step) % layers, y), device_id_type=mesh_id)
        pl.semaphore_wait(barrier, width - 1 + layers - 1)

        def tier(src_of, dst, size, where, place, wave, base, slot):
            first = pltpu.make_async_copy(src_of(where), dst, local.at[wave, slot])
            copies = [first]
            for step in range(1, size):
                dest = (where + step) % size
                copies.append(pltpu.make_async_remote_copy(
                    src_ref=src_of(dest), dst_ref=dst, send_sem=sems.at[0, wave, base + step - 1],
                    recv_sem=sems.at[1, wave, base + step - 1], device_id=place(dest), device_id_type=mesh_id,
                ))
            for copy in copies:
                copy.start()
            return copies

        def finish(copies):
            for copy in copies:
                copy.wait()

        row_place = lambda m: (chip, core, z, m)
        col_place = lambda m: (chip, core, m, y)
        t1 = [
            tier(lambda m, w=w: pay.at[pl.ds(m * group, group), w], land1.at[w, y], width, y, row_place, w, 0, 0)
            for w in range(waves)
        ]
        t2 = []
        for w in range(waves):
            finish(t1[w])
            for k in range(group):
                carry = jnp.zeros((part, cols), jnp.float32)
                total = jnp.zeros((1, cols), jnp.float32)
                order = range(width) if w < 2 else reversed(range(width))
                for m in order:
                    mark = land1[0, m, k, part : part + 1]
                    carry = jnp.exp(mark) * carry + land1[w, m, k, :part]
                    total = total + mark
                agg[w, k, :part] = carry
                agg[w, k, part:] = jnp.broadcast_to(total * (1 if w == 0 else 0), (8, cols))
            t2.append(tier(lambda m, w=w: agg.at[w, m], land2.at[w, z], layers, z, col_place, w, width - 1, 1))
        t3 = []
        for w in range(waves):
            finish(t2[w])
            carry = jnp.zeros((part, cols), jnp.float32)
            order = range(layers) if w < 2 else reversed(range(layers))
            for r in order:
                res[w, r] = carry
                carry = jnp.exp(land2[0, r, part : part + 1]) * carry + land2[w, r, :part]
            t3.append(tier(lambda m, w=w: res.at[w, m], land3.at[w, z], layers, z, col_place, w, width + layers - 2, 2))
        t4 = []
        for w in range(waves):
            finish(t3[w])
            for k in range(group):
                carry = land3[w, k]
                order = range(width) if w < 2 else reversed(range(width))
                for m in order:
                    out4[w, m, k] = carry
                    carry = jnp.exp(land1[0, m, k, part : part + 1]) * carry + land1[w, m, k, :part]
            t4.append(tier(lambda m, w=w: out4.at[w, m], land4.at[w, y], width, y, row_place, w, width + 2 * layers - 3, 3))
        for w in range(waves):
            finish(t4[w])
            out_ref[:, w * part : (w + 1) * part] = land4[w].reshape(heads, part, cols)

    marks = payload[:, 2 * rows :]
    blank = jnp.zeros_like(marks)
    body = jnp.stack(
        [
            jnp.concatenate([payload[:, w * part : (w + 1) * part], marks if w == 0 else blank], axis=1)
            for w in range(waves)
        ],
        axis=1,
    )
    return pl.pallas_call(
        kernel,
        out_shape=jax.ShapeDtypeStruct((heads, 2 * rows, cols), jnp.float32),
        in_specs=[pl.BlockSpec(memory_space=pltpu.VMEM)],
        out_specs=pl.BlockSpec(memory_space=pltpu.VMEM),
        scratch_shapes=[
            pltpu.VMEM((waves, width, group, part + 8, cols), jnp.float32),
            pltpu.VMEM((waves, group, part + 8, cols), jnp.float32),
            pltpu.VMEM((waves, layers, part + 8, cols), jnp.float32),
            pltpu.VMEM((waves, layers, part, cols), jnp.float32),
            pltpu.VMEM((waves, layers, part, cols), jnp.float32),
            pltpu.VMEM((waves, width, group, part, cols), jnp.float32),
            pltpu.VMEM((waves, width, group, part, cols), jnp.float32),
            pltpu.SemaphoreType.DMA((2, waves, per_wave)),
            pltpu.SemaphoreType.DMA((waves, 4)),
        ],
        compiler_params=pltpu.CompilerParams(
            collective_id=0, has_side_effects=True, vmem_limit_bytes=48 * 1024 * 1024
        ),
    )(body)


def exchange(own_state, own_grad, device_total):
    heads, rows, cols = own_state.shape
    marks = jnp.broadcast_to(device_total[:, None, None], (heads, 8, cols))
    payload = jnp.concatenate([own_state, own_grad, marks], axis=1)
    back = tiered_exchange(payload)
    return back[:, :rows], back[:, rows:]


def weight_grad_sum(tokens, grad_proj, scale):
    chips, cores = lax.axis_size("x"), lax.axis_size("core")
    layers, width = lax.axis_size("z"), lax.axis_size("y")
    count = layers * width
    length, depth = tokens.shape
    cols = grad_proj.shape[1]
    half = cols // 2
    slab = depth // (chips * cores)
    piece = slab // count
    by_owner = tokens.T.reshape(chips, cores, slab, length)
    mesh_id = pl.DeviceIdType.MESH
    ring = count - 1

    def kernel(tok_ref, gp_ref, out_ref, send1, land1, acc_a, acc_b, land_a, land_b,
               sum_a, sum_b, fin_a, fin_b, sems):
        chip, core = lax.axis_index("x"), lax.axis_index("core")
        z, y = lax.axis_index("z"), lax.axis_index("y")
        me = z * width + y
        spot = chip * layers + z
        other = 1 - core
        barrier = pltpu.get_barrier_semaphore()
        pl.semaphore_signal(barrier, inc=1, device_id=(chip, other, z, y), device_id_type=mesh_id)
        for step in range(1, count):
            dest = (me + step) % count
            pl.semaphore_signal(barrier, inc=1, device_id=(chip, core, dest // width, dest % width), device_id_type=mesh_id)
        for step in range(1, chips * layers):
            dest = (spot + step) % (chips * layers)
            pl.semaphore_signal(barrier, inc=1, device_id=(dest // layers, core, dest % layers, y), device_id_type=mesh_id)
        pl.semaphore_wait(barrier, count + chips * layers - 1)
        gp = gp_ref[...]
        for c in range(chips):
            send1[c] = jnp.dot(tok_ref[c, other], gp, preferred_element_type=jnp.float32)
        first = pltpu.make_async_remote_copy(
            src_ref=send1, dst_ref=land1, send_sem=sems.at[0, 0], recv_sem=sems.at[1, 0],
            device_id=(chip, other, z, y), device_id_type=mesh_id,
        )
        first.start()
        own = [jnp.dot(tok_ref[c, core], gp, preferred_element_type=jnp.float32) for c in range(chips)]
        first.wait()
        for c in range(chips):
            summed = own[c] + land1[c]
            acc_a[c] = summed[:, :half]
            blocks = summed[:, half:].reshape(layers, width, piece, half)
            for w in range(width):
                acc_b[w, c] = blocks[:, w]
        second = []
        for step in range(1, chips):
            dest = (chip + step) % chips
            second.append(pltpu.make_async_remote_copy(
                src_ref=acc_a.at[dest], dst_ref=land_a.at[step - 1], send_sem=sems.at[0, step],
                recv_sem=sems.at[1, step], device_id=(dest, core, z, y), device_id_type=mesh_id,
            ))
        for step in range(1, width):
            dest = (y + step) % width
            second.append(pltpu.make_async_remote_copy(
                src_ref=acc_b.at[dest], dst_ref=land_b.at[step - 1], send_sem=sems.at[0, chips + step],
                recv_sem=sems.at[1, chips + step], device_id=(chip, core, z, dest), device_id_type=mesh_id,
            ))
        for copy in second:
            copy.start()
        for copy in second:
            copy.wait()
        total = acc_a[chip]
        for step in range(1, chips):
            total = total + land_a[step - 1]
        sum_a[...] = total.reshape(count, piece, half)
        total = acc_b[y]
        for step in range(1, width):
            total = total + land_b[step - 1]
        sum_b[...] = total.reshape(chips * layers, piece, half)
        base = chips + width
        third = []
        for step in range(1, count):
            dest = (me + step) % count
            third.append(pltpu.make_async_remote_copy(
                src_ref=sum_a.at[dest], dst_ref=fin_a.at[step - 1], send_sem=sems.at[0, base + step],
                recv_sem=sems.at[1, base + step], device_id=(chip, core, dest // width, dest % width),
                device_id_type=mesh_id,
            ))
        for step in range(1, chips * layers):
            dest = (spot + step) % (chips * layers)
            third.append(pltpu.make_async_remote_copy(
                src_ref=sum_b.at[dest], dst_ref=fin_b.at[step - 1], send_sem=sems.at[0, base + ring + step],
                recv_sem=sems.at[1, base + ring + step], device_id=(dest // layers, core, dest % layers, y),
                device_id_type=mesh_id,
            ))
        for copy in third:
            copy.start()
        for copy in third:
            copy.wait()
        total = sum_a[me]
        for step in range(1, count):
            total = total + fin_a[step - 1]
        out_ref[:, :half] = total * scale
        total = sum_b[spot]
        for step in range(1, chips * layers):
            total = total + fin_b[step - 1]
        out_ref[:, half:] = total * scale

    return pl.pallas_call(
        kernel,
        out_shape=jax.ShapeDtypeStruct((piece, cols), jnp.float32),
        in_specs=[pl.BlockSpec(memory_space=pltpu.VMEM)] * 2,
        out_specs=pl.BlockSpec(memory_space=pltpu.VMEM),
        scratch_shapes=[
            pltpu.VMEM((chips, slab, cols), jnp.float32),
            pltpu.VMEM((chips, slab, cols), jnp.float32),
            pltpu.VMEM((chips, slab, half), jnp.float32),
            pltpu.VMEM((width, chips, layers, piece, half), jnp.float32),
            pltpu.VMEM((chips - 1, slab, half), jnp.float32),
            pltpu.VMEM((width - 1, chips, layers, piece, half), jnp.float32),
            pltpu.VMEM((count, piece, half), jnp.float32),
            pltpu.VMEM((chips * layers, piece, half), jnp.float32),
            pltpu.VMEM((count - 1, piece, half), jnp.float32),
            pltpu.VMEM((chips * layers - 1, piece, half), jnp.float32),
            pltpu.SemaphoreType.DMA((2, chips + width + count + chips * layers)),
        ],
        compiler_params=pltpu.CompilerParams(
            collective_id=1, has_side_effects=True, vmem_limit_bytes=48 * 1024 * 1024
        ),
    )(by_owner, grad_proj)


def on_device(layer_input, proj_weight, inputs, step_size, log_decay, skip_gain, grad_out):
    tokens = layer_input[0]
    length = tokens.shape[0]
    proj = jnp.dot(tokens, proj_weight, preferred_element_type=jnp.float32).astype(jnp.bfloat16)
    pieces = span_inputs(proj, inputs[0], grad_out[0], step_size[0], log_decay[0])
    own_state, own_grad, span_total = (pieces[9], pieces[10], pieces[6])
    empty_state = jnp.zeros((SHARD_CHANNELS, HEAD_DIM, STATE), jnp.float32)

    def advance(state_carry, piece):
        return (jnp.exp(piece[1])[:, None, None] * state_carry + piece[0], state_carry)

    last_state, local_starts = lax.scan(advance, empty_state, (own_state, span_total))
    last_grad, local_afters = lax.scan(advance, empty_state, (own_grad, span_total), reverse=True)
    state_entry, grad_entry = exchange(last_state, last_grad, jnp.sum(span_total, axis=0))
    running = jnp.cumsum(span_total, axis=0)
    before = running - span_total
    behind = jnp.sum(span_total, axis=0)[None] - running
    starts = local_starts + jnp.exp(before)[:, :, None, None] * state_entry[None]
    afters = local_afters + jnp.exp(behind)[:, :, None, None] * grad_entry[None]

    def finish(parts):
        return span_grads(*parts, skip_gain)

    grad_x, grad_proj = lax.map(finish, pieces[:9] + (starts, afters))
    grad_proj = grad_proj.reshape(length, 2 * STATE)
    scale_factor = 1.0 / (length * lax.axis_size("z") * lax.axis_size("y"))
    grad_weight = weight_grad_sum(tokens, grad_proj, scale_factor)
    return (grad_x, grad_weight)


def physical_mesh(mesh):
    grid = mesh.devices
    cores = len({d.core_on_chip for d in grid.flat})
    rows = len({d.coords[1] for d in grid.flat})
    dp, seq = grid.shape
    return Mesh(grid.reshape(dp // cores, cores, seq // rows, rows), ("x", "core", "z", "y"))


def solution(mesh):
    fine = physical_mesh(mesh)
    dp, seq = ("x", "core"), ("z", "y")
    return jax.shard_map(
        on_device,
        mesh=fine,
        in_specs=(
            P(dp, seq, None),
            P(),
            P(dp, seq, None),
            P(dp, None, seq),
            P(dp, None, seq),
            P(),
            P(dp, seq, None),
        ),
        out_specs=(P(dp, seq, None), P(dp + seq, None)),
        check_vma=False,
    )
```

```python
import jax
import jax.numpy as jnp
from jax import lax
from jax.experimental import pallas as pl
from jax.experimental.pallas import tpu as pltpu
from jax.sharding import Mesh, PartitionSpec as P

SHARD_CHANNELS = 32
HEAD_DIM = 64
STATE = 128
SPAN = 128


def span_inputs(proj, inputs, grad_out, step_size, log_decay):
    length = inputs.shape[0]
    spans = length // SPAN
    b_cols = proj[:, :STATE].reshape(spans, SPAN, STATE)
    c_cols = proj[:, STATE:].reshape(spans, SPAN, STATE)
    inputs_c = inputs.reshape(spans, SPAN, SHARD_CHANNELS, HEAD_DIM)
    grad_rows = grad_out.reshape(spans, SPAN, SHARD_CHANNELS, HEAD_DIM)
    step_rows = step_size.reshape(SHARD_CHANNELS, spans, SPAN).transpose(1, 0, 2)
    decay_sum = jnp.cumsum(
        log_decay.reshape(SHARD_CHANNELS, spans, SPAN).transpose(1, 0, 2), axis=2
    )
    span_total = decay_sum[:, :, -1]
    to_end = jnp.exp(span_total[:, :, None] - decay_sum)
    weighted = (
        inputs_c.astype(jnp.float32) * jnp.transpose(step_rows * to_end, (0, 2, 1))[..., None]
    ).astype(jnp.bfloat16)
    scaled = (
        grad_rows.astype(jnp.float32) * jnp.transpose(jnp.exp(decay_sum), (0, 2, 1))[..., None]
    ).astype(jnp.bfloat16)
    own_state = jnp.einsum("cqhp,cqn->chpn", weighted, b_cols, preferred_element_type=jnp.float32)
    own_grad = jnp.einsum("cqhp,cqn->chpn", scaled, c_cols, preferred_element_type=jnp.float32)
    return (
        b_cols,
        c_cols,
        inputs_c,
        grad_rows,
        step_rows,
        decay_sum,
        span_total,
        weighted,
        scaled,
        own_state,
        own_grad,
    )


def span_grads(
    b_cols,
    c_cols,
    inputs_c,
    grad_rows,
    step_rows,
    decay_sum,
    span_total,
    weighted,
    scaled,
    start,
    after,
    skip_gain,
):
    start_bf = start.astype(jnp.bfloat16)
    after_bf = after.astype(jnp.bfloat16)
    row_ids = lax.broadcasted_iota(jnp.int32, (SPAN, SPAN), 0)
    col_ids = lax.broadcasted_iota(jnp.int32, (SPAN, SPAN), 1)
    causal = row_ids >= col_ids
    log_gap = decay_sum[:, :, None] - decay_sum[:, None, :]
    decay_mat = jnp.exp(jnp.where(causal[None], log_gap, -jnp.inf))
    kernel = jnp.dot(c_cols, b_cols.T, preferred_element_type=jnp.float32)
    weights = (decay_mat * kernel[None]).astype(jnp.bfloat16)
    within = jnp.einsum("hsj,shp->jhp", weights, grad_rows, preferred_element_type=jnp.float32)
    carried = jnp.einsum("hpn,jn->jhp", after_bf, b_cols, preferred_element_type=jnp.float32)
    to_end = jnp.exp(span_total[:, None] - decay_sum)
    grad_x = step_rows.T[:, :, None] * (within + to_end.T[:, :, None] * carried) + skip_gain[
        None, :, None
    ] * grad_rows.astype(jnp.float32)
    intersection = jnp.einsum(
        "shp,jhp->hsj", grad_rows, inputs_c, preferred_element_type=jnp.float32
    )
    mixing = jnp.sum(decay_mat * step_rows[:, None, :] * intersection, axis=0).astype(jnp.bfloat16)
    grad_c = jnp.dot(mixing, b_cols, preferred_element_type=jnp.float32) + jnp.dot(
        scaled.reshape(SPAN, -1), start_bf.reshape(-1, STATE), preferred_element_type=jnp.float32
    )
    grad_b = jnp.dot(mixing.T, c_cols, preferred_element_type=jnp.float32) + jnp.dot(
        weighted.reshape(SPAN, -1), after_bf.reshape(-1, STATE), preferred_element_type=jnp.float32
    )
    grad_proj = jnp.concatenate([grad_b, grad_c], axis=1).astype(jnp.bfloat16)
    return (grad_x.astype(jnp.bfloat16).reshape(SPAN, -1), grad_proj)


def group_all_to_all(payload):
    width = lax.axis_size("y")
    count = lax.axis_size("z") * width

    def kernel(src_ref, out_ref, land, send_sems, recv_sems, local_sem):
        chip, core = lax.axis_index("x"), lax.axis_index("core")
        me = lax.axis_index("z") * width + lax.axis_index("y")
        local = pltpu.make_async_copy(src_ref.at[me], land.at[me], local_sem)
        local.start()
        outgoing = []
        for step in range(1, count):
            dest = (me + step) % count
            copy = pltpu.make_async_remote_copy(
                src_ref=src_ref.at[dest],
                dst_ref=land.at[me],
                send_sem=send_sems.at[step - 1],
                recv_sem=recv_sems.at[step - 1],
                device_id=(chip, core, dest // width, dest % width),
                device_id_type=pl.DeviceIdType.MESH,
            )
            copy.start()
            outgoing.append(copy)
        local.wait()
        for step in range(1, count):
            outgoing[step - 1].wait_send()
            origin = (me + count - step) % count
            pltpu.make_async_remote_copy(
                src_ref=src_ref.at[origin],
                dst_ref=land.at[origin],
                send_sem=send_sems.at[step - 1],
                recv_sem=recv_sems.at[step - 1],
                device_id=(chip, core, origin // width, origin % width),
                device_id_type=pl.DeviceIdType.MESH,
            ).wait_recv()
        out_ref[...] = land[...]

    return pl.pallas_call(
        kernel,
        out_shape=jax.ShapeDtypeStruct(payload.shape, payload.dtype),
        in_specs=[pl.BlockSpec(memory_space=pltpu.VMEM)],
        out_specs=pl.BlockSpec(memory_space=pltpu.VMEM),
        scratch_shapes=[
            pltpu.VMEM(payload.shape, payload.dtype),
            pltpu.SemaphoreType.DMA((count - 1,)),
            pltpu.SemaphoreType.DMA((count - 1,)),
            pltpu.SemaphoreType.DMA(()),
        ],
        compiler_params=pltpu.CompilerParams(has_side_effects=True, vmem_limit_bytes=48 * 1024 * 1024),
    )(payload)


def tiered_exchange(payload):
    width, layers = lax.axis_size("y"), lax.axis_size("z")
    heads, span, cols = payload.shape
    rows = (span - 8) // 2
    group = heads // width
    part = rows // 2
    waves = 4
    mesh_id = pl.DeviceIdType.MESH
    per_wave = 2 * (width - 1) + 2 * (layers - 1)

    def kernel(pay, out_ref, land1, agg, land2, res, land3, out4, land4, sems, local):
        chip, core = lax.axis_index("x"), lax.axis_index("core")
        z, y = lax.axis_index("z"), lax.axis_index("y")
        barrier = pltpu.get_barrier_semaphore()
        for step in range(1, width):
            pl.semaphore_signal(barrier, inc=1, device_id=(chip, core, z, (y + step) % width), device_id_type=mesh_id)
        for step in range(1, layers):
            pl.semaphore_signal(barrier, inc=1, device_id=(chip, core, (z + step) % layers, y), device_id_type=mesh_id)
        pl.semaphore_wait(barrier, width - 1 + layers - 1)

        def tier(src_of, dst, size, where, place, wave, base, slot):
            first = pltpu.make_async_copy(src_of(where), dst, local.at[wave, slot])
            copies = [first]
            for step in range(1, size):
                dest = (where + step) % size
                copies.append(pltpu.make_async_remote_copy(
                    src_ref=src_of(dest), dst_ref=dst, send_sem=sems.at[0, wave, base + step - 1],
                    recv_sem=sems.at[1, wave, base + step - 1], device_id=place(dest), device_id_type=mesh_id,
                ))
            for copy in copies:
                copy.start()
            return copies

        def finish(copies):
            for copy in copies:
                copy.wait()

        row_place = lambda m: (chip, core, z, m)
        col_place = lambda m: (chip, core, m, y)
        def span_of(w):
            return pl.ds(0, part + 8 if w == 0 else part)

        t1 = [
            tier(
                lambda m, w=w: pay.at[pl.ds(m * group, group), w, span_of(w)],
                land1.at[w, y, :, span_of(w)], width, y, row_place, w, 0, 0,
            )
            for w in range(waves)
        ]
        t2 = []
        for w in range(waves):
            finish(t1[w])
            for k in range(group):
                carry = jnp.zeros((part, cols), jnp.float32)
                total = jnp.zeros((1, cols), jnp.float32)
                order = range(width) if w < 2 else reversed(range(width))
                for m in order:
                    mark = land1[0, m, k, part : part + 1]
                    carry = jnp.exp(mark) * carry + land1[w, m, k, :part]
                    total = total + mark
                agg[w, k, :part] = carry
                agg[w, k, part:] = jnp.broadcast_to(total * (1 if w == 0 else 0), (8, cols))
            t2.append(tier(
                lambda m, w=w: agg.at[w, m, span_of(w)], land2.at[w, z, span_of(w)], layers, z, col_place, w, width - 1, 1,
            ))
        t3 = []
        for w in range(waves):
            finish(t2[w])
            carry = jnp.zeros((part, cols), jnp.float32)
            order = range(layers) if w < 2 else reversed(range(layers))
            for r in order:
                res[w, r] = carry
                carry = jnp.exp(land2[0, r, part : part + 1]) * carry + land2[w, r, :part]
            t3.append(tier(lambda m, w=w: res.at[w, m], land3.at[w, z], layers, z, col_place, w, width + layers - 2, 2))
        t4 = []
        for w in range(waves):
            finish(t3[w])
            for k in range(group):
                carry = land3[w, k]
                order = range(width) if w < 2 else reversed(range(width))
                for m in order:
                    out4[w, m, k] = carry
                    carry = jnp.exp(land1[0, m, k, part : part + 1]) * carry + land1[w, m, k, :part]
            t4.append(tier(lambda m, w=w: out4.at[w, m], land4.at[w, y], width, y, row_place, w, width + 2 * layers - 3, 3))
        for w in range(waves):
            finish(t4[w])
            out_ref[:, w * part : (w + 1) * part] = land4[w].reshape(heads, part, cols)

    marks = payload[:, 2 * rows :]
    blank = jnp.zeros_like(marks)
    body = jnp.stack(
        [
            jnp.concatenate([payload[:, w * part : (w + 1) * part], marks if w == 0 else blank], axis=1)
            for w in range(waves)
        ],
        axis=1,
    )
    return pl.pallas_call(
        kernel,
        out_shape=jax.ShapeDtypeStruct((heads, 2 * rows, cols), jnp.float32),
        in_specs=[pl.BlockSpec(memory_space=pltpu.VMEM)],
        out_specs=pl.BlockSpec(memory_space=pltpu.VMEM),
        scratch_shapes=[
            pltpu.VMEM((waves, width, group, part + 8, cols), jnp.float32),
            pltpu.VMEM((waves, group, part + 8, cols), jnp.float32),
            pltpu.VMEM((waves, layers, part + 8, cols), jnp.float32),
            pltpu.VMEM((waves, layers, part, cols), jnp.float32),
            pltpu.VMEM((waves, layers, part, cols), jnp.float32),
            pltpu.VMEM((waves, width, group, part, cols), jnp.float32),
            pltpu.VMEM((waves, width, group, part, cols), jnp.float32),
            pltpu.SemaphoreType.DMA((2, waves, per_wave)),
            pltpu.SemaphoreType.DMA((waves, 4)),
        ],
        compiler_params=pltpu.CompilerParams(
            collective_id=0, has_side_effects=True, vmem_limit_bytes=48 * 1024 * 1024
        ),
    )(body)


def exchange(own_state, own_grad, device_total):
    heads, rows, cols = own_state.shape
    marks = jnp.broadcast_to(device_total[:, None, None], (heads, 8, cols))
    payload = jnp.concatenate([own_state, own_grad, marks], axis=1)
    back = tiered_exchange(payload)
    return back[:, :rows], back[:, rows:]


def weight_grad_sum(tokens, grad_proj, scale):
    chips, cores = lax.axis_size("x"), lax.axis_size("core")
    layers, width = lax.axis_size("z"), lax.axis_size("y")
    count = layers * width
    length, depth = tokens.shape
    cols = grad_proj.shape[1]
    half = cols // 2
    slab = depth // (chips * cores)
    piece = slab // count
    by_owner = tokens.T.reshape(chips, cores, slab, length)
    mesh_id = pl.DeviceIdType.MESH
    ring = count - 1

    def kernel(tok_ref, gp_ref, out_ref, send1, land1, acc_a, acc_b, land_a, land_b,
               sum_a, sum_b, fin_a, fin_b, sems):
        chip, core = lax.axis_index("x"), lax.axis_index("core")
        z, y = lax.axis_index("z"), lax.axis_index("y")
        me = z * width + y
        spot = chip * layers + z
        other = 1 - core
        barrier = pltpu.get_barrier_semaphore()
        pl.semaphore_signal(barrier, inc=1, device_id=(chip, other, z, y), device_id_type=mesh_id)
        for step in range(1, count):
            dest = (me + step) % count
            pl.semaphore_signal(barrier, inc=1, device_id=(chip, core, dest // width, dest % width), device_id_type=mesh_id)
        for step in range(1, chips * layers):
            dest = (spot + step) % (chips * layers)
            pl.semaphore_signal(barrier, inc=1, device_id=(dest // layers, core, dest % layers, y), device_id_type=mesh_id)
        pl.semaphore_wait(barrier, count + chips * layers - 1)
        gp = gp_ref[...]
        for c in range(chips):
            send1[c] = jnp.dot(tok_ref[c, other], gp, preferred_element_type=jnp.float32)
        first = pltpu.make_async_remote_copy(
            src_ref=send1, dst_ref=land1, send_sem=sems.at[0, 0], recv_sem=sems.at[1, 0],
            device_id=(chip, other, z, y), device_id_type=mesh_id,
        )
        first.start()
        own = [jnp.dot(tok_ref[c, core], gp, preferred_element_type=jnp.float32) for c in range(chips)]
        first.wait()
        for c in range(chips):
            summed = own[c] + land1[c]
            acc_a[c] = summed[:, :half]
            blocks = summed[:, half:].reshape(layers, width, piece, half)
            for w in range(width):
                acc_b[w, c] = blocks[:, w]
        second = []
        for step in range(1, chips):
            dest = (chip + step) % chips
            second.append(pltpu.make_async_remote_copy(
                src_ref=acc_a.at[dest], dst_ref=land_a.at[step - 1], send_sem=sems.at[0, step],
                recv_sem=sems.at[1, step], device_id=(dest, core, z, y), device_id_type=mesh_id,
            ))
        for step in range(1, width):
            dest = (y + step) % width
            second.append(pltpu.make_async_remote_copy(
                src_ref=acc_b.at[dest], dst_ref=land_b.at[step - 1], send_sem=sems.at[0, chips + step],
                recv_sem=sems.at[1, chips + step], device_id=(chip, core, z, dest), device_id_type=mesh_id,
            ))
        for copy in second:
            copy.start()
        for copy in second:
            copy.wait()
        total = acc_a[chip]
        for step in range(1, chips):
            total = total + land_a[step - 1]
        sum_a[...] = total.reshape(count, piece, half)
        total = acc_b[y]
        for step in range(1, width):
            total = total + land_b[step - 1]
        sum_b[...] = total.reshape(chips * layers, piece, half)
        base = chips + width
        third = []
        for step in range(1, count):
            dest = (me + step) % count
            third.append(pltpu.make_async_remote_copy(
                src_ref=sum_a.at[dest], dst_ref=fin_a.at[step - 1], send_sem=sems.at[0, base + step],
                recv_sem=sems.at[1, base + step], device_id=(chip, core, dest // width, dest % width),
                device_id_type=mesh_id,
            ))
        for step in range(1, chips * layers):
            dest = (spot + step) % (chips * layers)
            third.append(pltpu.make_async_remote_copy(
                src_ref=sum_b.at[dest], dst_ref=fin_b.at[step - 1], send_sem=sems.at[0, base + ring + step],
                recv_sem=sems.at[1, base + ring + step], device_id=(dest // layers, core, dest % layers, y),
                device_id_type=mesh_id,
            ))
        for copy in third:
            copy.start()
        for copy in third:
            copy.wait()
        total = sum_a[me]
        for step in range(1, count):
            total = total + fin_a[step - 1]
        out_ref[:, :half] = total * scale
        total = sum_b[spot]
        for step in range(1, chips * layers):
            total = total + fin_b[step - 1]
        out_ref[:, half:] = total * scale

    return pl.pallas_call(
        kernel,
        out_shape=jax.ShapeDtypeStruct((piece, cols), jnp.float32),
        in_specs=[pl.BlockSpec(memory_space=pltpu.VMEM)] * 2,
        out_specs=pl.BlockSpec(memory_space=pltpu.VMEM),
        scratch_shapes=[
            pltpu.VMEM((chips, slab, cols), jnp.float32),
            pltpu.VMEM((chips, slab, cols), jnp.float32),
            pltpu.VMEM((chips, slab, half), jnp.float32),
            pltpu.VMEM((width, chips, layers, piece, half), jnp.float32),
            pltpu.VMEM((chips - 1, slab, half), jnp.float32),
            pltpu.VMEM((width - 1, chips, layers, piece, half), jnp.float32),
            pltpu.VMEM((count, piece, half), jnp.float32),
            pltpu.VMEM((chips * layers, piece, half), jnp.float32),
            pltpu.VMEM((count - 1, piece, half), jnp.float32),
            pltpu.VMEM((chips * layers - 1, piece, half), jnp.float32),
            pltpu.SemaphoreType.DMA((2, chips + width + count + chips * layers)),
        ],
        compiler_params=pltpu.CompilerParams(
            collective_id=1, has_side_effects=True, vmem_limit_bytes=48 * 1024 * 1024
        ),
    )(by_owner, grad_proj)


def on_device(layer_input, proj_weight, inputs, step_size, log_decay, skip_gain, grad_out):
    tokens = layer_input[0]
    length = tokens.shape[0]
    proj = jnp.dot(tokens, proj_weight, preferred_element_type=jnp.float32).astype(jnp.bfloat16)
    pieces = span_inputs(proj, inputs[0], grad_out[0], step_size[0], log_decay[0])
    own_state, own_grad, span_total = (pieces[9], pieces[10], pieces[6])
    empty_state = jnp.zeros((SHARD_CHANNELS, HEAD_DIM, STATE), jnp.float32)

    def advance(state_carry, piece):
        return (jnp.exp(piece[1])[:, None, None] * state_carry + piece[0], state_carry)

    last_state, local_starts = lax.scan(advance, empty_state, (own_state, span_total))
    last_grad, local_afters = lax.scan(advance, empty_state, (own_grad, span_total), reverse=True)
    state_entry, grad_entry = exchange(last_state, last_grad, jnp.sum(span_total, axis=0))
    running = jnp.cumsum(span_total, axis=0)
    before = running - span_total
    behind = jnp.sum(span_total, axis=0)[None] - running
    starts = local_starts + jnp.exp(before)[:, :, None, None] * state_entry[None]
    afters = local_afters + jnp.exp(behind)[:, :, None, None] * grad_entry[None]

    def finish(parts):
        return span_grads(*parts, skip_gain)

    grad_x, grad_proj = lax.map(finish, pieces[:9] + (starts, afters))
    grad_proj = grad_proj.reshape(length, 2 * STATE)
    scale_factor = 1.0 / (length * lax.axis_size("z") * lax.axis_size("y"))
    grad_weight = weight_grad_sum(tokens, grad_proj, scale_factor)
    return (grad_x, grad_weight)


def physical_mesh(mesh):
    grid = mesh.devices
    cores = len({d.core_on_chip for d in grid.flat})
    rows = len({d.coords[1] for d in grid.flat})
    dp, seq = grid.shape
    return Mesh(grid.reshape(dp // cores, cores, seq // rows, rows), ("x", "core", "z", "y"))


def solution(mesh):
    fine = physical_mesh(mesh)
    dp, seq = ("x", "core"), ("z", "y")
    return jax.shard_map(
        on_device,
        mesh=fine,
        in_specs=(
            P(dp, seq, None),
            P(),
            P(dp, seq, None),
            P(dp, None, seq),
            P(dp, None, seq),
            P(),
            P(dp, seq, None),
        ),
        out_specs=(P(dp, seq, None), P(dp + seq, None)),
        check_vma=False,
    )
```

```python
import jax
import jax.numpy as jnp
from jax import lax
from jax.experimental import pallas as pl
from jax.experimental.pallas import tpu as pltpu
from jax.sharding import Mesh, PartitionSpec as P

SHARD_CHANNELS = 32
HEAD_DIM = 64
STATE = 128
SPAN = 128


def span_inputs(proj, inputs, grad_out, step_size, log_decay):
    length = inputs.shape[0]
    spans = length // SPAN
    b_cols = proj[:, :STATE].reshape(spans, SPAN, STATE)
    c_cols = proj[:, STATE:].reshape(spans, SPAN, STATE)
    inputs_c = inputs.reshape(spans, SPAN, SHARD_CHANNELS, HEAD_DIM)
    grad_rows = grad_out.reshape(spans, SPAN, SHARD_CHANNELS, HEAD_DIM)
    step_rows = step_size.reshape(SHARD_CHANNELS, spans, SPAN).transpose(1, 0, 2)
    decay_sum = jnp.cumsum(
        log_decay.reshape(SHARD_CHANNELS, spans, SPAN).transpose(1, 0, 2), axis=2
    )
    span_total = decay_sum[:, :, -1]
    to_end = jnp.exp(span_total[:, :, None] - decay_sum)
    weighted = (
        inputs_c.astype(jnp.float32) * jnp.transpose(step_rows * to_end, (0, 2, 1))[..., None]
    ).astype(jnp.bfloat16)
    scaled = (
        grad_rows.astype(jnp.float32) * jnp.transpose(jnp.exp(decay_sum), (0, 2, 1))[..., None]
    ).astype(jnp.bfloat16)
    own_state = jnp.einsum("cqhp,cqn->chpn", weighted, b_cols, preferred_element_type=jnp.float32)
    own_grad = jnp.einsum("cqhp,cqn->chpn", scaled, c_cols, preferred_element_type=jnp.float32)
    return (
        b_cols,
        c_cols,
        inputs_c,
        grad_rows,
        step_rows,
        decay_sum,
        span_total,
        weighted,
        scaled,
        own_state,
        own_grad,
    )


def span_grads(
    b_cols,
    c_cols,
    inputs_c,
    grad_rows,
    step_rows,
    decay_sum,
    span_total,
    weighted,
    scaled,
    start,
    after,
    skip_gain,
):
    start_bf = start.astype(jnp.bfloat16)
    after_bf = after.astype(jnp.bfloat16)
    row_ids = lax.broadcasted_iota(jnp.int32, (SPAN, SPAN), 0)
    col_ids = lax.broadcasted_iota(jnp.int32, (SPAN, SPAN), 1)
    causal = row_ids >= col_ids
    log_gap = decay_sum[:, :, None] - decay_sum[:, None, :]
    decay_mat = jnp.exp(jnp.where(causal[None], log_gap, -jnp.inf))
    kernel = jnp.dot(c_cols, b_cols.T, preferred_element_type=jnp.float32)
    weights = (decay_mat * kernel[None]).astype(jnp.bfloat16)
    within = jnp.einsum("hsj,shp->jhp", weights, grad_rows, preferred_element_type=jnp.float32)
    carried = jnp.einsum("hpn,jn->jhp", after_bf, b_cols, preferred_element_type=jnp.float32)
    to_end = jnp.exp(span_total[:, None] - decay_sum)
    grad_x = step_rows.T[:, :, None] * (within + to_end.T[:, :, None] * carried) + skip_gain[
        None, :, None
    ] * grad_rows.astype(jnp.float32)
    intersection = jnp.einsum(
        "shp,jhp->hsj", grad_rows, inputs_c, preferred_element_type=jnp.float32
    )
    mixing = jnp.sum(decay_mat * step_rows[:, None, :] * intersection, axis=0).astype(jnp.bfloat16)
    grad_c = jnp.dot(mixing, b_cols, preferred_element_type=jnp.float32) + jnp.dot(
        scaled.reshape(SPAN, -1), start_bf.reshape(-1, STATE), preferred_element_type=jnp.float32
    )
    grad_b = jnp.dot(mixing.T, c_cols, preferred_element_type=jnp.float32) + jnp.dot(
        weighted.reshape(SPAN, -1), after_bf.reshape(-1, STATE), preferred_element_type=jnp.float32
    )
    grad_proj = jnp.concatenate([grad_b, grad_c], axis=1).astype(jnp.bfloat16)
    return (grad_x.astype(jnp.bfloat16).reshape(SPAN, -1), grad_proj)


def group_all_to_all(payload):
    width = lax.axis_size("y")
    count = lax.axis_size("z") * width

    def kernel(src_ref, out_ref, land, send_sems, recv_sems, local_sem):
        chip, core = lax.axis_index("x"), lax.axis_index("core")
        me = lax.axis_index("z") * width + lax.axis_index("y")
        local = pltpu.make_async_copy(src_ref.at[me], land.at[me], local_sem)
        local.start()
        outgoing = []
        for step in range(1, count):
            dest = (me + step) % count
            copy = pltpu.make_async_remote_copy(
                src_ref=src_ref.at[dest],
                dst_ref=land.at[me],
                send_sem=send_sems.at[step - 1],
                recv_sem=recv_sems.at[step - 1],
                device_id=(chip, core, dest // width, dest % width),
                device_id_type=pl.DeviceIdType.MESH,
            )
            copy.start()
            outgoing.append(copy)
        local.wait()
        for step in range(1, count):
            outgoing[step - 1].wait_send()
            origin = (me + count - step) % count
            pltpu.make_async_remote_copy(
                src_ref=src_ref.at[origin],
                dst_ref=land.at[origin],
                send_sem=send_sems.at[step - 1],
                recv_sem=recv_sems.at[step - 1],
                device_id=(chip, core, origin // width, origin % width),
                device_id_type=pl.DeviceIdType.MESH,
            ).wait_recv()
        out_ref[...] = land[...]

    return pl.pallas_call(
        kernel,
        out_shape=jax.ShapeDtypeStruct(payload.shape, payload.dtype),
        in_specs=[pl.BlockSpec(memory_space=pltpu.VMEM)],
        out_specs=pl.BlockSpec(memory_space=pltpu.VMEM),
        scratch_shapes=[
            pltpu.VMEM(payload.shape, payload.dtype),
            pltpu.SemaphoreType.DMA((count - 1,)),
            pltpu.SemaphoreType.DMA((count - 1,)),
            pltpu.SemaphoreType.DMA(()),
        ],
        compiler_params=pltpu.CompilerParams(has_side_effects=True, vmem_limit_bytes=48 * 1024 * 1024),
    )(payload)


def tiered_exchange(payload):
    width, layers = lax.axis_size("y"), lax.axis_size("z")
    heads, span, cols = payload.shape
    rows = (span - 8) // 2
    group = heads // width
    part = rows // 2
    waves = 4
    mesh_id = pl.DeviceIdType.MESH
    per_wave = 2 * (width - 1) + 2 * (layers - 1)

    def kernel(pay, out_ref, land1, agg, land2, res, land3, out4, land4, sems, local):
        chip, core = lax.axis_index("x"), lax.axis_index("core")
        z, y = lax.axis_index("z"), lax.axis_index("y")
        barrier = pltpu.get_barrier_semaphore()
        for step in range(1, width):
            pl.semaphore_signal(barrier, inc=1, device_id=(chip, core, z, (y + step) % width), device_id_type=mesh_id)
        for step in range(1, layers):
            pl.semaphore_signal(barrier, inc=1, device_id=(chip, core, (z + step) % layers, y), device_id_type=mesh_id)
        pl.semaphore_wait(barrier, width - 1 + layers - 1)

        def tier(src_of, dst, size, where, place, wave, base, slot):
            first = pltpu.make_async_copy(src_of(where), dst, local.at[wave, slot])
            copies = [first]
            for step in range(1, size):
                dest = (where + step) % size
                copies.append(pltpu.make_async_remote_copy(
                    src_ref=src_of(dest), dst_ref=dst, send_sem=sems.at[0, wave, base + step - 1],
                    recv_sem=sems.at[1, wave, base + step - 1], device_id=place(dest), device_id_type=mesh_id,
                ))
            for copy in copies:
                copy.start()
            return copies

        def finish(copies):
            for copy in copies:
                copy.wait()

        row_place = lambda m: (chip, core, z, m)
        col_place = lambda m: (chip, core, m, y)
        def span_of(w):
            return pl.ds(0, part + 8 if w == 0 else part)

        t1 = [
            tier(
                lambda m, w=w: pay.at[pl.ds(m * group, group), w, span_of(w)],
                land1.at[w, y, :, span_of(w)], width, y, row_place, w, 0, 0,
            )
            for w in range(waves)
        ]
        t2 = []
        for w in range(waves):
            finish(t1[w])
            for k in range(group):
                carry = jnp.zeros((part, cols), jnp.float32)
                total = jnp.zeros((1, cols), jnp.float32)
                order = range(width) if w < 2 else reversed(range(width))
                for m in order:
                    mark = land1[0, m, k, part : part + 1]
                    carry = jnp.exp(mark) * carry + land1[w, m, k, :part]
                    total = total + mark
                agg[w, k, :part] = carry
                agg[w, k, part:] = jnp.broadcast_to(total * (1 if w == 0 else 0), (8, cols))
            t2.append(tier(
                lambda m, w=w: agg.at[w, m, span_of(w)], land2.at[w, z, span_of(w)], layers, z, col_place, w, width - 1, 1,
            ))
        t3 = []
        for w in range(waves):
            finish(t2[w])
            carry = jnp.zeros((part, cols), jnp.float32)
            order = range(layers) if w < 2 else reversed(range(layers))
            for r in order:
                res[w, r] = carry
                carry = jnp.exp(land2[0, r, part : part + 1]) * carry + land2[w, r, :part]
            t3.append(tier(lambda m, w=w: res.at[w, m], land3.at[w, z], layers, z, col_place, w, width + layers - 2, 2))
        t4 = []
        for w in range(waves):
            finish(t3[w])
            for k in range(group):
                carry = land3[w, k]
                order = range(width) if w < 2 else reversed(range(width))
                for m in order:
                    out4[w, m, k] = carry
                    carry = jnp.exp(land1[0, m, k, part : part + 1]) * carry + land1[w, m, k, :part]
            t4.append(tier(lambda m, w=w: out4.at[w, m], land4.at[w, y], width, y, row_place, w, width + 2 * layers - 3, 3))
        for w in range(waves):
            finish(t4[w])
            out_ref[:, w * part : (w + 1) * part] = land4[w].reshape(heads, part, cols)

    marks = payload[:, 2 * rows :]
    blank = jnp.zeros_like(marks)
    body = jnp.stack(
        [
            jnp.concatenate([payload[:, w * part : (w + 1) * part], marks if w == 0 else blank], axis=1)
            for w in range(waves)
        ],
        axis=1,
    )
    return pl.pallas_call(
        kernel,
        out_shape=jax.ShapeDtypeStruct((heads, 2 * rows, cols), jnp.float32),
        in_specs=[pl.BlockSpec(memory_space=pltpu.VMEM)],
        out_specs=pl.BlockSpec(memory_space=pltpu.VMEM),
        scratch_shapes=[
            pltpu.VMEM((waves, width, group, part + 8, cols), jnp.float32),
            pltpu.VMEM((waves, group, part + 8, cols), jnp.float32),
            pltpu.VMEM((waves, layers, part + 8, cols), jnp.float32),
            pltpu.VMEM((waves, layers, part, cols), jnp.float32),
            pltpu.VMEM((waves, layers, part, cols), jnp.float32),
            pltpu.VMEM((waves, width, group, part, cols), jnp.float32),
            pltpu.VMEM((waves, width, group, part, cols), jnp.float32),
            pltpu.SemaphoreType.DMA((2, waves, per_wave)),
            pltpu.SemaphoreType.DMA((waves, 4)),
        ],
        compiler_params=pltpu.CompilerParams(
            collective_id=0, has_side_effects=True, vmem_limit_bytes=48 * 1024 * 1024
        ),
    )(body)


def exchange(own_state, own_grad, device_total):
    heads, rows, cols = own_state.shape
    marks = jnp.broadcast_to(device_total[:, None, None], (heads, 8, cols))
    payload = jnp.concatenate([own_state, own_grad, marks], axis=1)
    back = tiered_exchange(payload)
    return back[:, :rows], back[:, rows:]


def weight_grad_sum(tokens, grad_proj, scale):
    chips, cores = lax.axis_size("x"), lax.axis_size("core")
    layers, width = lax.axis_size("z"), lax.axis_size("y")
    count = layers * width
    length, depth = tokens.shape
    cols = grad_proj.shape[1]
    half = cols // 2
    slab = depth // (chips * cores)
    piece = slab // count
    by_owner = tokens.T.reshape(chips, cores, slab, length)
    mesh_id = pl.DeviceIdType.MESH
    ring = count - 1

    def kernel(tok_ref, gp_ref, out_ref, send1, land1, acc_a, acc_b, land_a, land_b,
               sum_a, sum_b, fin_a, fin_b, sems):
        chip, core = lax.axis_index("x"), lax.axis_index("core")
        z, y = lax.axis_index("z"), lax.axis_index("y")
        me = z * width + y
        spot = chip * layers + z
        other = 1 - core
        barrier = pltpu.get_barrier_semaphore()
        pl.semaphore_signal(barrier, inc=1, device_id=(chip, other, z, y), device_id_type=mesh_id)
        for step in range(1, count):
            dest = (me + step) % count
            pl.semaphore_signal(barrier, inc=1, device_id=(chip, core, dest // width, dest % width), device_id_type=mesh_id)
        for step in range(1, chips * layers):
            dest = (spot + step) % (chips * layers)
            pl.semaphore_signal(barrier, inc=1, device_id=(dest // layers, core, dest % layers, y), device_id_type=mesh_id)
        pl.semaphore_wait(barrier, count + chips * layers - 1)
        gp = gp_ref[...]
        for c in range(chips):
            send1[c] = jnp.dot(tok_ref[c, other], gp, preferred_element_type=jnp.float32)
        first = pltpu.make_async_remote_copy(
            src_ref=send1, dst_ref=land1, send_sem=sems.at[0, 0], recv_sem=sems.at[1, 0],
            device_id=(chip, other, z, y), device_id_type=mesh_id,
        )
        first.start()
        own = [jnp.dot(tok_ref[c, core], gp, preferred_element_type=jnp.float32) for c in range(chips)]
        first.wait()
        for c in range(chips):
            summed = own[c] + land1[c]
            acc_a[c] = summed[:, :half]
            blocks = summed[:, half:].reshape(layers, width, piece, half)
            for w in range(width):
                acc_b[w, c] = blocks[:, w]
        second = []
        for step in range(1, chips):
            dest = (chip + step) % chips
            second.append(pltpu.make_async_remote_copy(
                src_ref=acc_a.at[dest], dst_ref=land_a.at[step - 1], send_sem=sems.at[0, step],
                recv_sem=sems.at[1, step], device_id=(dest, core, z, y), device_id_type=mesh_id,
            ))
        for step in range(1, width):
            dest = (y + step) % width
            second.append(pltpu.make_async_remote_copy(
                src_ref=acc_b.at[dest], dst_ref=land_b.at[step - 1], send_sem=sems.at[0, chips + step],
                recv_sem=sems.at[1, chips + step], device_id=(chip, core, z, dest), device_id_type=mesh_id,
            ))
        for copy in second:
            copy.start()
        base = chips + width
        third_a = []
        for copy in second[: chips - 1]:
            copy.wait()
        total = acc_a[chip]
        for step in range(1, chips):
            total = total + land_a[step - 1]
        sum_a[...] = total.reshape(count, piece, half)
        for step in range(1, count):
            dest = (me + step) % count
            third_a.append(pltpu.make_async_remote_copy(
                src_ref=sum_a.at[dest], dst_ref=fin_a.at[step - 1], send_sem=sems.at[0, base + step],
                recv_sem=sems.at[1, base + step], device_id=(chip, core, dest // width, dest % width),
                device_id_type=mesh_id,
            ))
        for copy in third_a:
            copy.start()
        third_b = []
        for copy in second[chips - 1 :]:
            copy.wait()
        total = acc_b[y]
        for step in range(1, width):
            total = total + land_b[step - 1]
        sum_b[...] = total.reshape(chips * layers, piece, half)
        for step in range(1, chips * layers):
            dest = (spot + step) % (chips * layers)
            third_b.append(pltpu.make_async_remote_copy(
                src_ref=sum_b.at[dest], dst_ref=fin_b.at[step - 1], send_sem=sems.at[0, base + ring + step],
                recv_sem=sems.at[1, base + ring + step], device_id=(dest // layers, core, dest % layers, y),
                device_id_type=mesh_id,
            ))
        for copy in third_b:
            copy.start()
        for copy in third_a:
            copy.wait()
        total = sum_a[me]
        for step in range(1, count):
            total = total + fin_a[step - 1]
        out_ref[:, :half] = total * scale
        for copy in third_b:
            copy.wait()
        total = sum_b[spot]
        for step in range(1, chips * layers):
            total = total + fin_b[step - 1]
        out_ref[:, half:] = total * scale

    return pl.pallas_call(
        kernel,
        out_shape=jax.ShapeDtypeStruct((piece, cols), jnp.float32),
        in_specs=[pl.BlockSpec(memory_space=pltpu.VMEM)] * 2,
        out_specs=pl.BlockSpec(memory_space=pltpu.VMEM),
        scratch_shapes=[
            pltpu.VMEM((chips, slab, cols), jnp.float32),
            pltpu.VMEM((chips, slab, cols), jnp.float32),
            pltpu.VMEM((chips, slab, half), jnp.float32),
            pltpu.VMEM((width, chips, layers, piece, half), jnp.float32),
            pltpu.VMEM((chips - 1, slab, half), jnp.float32),
            pltpu.VMEM((width - 1, chips, layers, piece, half), jnp.float32),
            pltpu.VMEM((count, piece, half), jnp.float32),
            pltpu.VMEM((chips * layers, piece, half), jnp.float32),
            pltpu.VMEM((count - 1, piece, half), jnp.float32),
            pltpu.VMEM((chips * layers - 1, piece, half), jnp.float32),
            pltpu.SemaphoreType.DMA((2, chips + width + count + chips * layers)),
        ],
        compiler_params=pltpu.CompilerParams(
            collective_id=1, has_side_effects=True, vmem_limit_bytes=48 * 1024 * 1024
        ),
    )(by_owner, grad_proj)


def on_device(layer_input, proj_weight, inputs, step_size, log_decay, skip_gain, grad_out):
    tokens = layer_input[0]
    length = tokens.shape[0]
    proj = jnp.dot(tokens, proj_weight, preferred_element_type=jnp.float32).astype(jnp.bfloat16)
    pieces = span_inputs(proj, inputs[0], grad_out[0], step_size[0], log_decay[0])
    own_state, own_grad, span_total = (pieces[9], pieces[10], pieces[6])
    empty_state = jnp.zeros((SHARD_CHANNELS, HEAD_DIM, STATE), jnp.float32)

    def advance(state_carry, piece):
        return (jnp.exp(piece[1])[:, None, None] * state_carry + piece[0], state_carry)

    last_state, local_starts = lax.scan(advance, empty_state, (own_state, span_total))
    last_grad, local_afters = lax.scan(advance, empty_state, (own_grad, span_total), reverse=True)
    state_entry, grad_entry = exchange(last_state, last_grad, jnp.sum(span_total, axis=0))
    running = jnp.cumsum(span_total, axis=0)
    before = running - span_total
    behind = jnp.sum(span_total, axis=0)[None] - running
    starts = local_starts + jnp.exp(before)[:, :, None, None] * state_entry[None]
    afters = local_afters + jnp.exp(behind)[:, :, None, None] * grad_entry[None]

    def finish(parts):
        return span_grads(*parts, skip_gain)

    grad_x, grad_proj = lax.map(finish, pieces[:9] + (starts, afters))
    grad_proj = grad_proj.reshape(length, 2 * STATE)
    scale_factor = 1.0 / (length * lax.axis_size("z") * lax.axis_size("y"))
    grad_weight = weight_grad_sum(tokens, grad_proj, scale_factor)
    return (grad_x, grad_weight)


def physical_mesh(mesh):
    grid = mesh.devices
    cores = len({d.core_on_chip for d in grid.flat})
    rows = len({d.coords[1] for d in grid.flat})
    dp, seq = grid.shape
    return Mesh(grid.reshape(dp // cores, cores, seq // rows, rows), ("x", "core", "z", "y"))


def solution(mesh):
    fine = physical_mesh(mesh)
    dp, seq = ("x", "core"), ("z", "y")
    return jax.shard_map(
        on_device,
        mesh=fine,
        in_specs=(
            P(dp, seq, None),
            P(),
            P(dp, seq, None),
            P(dp, None, seq),
            P(dp, None, seq),
            P(),
            P(dp, seq, None),
        ),
        out_specs=(P(dp, seq, None), P(dp + seq, None)),
        check_vma=False,
    )
```

```python
import jax
import jax.numpy as jnp
from jax import lax
from jax.experimental import pallas as pl
from jax.experimental.pallas import tpu as pltpu
from jax.sharding import Mesh, PartitionSpec as P

SHARD_CHANNELS = 32
HEAD_DIM = 64
STATE = 128
SPAN = 128


def span_inputs(proj, inputs, grad_out, step_size, log_decay):
    length = inputs.shape[0]
    spans = length // SPAN
    b_cols = proj[:, :STATE].reshape(spans, SPAN, STATE)
    c_cols = proj[:, STATE:].reshape(spans, SPAN, STATE)
    inputs_c = inputs.reshape(spans, SPAN, SHARD_CHANNELS, HEAD_DIM)
    grad_rows = grad_out.reshape(spans, SPAN, SHARD_CHANNELS, HEAD_DIM)
    step_rows = step_size.reshape(SHARD_CHANNELS, spans, SPAN).transpose(1, 0, 2)
    decay_sum = jnp.cumsum(
        log_decay.reshape(SHARD_CHANNELS, spans, SPAN).transpose(1, 0, 2), axis=2
    )
    span_total = decay_sum[:, :, -1]
    to_end = jnp.exp(span_total[:, :, None] - decay_sum)
    weighted = (
        inputs_c.astype(jnp.float32) * jnp.transpose(step_rows * to_end, (0, 2, 1))[..., None]
    ).astype(jnp.bfloat16)
    scaled = (
        grad_rows.astype(jnp.float32) * jnp.transpose(jnp.exp(decay_sum), (0, 2, 1))[..., None]
    ).astype(jnp.bfloat16)
    own_state = jnp.einsum("cqhp,cqn->chpn", weighted, b_cols, preferred_element_type=jnp.float32)
    own_grad = jnp.einsum("cqhp,cqn->chpn", scaled, c_cols, preferred_element_type=jnp.float32)
    return (
        b_cols,
        c_cols,
        inputs_c,
        grad_rows,
        step_rows,
        decay_sum,
        span_total,
        weighted,
        scaled,
        own_state,
        own_grad,
    )


def span_grads(
    b_cols,
    c_cols,
    inputs_c,
    grad_rows,
    step_rows,
    decay_sum,
    span_total,
    weighted,
    scaled,
    start,
    after,
    skip_gain,
):
    start_bf = start.astype(jnp.bfloat16)
    after_bf = after.astype(jnp.bfloat16)
    row_ids = lax.broadcasted_iota(jnp.int32, (SPAN, SPAN), 0)
    col_ids = lax.broadcasted_iota(jnp.int32, (SPAN, SPAN), 1)
    causal = row_ids >= col_ids
    log_gap = decay_sum[:, :, None] - decay_sum[:, None, :]
    decay_mat = jnp.exp(jnp.where(causal[None], log_gap, -jnp.inf))
    kernel = jnp.dot(c_cols, b_cols.T, preferred_element_type=jnp.float32)
    weights = (decay_mat * kernel[None]).astype(jnp.bfloat16)
    within = jnp.einsum("hsj,shp->jhp", weights, grad_rows, preferred_element_type=jnp.float32)
    carried = jnp.einsum("hpn,jn->jhp", after_bf, b_cols, preferred_element_type=jnp.float32)
    to_end = jnp.exp(span_total[:, None] - decay_sum)
    grad_x = step_rows.T[:, :, None] * (within + to_end.T[:, :, None] * carried) + skip_gain[
        None, :, None
    ] * grad_rows.astype(jnp.float32)
    intersection = jnp.einsum(
        "shp,jhp->hsj", grad_rows, inputs_c, preferred_element_type=jnp.float32
    )
    mixing = jnp.sum(decay_mat * step_rows[:, None, :] * intersection, axis=0).astype(jnp.bfloat16)
    grad_c = jnp.dot(mixing, b_cols, preferred_element_type=jnp.float32) + jnp.dot(
        scaled.reshape(SPAN, -1), start_bf.reshape(-1, STATE), preferred_element_type=jnp.float32
    )
    grad_b = jnp.dot(mixing.T, c_cols, preferred_element_type=jnp.float32) + jnp.dot(
        weighted.reshape(SPAN, -1), after_bf.reshape(-1, STATE), preferred_element_type=jnp.float32
    )
    grad_proj = jnp.concatenate([grad_b, grad_c], axis=1).astype(jnp.bfloat16)
    return (grad_x.astype(jnp.bfloat16).reshape(SPAN, -1), grad_proj)


def group_all_to_all(payload):
    width = lax.axis_size("y")
    count = lax.axis_size("z") * width

    def kernel(src_ref, out_ref, land, send_sems, recv_sems, local_sem):
        chip, core = lax.axis_index("x"), lax.axis_index("core")
        me = lax.axis_index("z") * width + lax.axis_index("y")
        local = pltpu.make_async_copy(src_ref.at[me], land.at[me], local_sem)
        local.start()
        outgoing = []
        for step in range(1, count):
            dest = (me + step) % count
            copy = pltpu.make_async_remote_copy(
                src_ref=src_ref.at[dest],
                dst_ref=land.at[me],
                send_sem=send_sems.at[step - 1],
                recv_sem=recv_sems.at[step - 1],
                device_id=(chip, core, dest // width, dest % width),
                device_id_type=pl.DeviceIdType.MESH,
            )
            copy.start()
            outgoing.append(copy)
        local.wait()
        for step in range(1, count):
            outgoing[step - 1].wait_send()
            origin = (me + count - step) % count
            pltpu.make_async_remote_copy(
                src_ref=src_ref.at[origin],
                dst_ref=land.at[origin],
                send_sem=send_sems.at[step - 1],
                recv_sem=recv_sems.at[step - 1],
                device_id=(chip, core, origin // width, origin % width),
                device_id_type=pl.DeviceIdType.MESH,
            ).wait_recv()
        out_ref[...] = land[...]

    return pl.pallas_call(
        kernel,
        out_shape=jax.ShapeDtypeStruct(payload.shape, payload.dtype),
        in_specs=[pl.BlockSpec(memory_space=pltpu.VMEM)],
        out_specs=pl.BlockSpec(memory_space=pltpu.VMEM),
        scratch_shapes=[
            pltpu.VMEM(payload.shape, payload.dtype),
            pltpu.SemaphoreType.DMA((count - 1,)),
            pltpu.SemaphoreType.DMA((count - 1,)),
            pltpu.SemaphoreType.DMA(()),
        ],
        compiler_params=pltpu.CompilerParams(has_side_effects=True, vmem_limit_bytes=48 * 1024 * 1024),
    )(payload)


def tiered_exchange(payload):
    width, layers = lax.axis_size("y"), lax.axis_size("z")
    heads, span, cols = payload.shape
    rows = (span - 8) // 2
    group = heads // width
    waves = 8
    part = rows * 2 // waves
    mesh_id = pl.DeviceIdType.MESH
    per_wave = 2 * (width - 1) + 2 * (layers - 1)

    def kernel(pay, out_ref, land1, agg, land2, res, land3, out4, land4, sems, local):
        chip, core = lax.axis_index("x"), lax.axis_index("core")
        z, y = lax.axis_index("z"), lax.axis_index("y")
        barrier = pltpu.get_barrier_semaphore()
        for step in range(1, width):
            pl.semaphore_signal(barrier, inc=1, device_id=(chip, core, z, (y + step) % width), device_id_type=mesh_id)
        for step in range(1, layers):
            pl.semaphore_signal(barrier, inc=1, device_id=(chip, core, (z + step) % layers, y), device_id_type=mesh_id)
        pl.semaphore_wait(barrier, width - 1 + layers - 1)

        def tier(src_of, dst, size, where, place, wave, base, slot):
            first = pltpu.make_async_copy(src_of(where), dst, local.at[wave, slot])
            copies = [first]
            for step in range(1, size):
                dest = (where + step) % size
                copies.append(pltpu.make_async_remote_copy(
                    src_ref=src_of(dest), dst_ref=dst, send_sem=sems.at[0, wave, base + step - 1],
                    recv_sem=sems.at[1, wave, base + step - 1], device_id=place(dest), device_id_type=mesh_id,
                ))
            for copy in copies:
                copy.start()
            return copies

        def finish(copies):
            for copy in copies:
                copy.wait()

        row_place = lambda m: (chip, core, z, m)
        col_place = lambda m: (chip, core, m, y)
        def span_of(w):
            return pl.ds(0, part + 8 if w == 0 else part)

        t1 = [
            tier(
                lambda m, w=w: pay.at[pl.ds(m * group, group), w, span_of(w)],
                land1.at[w, y, :, span_of(w)], width, y, row_place, w, 0, 0,
            )
            for w in range(waves)
        ]
        t2 = []
        for w in range(waves):
            finish(t1[w])
            for k in range(group):
                carry = jnp.zeros((part, cols), jnp.float32)
                total = jnp.zeros((1, cols), jnp.float32)
                order = range(width) if w < waves // 2 else reversed(range(width))
                for m in order:
                    mark = land1[0, m, k, part : part + 1]
                    carry = jnp.exp(mark) * carry + land1[w, m, k, :part]
                    total = total + mark
                agg[w, k, :part] = carry
                agg[w, k, part:] = jnp.broadcast_to(total * (1 if w == 0 else 0), (8, cols))
            t2.append(tier(
                lambda m, w=w: agg.at[w, m, span_of(w)], land2.at[w, z, span_of(w)], layers, z, col_place, w, width - 1, 1,
            ))
        t3 = []
        for w in range(waves):
            finish(t2[w])
            carry = jnp.zeros((part, cols), jnp.float32)
            order = range(layers) if w < waves // 2 else reversed(range(layers))
            for r in order:
                res[w, r] = carry
                carry = jnp.exp(land2[0, r, part : part + 1]) * carry + land2[w, r, :part]
            t3.append(tier(lambda m, w=w: res.at[w, m], land3.at[w, z], layers, z, col_place, w, width + layers - 2, 2))
        t4 = []
        for w in range(waves):
            finish(t3[w])
            for k in range(group):
                carry = land3[w, k]
                order = range(width) if w < waves // 2 else reversed(range(width))
                for m in order:
                    out4[w, m, k] = carry
                    carry = jnp.exp(land1[0, m, k, part : part + 1]) * carry + land1[w, m, k, :part]
            t4.append(tier(lambda m, w=w: out4.at[w, m], land4.at[w, y], width, y, row_place, w, width + 2 * layers - 3, 3))
        for w in range(waves):
            finish(t4[w])
            out_ref[:, w * part : (w + 1) * part] = land4[w].reshape(heads, part, cols)

    marks = payload[:, 2 * rows :]
    blank = jnp.zeros_like(marks)
    body = jnp.stack(
        [
            jnp.concatenate([payload[:, w * part : (w + 1) * part], marks if w == 0 else blank], axis=1)
            for w in range(waves)
        ],
        axis=1,
    )
    return pl.pallas_call(
        kernel,
        out_shape=jax.ShapeDtypeStruct((heads, 2 * rows, cols), jnp.float32),
        in_specs=[pl.BlockSpec(memory_space=pltpu.VMEM)],
        out_specs=pl.BlockSpec(memory_space=pltpu.VMEM),
        scratch_shapes=[
            pltpu.VMEM((waves, width, group, part + 8, cols), jnp.float32),
            pltpu.VMEM((waves, group, part + 8, cols), jnp.float32),
            pltpu.VMEM((waves, layers, part + 8, cols), jnp.float32),
            pltpu.VMEM((waves, layers, part, cols), jnp.float32),
            pltpu.VMEM((waves, layers, part, cols), jnp.float32),
            pltpu.VMEM((waves, width, group, part, cols), jnp.float32),
            pltpu.VMEM((waves, width, group, part, cols), jnp.float32),
            pltpu.SemaphoreType.DMA((2, waves, per_wave)),
            pltpu.SemaphoreType.DMA((waves, 4)),
        ],
        compiler_params=pltpu.CompilerParams(
            collective_id=0, has_side_effects=True, vmem_limit_bytes=48 * 1024 * 1024
        ),
    )(body)


def exchange(own_state, own_grad, device_total):
    heads, rows, cols = own_state.shape
    marks = jnp.broadcast_to(device_total[:, None, None], (heads, 8, cols))
    payload = jnp.concatenate([own_state, own_grad, marks], axis=1)
    back = tiered_exchange(payload)
    return back[:, :rows], back[:, rows:]


def weight_grad_sum(tokens, grad_proj, scale):
    chips, cores = lax.axis_size("x"), lax.axis_size("core")
    layers, width = lax.axis_size("z"), lax.axis_size("y")
    count = layers * width
    length, depth = tokens.shape
    cols = grad_proj.shape[1]
    half = cols // 2
    slab = depth // (chips * cores)
    piece = slab // count
    by_owner = tokens.T.reshape(chips, cores, slab, length)
    mesh_id = pl.DeviceIdType.MESH
    ring = count - 1

    def kernel(tok_ref, gp_ref, out_ref, send1, land1, acc_a, acc_b, land_a, land_b,
               sum_a, sum_b, fin_a, fin_b, sems):
        chip, core = lax.axis_index("x"), lax.axis_index("core")
        z, y = lax.axis_index("z"), lax.axis_index("y")
        me = z * width + y
        spot = chip * layers + z
        other = 1 - core
        barrier = pltpu.get_barrier_semaphore()
        pl.semaphore_signal(barrier, inc=1, device_id=(chip, other, z, y), device_id_type=mesh_id)
        for step in range(1, count):
            dest = (me + step) % count
            pl.semaphore_signal(barrier, inc=1, device_id=(chip, core, dest // width, dest % width), device_id_type=mesh_id)
        for step in range(1, chips * layers):
            dest = (spot + step) % (chips * layers)
            pl.semaphore_signal(barrier, inc=1, device_id=(dest // layers, core, dest % layers, y), device_id_type=mesh_id)
        pl.semaphore_wait(barrier, count + chips * layers - 1)
        gp = gp_ref[...]
        for c in range(chips):
            send1[c] = jnp.dot(tok_ref[c, other], gp, preferred_element_type=jnp.float32)
        first = pltpu.make_async_remote_copy(
            src_ref=send1, dst_ref=land1, send_sem=sems.at[0, 0], recv_sem=sems.at[1, 0],
            device_id=(chip, other, z, y), device_id_type=mesh_id,
        )
        first.start()
        own = [jnp.dot(tok_ref[c, core], gp, preferred_element_type=jnp.float32) for c in range(chips)]
        first.wait()
        for c in range(chips):
            summed = own[c] + land1[c]
            acc_a[c] = summed[:, :half]
            blocks = summed[:, half:].reshape(layers, width, piece, half)
            for w in range(width):
                acc_b[w, c] = blocks[:, w]
        second = []
        for step in range(1, chips):
            dest = (chip + step) % chips
            second.append(pltpu.make_async_remote_copy(
                src_ref=acc_a.at[dest], dst_ref=land_a.at[step - 1], send_sem=sems.at[0, step],
                recv_sem=sems.at[1, step], device_id=(dest, core, z, y), device_id_type=mesh_id,
            ))
        for step in range(1, width):
            dest = (y + step) % width
            second.append(pltpu.make_async_remote_copy(
                src_ref=acc_b.at[dest], dst_ref=land_b.at[step - 1], send_sem=sems.at[0, chips + step],
                recv_sem=sems.at[1, chips + step], device_id=(chip, core, z, dest), device_id_type=mesh_id,
            ))
        for copy in second:
            copy.start()
        base = chips + width
        third_a = []
        for copy in second[: chips - 1]:
            copy.wait()
        total = acc_a[chip]
        for step in range(1, chips):
            total = total + land_a[step - 1]
        sum_a[...] = total.reshape(count, piece, half)
        for step in range(1, count):
            dest = (me + step) % count
            third_a.append(pltpu.make_async_remote_copy(
                src_ref=sum_a.at[dest], dst_ref=fin_a.at[step - 1], send_sem=sems.at[0, base + step],
                recv_sem=sems.at[1, base + step], device_id=(chip, core, dest // width, dest % width),
                device_id_type=mesh_id,
            ))
        for copy in third_a:
            copy.start()
        third_b = []
        for copy in second[chips - 1 :]:
            copy.wait()
        total = acc_b[y]
        for step in range(1, width):
            total = total + land_b[step - 1]
        sum_b[...] = total.reshape(chips * layers, piece, half)
        for step in range(1, chips * layers):
            dest = (spot + step) % (chips * layers)
            third_b.append(pltpu.make_async_remote_copy(
                src_ref=sum_b.at[dest], dst_ref=fin_b.at[step - 1], send_sem=sems.at[0, base + ring + step],
                recv_sem=sems.at[1, base + ring + step], device_id=(dest // layers, core, dest % layers, y),
                device_id_type=mesh_id,
            ))
        for copy in third_b:
            copy.start()
        for copy in third_a:
            copy.wait()
        total = sum_a[me]
        for step in range(1, count):
            total = total + fin_a[step - 1]
        out_ref[:, :half] = total * scale
        for copy in third_b:
            copy.wait()
        total = sum_b[spot]
        for step in range(1, chips * layers):
            total = total + fin_b[step - 1]
        out_ref[:, half:] = total * scale

    return pl.pallas_call(
        kernel,
        out_shape=jax.ShapeDtypeStruct((piece, cols), jnp.float32),
        in_specs=[pl.BlockSpec(memory_space=pltpu.VMEM)] * 2,
        out_specs=pl.BlockSpec(memory_space=pltpu.VMEM),
        scratch_shapes=[
            pltpu.VMEM((chips, slab, cols), jnp.float32),
            pltpu.VMEM((chips, slab, cols), jnp.float32),
            pltpu.VMEM((chips, slab, half), jnp.float32),
            pltpu.VMEM((width, chips, layers, piece, half), jnp.float32),
            pltpu.VMEM((chips - 1, slab, half), jnp.float32),
            pltpu.VMEM((width - 1, chips, layers, piece, half), jnp.float32),
            pltpu.VMEM((count, piece, half), jnp.float32),
            pltpu.VMEM((chips * layers, piece, half), jnp.float32),
            pltpu.VMEM((count - 1, piece, half), jnp.float32),
            pltpu.VMEM((chips * layers - 1, piece, half), jnp.float32),
            pltpu.SemaphoreType.DMA((2, chips + width + count + chips * layers)),
        ],
        compiler_params=pltpu.CompilerParams(
            collective_id=1, has_side_effects=True, vmem_limit_bytes=48 * 1024 * 1024
        ),
    )(by_owner, grad_proj)


def on_device(layer_input, proj_weight, inputs, step_size, log_decay, skip_gain, grad_out):
    tokens = layer_input[0]
    length = tokens.shape[0]
    proj = jnp.dot(tokens, proj_weight, preferred_element_type=jnp.float32).astype(jnp.bfloat16)
    pieces = span_inputs(proj, inputs[0], grad_out[0], step_size[0], log_decay[0])
    own_state, own_grad, span_total = (pieces[9], pieces[10], pieces[6])
    empty_state = jnp.zeros((SHARD_CHANNELS, HEAD_DIM, STATE), jnp.float32)

    def advance(state_carry, piece):
        return (jnp.exp(piece[1])[:, None, None] * state_carry + piece[0], state_carry)

    last_state, local_starts = lax.scan(advance, empty_state, (own_state, span_total))
    last_grad, local_afters = lax.scan(advance, empty_state, (own_grad, span_total), reverse=True)
    state_entry, grad_entry = exchange(last_state, last_grad, jnp.sum(span_total, axis=0))
    running = jnp.cumsum(span_total, axis=0)
    before = running - span_total
    behind = jnp.sum(span_total, axis=0)[None] - running
    starts = local_starts + jnp.exp(before)[:, :, None, None] * state_entry[None]
    afters = local_afters + jnp.exp(behind)[:, :, None, None] * grad_entry[None]

    def finish(parts):
        return span_grads(*parts, skip_gain)

    grad_x, grad_proj = lax.map(finish, pieces[:9] + (starts, afters))
    grad_proj = grad_proj.reshape(length, 2 * STATE)
    scale_factor = 1.0 / (length * lax.axis_size("z") * lax.axis_size("y"))
    grad_weight = weight_grad_sum(tokens, grad_proj, scale_factor)
    return (grad_x, grad_weight)


def physical_mesh(mesh):
    grid = mesh.devices
    cores = len({d.core_on_chip for d in grid.flat})
    rows = len({d.coords[1] for d in grid.flat})
    dp, seq = grid.shape
    return Mesh(grid.reshape(dp // cores, cores, seq // rows, rows), ("x", "core", "z", "y"))


def solution(mesh):
    fine = physical_mesh(mesh)
    dp, seq = ("x", "core"), ("z", "y")
    return jax.shard_map(
        on_device,
        mesh=fine,
        in_specs=(
            P(dp, seq, None),
            P(),
            P(dp, seq, None),
            P(dp, None, seq),
            P(dp, None, seq),
            P(),
            P(dp, seq, None),
        ),
        out_specs=(P(dp, seq, None), P(dp + seq, None)),
        check_vma=False,
    )
```
